32 devices in a mesh: section: 2 (over core), table: 16 (over z, y, x).
Axes of the slice: x: 2, y: 2, z: 4, core: 2. Of those that a mesh axis runs over, the one named last changes fastest.
Arguments:
- gate_a: bfloat16 [2, 1024, 4096], P('section', 'table'), may hold values from -6 to 6
- cotangent_a: bfloat16 [2, 1024, 4096], P('section', 'table'), may hold values from -6 to 6
- gate_b: bfloat16 [2, 1024, 4096], P('section', 'table'), may hold values from -6 to 6
- table: bfloat16 [1024, 4096], P('table'), may hold values from -6 to 6
- row_ids: int32 [2, 2, 16, 128], P('section', None, 'table'), may hold values from 0 to 1023, as said below
- slots: int32 [2, 2, 1024, 128], P('section', None, 'table'), may hold values from 0 to 127, as said below
- weights: float32 [2, 2, 1024, 128], P('section', None, 'table'), may hold values from 0.02 to 0.2
Outputs:
- mixed_b: bfloat16 [2, 1024, 4096], P('section', 'table')
- grad_gate_a: bfloat16 [2, 1024, 4096], P('section', 'table')
- grad_weights_a: float32 [2, 1024, 128], P('section', 'table')
- grad_table: float32 [1024, 4096], P('table', 'section')
The draws below stay inside these ranges and needn't reach their ends.
Inputs may be any that keep to these rules, and one draw needn't show every extreme that they name: `row_ids`: row r is held by index r // 64 of table. The 128 ids of one list are distinct, and at most 8 of them are held by one index of table; in every section and micro-batch some index of table holds 8 ids of every device's list. `slots`: the 32 picks of one token and head are distinct, and every position of a device's list is picked by some token of that device and micro-batch.
All inputs are finite; a program needn't handle non-finite values.
Results may differ from the reference program's by a relative error of at most 0.0057.
Values may be sent and summed in bfloat16 or wider, within the bound.
A program may use at most 128 MiB of HBM per device.

```python
import math
import jax
import jax.numpy as jnp
from jax import lax

D = 4096
HEADS = 4
TOPK = 32
TOK_DEV = 64
ROWS_DEV = 64
USED = 128
ROW_LIMIT = 8
PICKS = 128
TOKENS = 1024
ROWS = 1024
N_SECTION = 2
N_TABLE = 16


def owner_rows(table_group, device_key):
    popular_key, boost_key = jax.random.split(table_group)
    hottest = jax.random.randint(popular_key, (), 0, N_TABLE)
    score_boost = jax.random.randint(boost_key, (N_TABLE,), 0, 4) * 8192
    scoring_key, key_order, key_shuffle = jax.random.split(device_key, 3)
    row_scores = jax.random.randint(scoring_key, (N_TABLE, ROW_LIMIT), 0, 16384) + score_boost[:, None]
    owner_ids = jnp.arange(N_TABLE, dtype=jnp.int32)
    row_scores = jnp.where(owner_ids[:, None] == hottest, 1 << 17, row_scores)
    ranked = row_scores.reshape(-1) * (N_TABLE * ROW_LIMIT) + jnp.arange(N_TABLE * ROW_LIMIT, dtype=jnp.int32)
    _, chosen = lax.top_k(ranked, USED)
    owner_of = chosen // ROW_LIMIT
    column = chosen % ROW_LIMIT
    order_keys = jax.random.randint(key_order, (N_TABLE, ROWS_DEV), 0, 1 << 16) * ROWS_DEV + jnp.arange(ROWS_DEV, dtype=jnp.int32)[None, :]
    shuffled = jnp.argsort(order_keys, axis=1)
    within = shuffled[owner_of, column]
    listed = owner_of * ROWS_DEV + within
    return listed[jax.random.permutation(key_shuffle, USED)]


def draw_row_ids(key, part):

    def group_lists(index):
        table_group = jax.random.fold_in(key, 7000 + index)

        def one_device(device):
            return owner_rows(table_group, jax.random.fold_in(table_group, 100 + device))
        return jax.vmap(one_device)(jnp.arange(N_TABLE))
    lists = jax.vmap(group_lists)(jnp.arange(N_SECTION * 2))
    return lists.reshape(N_SECTION, 2, N_TABLE, USED).astype(jnp.int32)


def slot_block(block_key):
    key_pairs, key_slots, scoring_key = jax.random.split(block_key, 3)
    pair_rank = jnp.argsort(jax.random.permutation(key_pairs, TOK_DEV * HEADS))
    slot_rank = jnp.argsort(jax.random.permutation(key_slots, USED))
    row_scores = jax.random.randint(scoring_key, (TOK_DEV * HEADS, USED), 0, 1 << 16)
    forced = pair_rank[:, None] == (slot_rank // TOPK)[None, :]
    row_scores = jnp.where(forced, 1 << 17, row_scores)
    ranked = row_scores * USED + jnp.arange(USED, dtype=jnp.int32)[None, :]
    _, picked = lax.top_k(ranked, TOPK)
    return picked.reshape(TOK_DEV, PICKS).astype(jnp.int32)


def draw_slots(key, part):

    def one_block(index):
        return slot_block(jax.random.fold_in(key, 9000 + index))
    blocks = jax.vmap(one_block)(jnp.arange(N_SECTION * 2 * N_TABLE))
    return blocks.reshape(N_SECTION, 2, N_TABLE * TOK_DEV, PICKS)


def level_of(rng, dims, pieces, least, largest):
    level, own = 1.0, jax.random.fold_in(rng, 6)
    for axis_at, shards_of in pieces:
        draws = jnp.exp(jax.random.uniform(jax.random.fold_in(own, axis_at), (shards_of,), jnp.float32, least / len(pieces), largest / len(pieces)))
        level = level * jnp.repeat(draws, dims[axis_at] // shards_of).reshape([-1 if axis == axis_at else 1 for axis in range(len(dims))])
    return level


def scatter_about(rng, extent, scale, most, cuts=(), held_as=jnp.bfloat16):
    gain = level_of(rng, extent, cuts, -0.22, 0.18) if cuts else 1.0
    result = jax.random.normal(rng, extent, jnp.float32) * scale * gain
    return jnp.minimum(jnp.maximum(result, -most), most).astype(held_as)


def setup_inputs(seed: int = 0) -> dict:
    splits = jax.random.split(jax.random.key(seed), 8)
    return {
        "gate_a": scatter_about(splits[0], (N_SECTION, TOKENS, D), 1.0, 6.0, ((0, 2), (1, 16))),
        "cotangent_a": scatter_about(splits[1], (N_SECTION, TOKENS, D), 1.0, 6.0, ((0, 2), (1, 16))),
        "gate_b": scatter_about(splits[2], (N_SECTION, TOKENS, D), 1.0, 6.0, ((0, 2), (1, 16))),
        "table": scatter_about(splits[3], (ROWS, D), 1.0, 6.0, ((0, 16),)),
        "row_ids": draw_row_ids(jax.random.fold_in(splits[7], 71), 0),
        "slots": draw_slots(jax.random.fold_in(splits[7], 71), 0),
        "weights": jnp.clip(jnp.exp(math.log(0.2) - 2.3025851 * jax.random.uniform(splits[6], (N_SECTION, 2, TOKENS, PICKS), jnp.float32) ** level_of(splits[6], (N_SECTION, 2, TOKENS, PICKS), ((0, 2), (2, 16)), -0.2, 0.2)), 0.02, 0.2),
    }


def combine_table(slot_rows, weight_rows, listed):
    matches = slot_rows[:, :, None] == jnp.arange(listed, dtype=jnp.int32)[None, None, :]
    return jnp.sum(jnp.where(matches, weight_rows[:, :, None], jnp.zeros_like(weight_rows[:, :, None])), axis=1).astype(jnp.bfloat16)


def reference(gate_a, cotangent_a, gate_b, table, row_ids, slots, weights):
    section_count = gate_a.shape[0]
    tokens = gate_a.shape[1] // N_TABLE
    features = table.shape[1]

    def split_tokens(values):
        return values.reshape((section_count * N_TABLE, tokens) + values.shape[2:])

    def split_micro(values):
        values = values.reshape(section_count, 2, N_TABLE, tokens, values.shape[-1])
        return jnp.transpose(values, (0, 2, 1, 3, 4)).reshape(section_count * N_TABLE, 2, tokens, values.shape[-1])

    id_lists = jnp.transpose(row_ids, (0, 2, 1, 3)).reshape(section_count * N_TABLE, 2, USED)

    def device_step(grad_table, inputs):
        gate_one, cotangent_one, gate_two, list_pair, slot_pair, weight_pair = inputs
        fetched_a = jnp.take(table, list_pair[0], axis=0)
        fetched_b = jnp.take(table, list_pair[1], axis=0)
        mixing_a = combine_table(slot_pair[0], weight_pair[0], USED)
        mixing_b = combine_table(slot_pair[1], weight_pair[1], USED)
        memory_b = jnp.dot(mixing_b, fetched_b, preferred_element_type=jnp.float32)
        gate_value = gate_two.astype(jnp.float32)
        mixed = (gate_value * jax.nn.sigmoid(gate_value) * memory_b).astype(jnp.bfloat16)
        memory_a = jnp.dot(mixing_a, fetched_a, preferred_element_type=jnp.float32)
        gate_value = gate_one.astype(jnp.float32)
        incoming = cotangent_one.astype(jnp.float32)
        logistic = jax.nn.sigmoid(gate_value)
        grad_gate = (incoming * memory_a * logistic * (1.0 + gate_value * (1.0 - logistic))).astype(jnp.bfloat16)
        grad_memory = (incoming * gate_value * logistic).astype(jnp.bfloat16)
        row_scores = lax.dot_general(grad_memory, fetched_a, (((1,), (1,)), ((), ())), preferred_element_type=jnp.float32)
        grad_weights = jnp.take_along_axis(row_scores, slot_pair[0], axis=1)
        grad_rows = lax.dot_general(mixing_a, grad_memory, (((0,), (0,)), ((), ())), preferred_element_type=jnp.float32).astype(jnp.bfloat16)
        grad_table = grad_table.at[list_pair[0]].add(grad_rows.astype(jnp.float32))
        return grad_table, (mixed, grad_gate, grad_weights)

    inputs = (split_tokens(gate_a), split_tokens(cotangent_a), split_tokens(gate_b), id_lists, split_micro(slots), split_micro(weights))
    grad_table, outputs = lax.scan(device_step, jnp.zeros(table.shape, jnp.float32), inputs)
    mixed, grad_gate, grad_weights = outputs
    mixed = mixed.reshape(section_count, N_TABLE * tokens, features)
    grad_gate = grad_gate.reshape(section_count, N_TABLE * tokens, features)
    grad_weights = grad_weights.reshape(section_count, N_TABLE * tokens, grad_weights.shape[-1])
    return mixed, grad_gate, grad_weights, grad_table
```

```python
import jax
import jax.numpy as jnp
from jax import lax
from jax.experimental import pallas as pl
from jax.experimental.pallas import tpu as pltpu
from jax.sharding import PartitionSpec as P

ROW_LIMIT = 8
CHUNK = 512
LAYERS = 4
PIECES = 4
UNROLL = 8
MESH = pl.DeviceIdType.MESH
BF16, F32 = jnp.bfloat16, jnp.float32


def iota(shape, axis):
    return lax.broadcasted_iota(jnp.int32, shape, axis)


def hot(mask):
    return mask.astype(F32).astype(BF16)


def contract(lhs, rhs, dims, **options):
    return lax.dot_general(lhs, rhs, (dims, ((), ())), preferred_element_type=F32, **options)


def locate(ids, owners, plane, rows_dev):
    listed = ids.shape[1]
    line = iota((owners, listed), 0)
    layer = line & (LAYERS - 1)
    column = lax.shift_right_logical(line, LAYERS.bit_length() - 1)
    first = (layer * plane + column) * rows_dev
    member = ((ids >= first) & (ids < first + rows_dev)).astype(F32)
    before = iota((listed, listed), 0) < iota((listed, listed), 1)
    earlier = contract(member.astype(BF16), hot(before), ((1,), (0,)))
    rank = jnp.sum(member * earlier, axis=0, keepdims=True).astype(jnp.int32)
    spot = jnp.sum(member * line.astype(F32), axis=0, keepdims=True).astype(jnp.int32)
    start = jnp.sum(member * first.astype(F32), axis=0, keepdims=True).astype(jnp.int32)
    held = (member * (ids - start + 1).astype(F32)).astype(BF16)
    return rank, spot, held


def mix_picks(slots_t, weights_t, listed):
    picks, tokens = slots_t.shape
    position = iota((listed, tokens), 0).astype(F32)

    def group(g, total):
        base = pl.multiple_of(g * UNROLL, UNROLL)
        slot = slots_t[pl.ds(base, UNROLL), :]
        weight = weights_t[pl.ds(base, UNROLL), :]
        for p in range(UNROLL):
            hit = slot[p : p + 1] == position
            total = total + jnp.where(hit, weight[p : p + 1], 0.0)
        return total

    start = jnp.zeros((listed, tokens), F32)
    return lax.fori_loop(0, picks // UNROLL, group, start)


def drain(block, sem):
    pltpu.make_async_copy(block, block, sem).wait()


def exchange(
    gate_a_in, cot_a_in, gate_b_in, table_in, row_ids, slots, weights,
    mixed_b, grad_gate, grad_weights, grad_table,
    gate_a, cot_a, gate_b, col, slots_t, weights_t, mix_wide, mix_tall, wide_list,
    message, asked, codes, grads_out, arrived, rows_out, fetched, grad_memory, scores,
    rs_out, rs_in,
    load, ask_send, ask_recv, tab_send, tab_recv, par_send, par_recv,
    grad_send, grad_recv, row_send, row_recv, rs_send, rs_recv,
):
    sections = lax.axis_size("section")
    owners = lax.axis_size("table")
    plane = owners // LAYERS
    rows_dev, features = table_in.shape
    tokens = gate_a.shape[0]
    listed = row_ids.shape[1]
    part = features // sections
    group = sections * plane
    width = codes.shape[2] - asked_width(group)
    piece = features // PIECES
    last = LAYERS - 1

    sec = lax.axis_index("section")
    me = lax.axis_index("table")
    z = me // plane
    p_me = lax.rem(me, plane)
    seat = sec * plane + p_me
    parity = lax.rem(sec, 2)
    partner = sec + 1 - 2 * parity
    step_z = 1 - 2 * parity
    ahead_ok = (z + step_z >= 0) & (z + step_z <= last)

    def peer(hop):
        if plane & (plane - 1):
            return lax.rem(p_me + hop, plane)
        other, bit = p_me, 1
        while bit < plane:
            if hop & bit:
                other = other + bit - 2 * bit * lax.rem(p_me // bit, 2)
            bit *= 2
        return other

    def other_section(hop):
        return lax.rem(sec + hop, sections)

    def at(layer, place):
        return layer * plane + place

    def greet(s, t):
        pl.semaphore_signal(
            pltpu.get_barrier_semaphore(), inc=1,
            device_id={"section": s, "table": t}, device_id_type=MESH,
        )

    def remote(source, target, send, recv, s, t):
        pltpu.make_async_remote_copy(
            src_ref=source, dst_ref=target, send_sem=send, recv_sem=recv,
            device_id={"section": s, "table": t}, device_id_type=MESH,
        ).start()

    for hop in range(plane):
        for turn in range(sections):
            if hop or turn:
                greet(other_section(turn), at(z, peer(hop)))

    @pl.when(z > 0)
    def _():
        greet(sec, at(z - 1, p_me))

    @pl.when(z < last)
    def _():
        greet(sec, at(z + 1, p_me))

    pltpu.make_async_copy(table_in, col.at[z], load.at[0]).start()
    pltpu.make_async_copy(gate_a_in, gate_a, load.at[1]).start()
    pltpu.make_async_copy(cot_a_in, cot_a, load.at[2]).start()
    pltpu.make_async_copy(gate_b_in, gate_b, load.at[3]).start()

    ids = row_ids[...]
    rank_a, spot_a, held_a = locate(ids[0:1], owners, plane, rows_dev)
    rank_b, spot_b, held_b = locate(ids[1:2], owners, plane, rows_dev)
    lane = iota((codes.shape[2], listed), 0)
    base = p_me * (2 * ROW_LIMIT)
    lanes_a = hot((lane == rank_a + base) | (lane == rank_a + (seat * ROW_LIMIT + width)))
    lanes_b = hot(lane == rank_b + (base + ROW_LIMIT))
    asking = contract(held_a, lanes_a, ((1,), (1,))) + contract(held_b, lanes_b, ((1,), (1,)))
    for q in range(plane):
        message[q] = asking[q * LAYERS : (q + 1) * LAYERS]

    signals = group - 1 + jnp.where(z > 0, 1, 0) + jnp.where(z < last, 1, 0)
    pl.semaphore_wait(pltpu.get_barrier_semaphore(), signals)

    drain(col.at[z], load.at[0])

    @pl.when(ahead_ok)
    def _():
        remote(col.at[z], col.at[z], tab_send, tab_recv.at[z], sec, at(z + step_z, p_me))

    for hop in range(plane):
        q = peer(hop)
        for turn in range(sections):
            if hop or turn:
                remote(
                    message.at[q], asked.at[seat], ask_send, ask_recv,
                    other_section(turn), at(z, q),
                )
    pltpu.make_async_copy(message.at[p_me], asked.at[seat], ask_recv).start()

    slots_t[...] = jnp.transpose(slots[...].reshape(2 * tokens, -1).astype(F32))
    weights_t[...] = jnp.transpose(weights[...].reshape(2 * tokens, -1))
    mixing_t = mix_picks(slots_t, weights_t, listed).astype(BF16)
    space = iota((owners * 2 * ROW_LIMIT, listed), 0)
    wide_a = hot(space == spot_a * (2 * ROW_LIMIT) + rank_a)
    wide_b = hot(space == spot_b * (2 * ROW_LIMIT) + (rank_b + ROW_LIMIT))
    tall_a = hot(iota((owners * ROW_LIMIT, listed), 0) == spot_a * ROW_LIMIT + rank_a)
    wide_list[...] = wide_a
    mix_tall[...] = contract(tall_a, mixing_t[:, :tokens], ((1,), (0,))).astype(BF16)

    drain(gate_a, load.at[1])
    drain(cot_a, load.at[2])
    for half in range(sections):

        @pl.loop(0, part // CHUNK)
        def _(c):
            inner = pl.ds(pl.multiple_of(c * CHUNK, CHUNK), CHUNK)
            cols = pl.ds(pl.multiple_of(half * part + c * CHUNK, CHUNK), CHUNK)
            gate = gate_a[:, cols].astype(F32)
            value = (cot_a[:, cols].astype(F32) * gate * jax.nn.sigmoid(gate)).astype(BF16)
            grad_memory[:, cols] = value
            rows = contract(mix_tall[...], value, ((1,), (0,))).astype(BF16)
            grads_out[half, :, :, :, inner] = rows.reshape(plane, LAYERS, ROW_LIMIT, CHUNK)

        for hop in range(1, plane):
            q = peer(hop)
            remote(
                grads_out.at[half, q], arrived.at[:, seat], grad_send, grad_recv, half, at(z, q)
            )

        @pl.when(sec == half)
        def _():
            pltpu.make_async_copy(
                grads_out.at[half, p_me], arrived.at[:, seat], grad_recv
            ).start()

        @pl.when(sec != half)
        def _():
            remote(
                grads_out.at[half, p_me], arrived.at[:, seat], grad_send, grad_recv, half, me
            )

    drain(asked, ask_recv)
    serving, summing = asked[sec * plane, :, :width], asked[0, :, width:]
    for q in range(1, plane):
        serving = serving + asked[sec * plane + q, :, :width]
    for q in range(1, group):
        summing = summing + asked[q, :, width:]
    for layer in range(LAYERS):
        codes[layer, :, :width] = serving[layer : layer + 1]
        codes[layer, :, width:] = summing[layer : layer + 1]

    def serve(layer):
        code = codes[layer, :, :width]
        pick = (iota((rows_dev, width), 0).astype(F32) == code - 1.0).astype(F32)
        pick = jnp.transpose(pick)[: plane * 2 * ROW_LIMIT].astype(BF16)
        for c in range(PIECES):
            for k in range(piece // CHUNK):
                cols = pl.ds(c * piece + k * CHUNK, CHUNK)
                rows = contract(pick, col[layer, :, cols], ((1,), (0,))).astype(BF16)
                rows_out[layer, :, :, cols] = rows.reshape(plane, 2 * ROW_LIMIT, CHUNK)
            cols = pl.ds(c * piece, piece)
            for hop in range(1, plane):
                q = peer(hop)
                remote(
                    rows_out.at[layer, q, :, cols], fetched.at[p_me, layer, :, cols],
                    row_send, row_recv.at[c], sec, at(z, q),
                )
            pltpu.make_async_copy(
                rows_out.at[layer, p_me, :, cols], fetched.at[p_me, layer, :, cols],
                row_recv.at[c],
            ).start()

    def summed(layer, cols):
        code = codes[layer, :, width:][:, : group * ROW_LIMIT]
        pick = hot(iota((rows_dev, group * ROW_LIMIT), 0).astype(F32) == code - 1.0)
        block = arrived[layer, :, :, cols].reshape(group * ROW_LIMIT, -1)
        return contract(pick, block, ((1,), (0,)))

    def table_hop(h):
        behind, ahead = z - step_z * h, z + step_z * h

        @pl.when((behind >= 0) & (behind <= last))
        def _():
            drain(col.at[behind], tab_recv.at[behind])

            @pl.when(ahead_ok)
            def _():
                remote(
                    col.at[behind], col.at[behind], tab_send, tab_recv.at[behind],
                    sec, at(z + step_z, p_me),
                )

            remote(col.at[behind], col.at[behind], par_send, par_recv.at[behind], partner, me)
            serve(behind)

        @pl.when((ahead >= 0) & (ahead <= last))
        def _():
            drain(col.at[ahead], par_recv.at[ahead])
            serve(ahead)

    def reduce_step(k):
        for way in range(2):
            place = z if way == 0 else last - z
            far = last - (k - place)
            layer = far if way == 0 else last - far
            target = z + 1 if way == 0 else z - 1

            def pass_on(earlier):
                @pl.loop(0, part // CHUNK)
                def _(c):
                    cols = pl.ds(pl.multiple_of(c * CHUNK, CHUNK), CHUNK)
                    total = summed(layer, cols)
                    if earlier:
                        total = total + rs_in[way, k - 1, :, cols].astype(F32)
                    rs_out[way, k, :, cols] = total.astype(BF16)

                remote(
                    rs_out.at[way, k], rs_in.at[way, k], rs_send, rs_recv.at[way, k],
                    sec, at(target, p_me),
                )

            @pl.when(place == 0)
            def _():
                pass_on(False)

            if k:

                @pl.when((place > 0) & (place <= k))
                def _():
                    drain(rs_in.at[way, k - 1], rs_recv.at[way, k - 1])
                    pass_on(True)

    serve(z)
    table_hop(1)

    mix_wide[:tokens] = contract(mixing_t[:, :tokens], wide_a, ((0,), (1,))).astype(BF16)
    mix_wide[tokens:] = contract(mixing_t[:, tokens:], wide_b, ((0,), (1,))).astype(BF16)
    scores[...] = jnp.zeros_like(scores)
    drain(arrived, grad_recv)

    for h in range(2, LAYERS):
        reduce_step(h - 2)
        table_hop(h)
    reduce_step(LAYERS - 2)

    drain(gate_b, load.at[3])
    for c in range(PIECES):
        drain(fetched.at[:, :, :, pl.ds(c * piece, piece)], row_recv.at[c])
        for k in range(piece // CHUNK):
            cols = pl.ds(c * piece + k * CHUNK, CHUNK)
            rows = fetched[:, :, :, cols].reshape(owners * 2 * ROW_LIMIT, CHUNK)
            memory = contract(mix_wide[...], rows, ((1,), (0,)))
            gate = gate_a[:, cols].astype(F32)
            sig = jax.nn.sigmoid(gate)
            incoming = cot_a[:, cols].astype(F32)
            grad_gate[:, cols] = (
                incoming * memory[:tokens] * sig * (1.0 + gate * (1.0 - sig))
            ).astype(BF16)
            scores[...] += contract(grad_memory[:, cols], rows, ((1,), (1,)))
            gate = gate_b[:, cols].astype(F32)
            mixed_b[:, cols] = (gate * jax.nn.sigmoid(gate) * memory[tokens:]).astype(BF16)

    found = contract(
        scores[...], wide_list[...].astype(F32), ((1,), (0,)), precision=lax.Precision.HIGHEST
    )
    grad_weights[...] = jnp.take_along_axis(found, slots[0], axis=1)

    @pl.loop(0, part // CHUNK)
    def _(c):
        cols = pl.ds(pl.multiple_of(c * CHUNK, CHUNK), CHUNK)
        grad_table[:, cols] = summed(z, cols)

    for way in range(2):

        @pl.when((z > 0) if way == 0 else (z < last))
        def _():
            drain(rs_in.at[way, last - 1], rs_recv.at[way, last - 1])
            grad_table[...] += rs_in[way, last - 1].astype(F32)

    drain(asked.at[pl.ds(0, group - 1)], ask_send)
    drain(arrived.at[:, pl.ds(0, group - 1)], grad_send)
    drain(rows_out.at[:, pl.ds(0, plane - 1)], row_send)

    @pl.when(ahead_ok)
    def _():
        drain(col.at[z], tab_send)

    for h in range(1, LAYERS):
        behind = z - step_z * h

        @pl.when((behind >= 0) & (behind <= last))
        def _():
            drain(col.at[behind], par_send)

            @pl.when(ahead_ok)
            def _():
                drain(col.at[behind], tab_send)

    for k in range(last):
        for way in range(2):

            @pl.when(k >= (z if way == 0 else last - z))
            def _():
                drain(rs_out.at[way, k], rs_send)


def asked_width(group):
    return -(-group * ROW_LIMIT // 128) * 128


def local(gate_a, cotangent_a, gate_b, table, row_ids, slots, weights):
    owners = lax.axis_size("table")
    sections = lax.axis_size("section")
    plane = owners // LAYERS
    group = sections * plane
    rows_dev, features = table.shape
    tokens = gate_a.shape[1]
    listed = row_ids.shape[-1]
    picks = slots.shape[-1]
    part = features // sections
    lanes = -(-plane * 2 * ROW_LIMIT // 128) * 128 + asked_width(group)
    slot_rows = owners * 2 * ROW_LIMIT
    vmem = pl.BlockSpec(memory_space=pltpu.VMEM)
    hbm = pl.BlockSpec(memory_space=pl.ANY)
    dma = pltpu.SemaphoreType.DMA
    mixed_b, grad_gate, grad_weights, grad_table = pl.pallas_call(
        exchange,
        out_shape=(
            pltpu.VMEM((tokens, features), BF16),
            pltpu.VMEM((tokens, features), BF16),
            pltpu.VMEM((tokens, picks), F32),
            pltpu.VMEM((rows_dev, part), F32),
        ),
        in_specs=[hbm] * 4 + [vmem] * 3,
        out_specs=(vmem,) * 4,
        scratch_shapes=[
            pltpu.VMEM((tokens, features), BF16),
            pltpu.VMEM((tokens, features), BF16),
            pltpu.VMEM((tokens, features), BF16),
            pltpu.VMEM((LAYERS, rows_dev, features), BF16),
            pltpu.VMEM((picks, 2 * tokens), F32),
            pltpu.VMEM((picks, 2 * tokens), F32),
            pltpu.VMEM((2 * tokens, slot_rows), BF16),
            pltpu.VMEM((owners * ROW_LIMIT, tokens), BF16),
            pltpu.VMEM((slot_rows, listed), BF16),
            pltpu.VMEM((plane, LAYERS, lanes), F32),
            pltpu.VMEM((group, LAYERS, lanes), F32),
            pltpu.VMEM((LAYERS, 1, lanes), F32),
            pltpu.VMEM((sections, plane, LAYERS, ROW_LIMIT, part), BF16),
            pltpu.VMEM((LAYERS, group, ROW_LIMIT, part), BF16),
            pltpu.VMEM((LAYERS, plane, 2 * ROW_LIMIT, features), BF16),
            pltpu.VMEM((plane, LAYERS, 2 * ROW_LIMIT, features), BF16),
            pltpu.VMEM((tokens, features), BF16),
            pltpu.VMEM((tokens, slot_rows), F32),
            pltpu.VMEM((2, LAYERS - 1, rows_dev, part), BF16),
            pltpu.VMEM((2, LAYERS - 1, rows_dev, part), BF16),
            dma((4,)),
            dma, dma,
            dma, dma((LAYERS,)),
            dma, dma((LAYERS,)),
            dma, dma,
            dma, dma((PIECES,)),
            dma, dma((2, LAYERS - 1)),
        ],
        compiler_params=pltpu.CompilerParams(
            collective_id=0, has_side_effects=True, vmem_limit_bytes=60 * 1024 * 1024
        ),
    )(
        gate_a[0], cotangent_a[0], gate_b[0], table, row_ids[0, :, 0], slots[0], weights[0]
    )
    return mixed_b[None], grad_gate[None], grad_weights[None], grad_table


def solution(mesh):
    return jax.shard_map(
        local,
        mesh=mesh,
        in_specs=(
            P("section", "table", None),
            P("section", "table", None),
            P("section", "table", None),
            P("table", None),
            P("section", None, "table", None),
            P("section", None, "table", None),
            P("section", None, "table", None),
        ),
        out_specs=(
            P("section", "table", None),
            P("section", "table", None),
            P("section", "table", None),
            P("table", "section"),
        ),
        check_vma=False,
    )
```

```python
import jax
import jax.numpy as jnp
from jax import lax
from jax.experimental import pallas as pl
from jax.experimental.pallas import tpu as pltpu
from jax.sharding import PartitionSpec as P

ROW_LIMIT = 8
CHUNK = 512
LAYERS = 4
PIECES = 4
UNROLL = 8
MESH = pl.DeviceIdType.MESH
BF16, F32 = jnp.bfloat16, jnp.float32


def iota(shape, axis):
    return lax.broadcasted_iota(jnp.int32, shape, axis)


def hot(mask):
    return mask.astype(F32).astype(BF16)


def contract(lhs, rhs, dims, **options):
    return lax.dot_general(lhs, rhs, (dims, ((), ())), preferred_element_type=F32, **options)


def locate(ids, owners, plane, rows_dev):
    listed = ids.shape[1]
    line = iota((owners, listed), 0)
    layer = line & (LAYERS - 1)
    column = lax.shift_right_logical(line, LAYERS.bit_length() - 1)
    first = (layer * plane + column) * rows_dev
    member = ((ids >= first) & (ids < first + rows_dev)).astype(F32)
    before = iota((listed, listed), 0) < iota((listed, listed), 1)
    earlier = contract(member.astype(BF16), hot(before), ((1,), (0,)))
    rank = jnp.sum(member * earlier, axis=0, keepdims=True).astype(jnp.int32)
    spot = jnp.sum(member * line.astype(F32), axis=0, keepdims=True).astype(jnp.int32)
    start = jnp.sum(member * first.astype(F32), axis=0, keepdims=True).astype(jnp.int32)
    held = (member * (ids - start + 1).astype(F32)).astype(BF16)
    return rank, spot, held


def mix_picks(slots_t, weights_t, listed):
    picks, tokens = slots_t.shape
    position = iota((listed, tokens), 0).astype(F32)

    def group(g, total):
        base = pl.multiple_of(g * UNROLL, UNROLL)
        slot = slots_t[pl.ds(base, UNROLL), :]
        weight = weights_t[pl.ds(base, UNROLL), :]
        for p in range(UNROLL):
            hit = slot[p : p + 1] == position
            total = total + jnp.where(hit, weight[p : p + 1], 0.0)
        return total

    start = jnp.zeros((listed, tokens), F32)
    return lax.fori_loop(0, picks // UNROLL, group, start)


def drain(block, sem):
    pltpu.make_async_copy(block, block, sem).wait()


def exchange(
    gate_a_in, cot_a_in, gate_b_in, table_in, row_ids, slots, weights,
    mixed_b, grad_gate, grad_weights, grad_table,
    gate_a, cot_a, gate_b, col, slots_t, weights_t, mix_wide, mix_tall, wide_list,
    message, asked, codes, grads_out, arrived, rows_out, fetched, grad_memory, scores,
    rs_out, rs_in,
    load, ask_send, ask_recv, tab_send, tab_recv, par_send, par_recv,
    grad_send, grad_recv, row_send, row_recv, rs_send, rs_recv,
):
    sections = lax.axis_size("section")
    owners = lax.axis_size("table")
    plane = owners // LAYERS
    rows_dev, features = table_in.shape
    tokens = gate_a.shape[0]
    listed = row_ids.shape[1]
    part = features // sections
    group = sections * plane
    width = codes.shape[2] - asked_width(group)
    piece = features // PIECES
    last = LAYERS - 1

    sec = lax.axis_index("section")
    me = lax.axis_index("table")
    z = me // plane
    p_me = lax.rem(me, plane)
    seat = sec * plane + p_me
    parity = lax.rem(sec, 2)
    partner = sec + 1 - 2 * parity
    step_z = 1 - 2 * parity
    ahead_ok = (z + step_z >= 0) & (z + step_z <= last)

    def peer(hop):
        if plane & (plane - 1):
            return lax.rem(p_me + hop, plane)
        other, bit = p_me, 1
        while bit < plane:
            if hop & bit:
                other = other + bit - 2 * bit * lax.rem(p_me // bit, 2)
            bit *= 2
        return other

    def other_section(hop):
        return lax.rem(sec + hop, sections)

    def need(k):
        return jnp.where(z < LAYERS // 2, last - k, k)

    def at(layer, place):
        return layer * plane + place

    def greet(s, t):
        pl.semaphore_signal(
            pltpu.get_barrier_semaphore(), inc=1,
            device_id={"section": s, "table": t}, device_id_type=MESH,
        )

    def remote(source, target, send, recv, s, t):
        pltpu.make_async_remote_copy(
            src_ref=source, dst_ref=target, send_sem=send, recv_sem=recv,
            device_id={"section": s, "table": t}, device_id_type=MESH,
        ).start()

    for hop in range(plane):
        for turn in range(sections):
            if hop or turn:
                greet(other_section(turn), at(z, peer(hop)))

    @pl.when(z > 0)
    def _():
        greet(sec, at(z - 1, p_me))

    @pl.when(z < last)
    def _():
        greet(sec, at(z + 1, p_me))

    pltpu.make_async_copy(table_in, col.at[z], load.at[0]).start()
    pltpu.make_async_copy(gate_a_in, gate_a, load.at[1]).start()
    pltpu.make_async_copy(cot_a_in, cot_a, load.at[2]).start()
    pltpu.make_async_copy(gate_b_in, gate_b, load.at[3]).start()

    ids = row_ids[...]
    rank_a, spot_a, held_a = locate(ids[0:1], owners, plane, rows_dev)
    rank_b, spot_b, held_b = locate(ids[1:2], owners, plane, rows_dev)
    lane = iota((codes.shape[2], listed), 0)
    base = p_me * (2 * ROW_LIMIT)
    lanes_a = hot((lane == rank_a + base) | (lane == rank_a + (seat * ROW_LIMIT + width)))
    lanes_b = hot(lane == rank_b + (base + ROW_LIMIT))
    asking = contract(held_a, lanes_a, ((1,), (1,))) + contract(held_b, lanes_b, ((1,), (1,)))
    for q in range(plane):
        message[q] = asking[q * LAYERS : (q + 1) * LAYERS]

    slots_t[...] = jnp.transpose(slots[...].reshape(2 * tokens, -1).astype(F32))
    weights_t[...] = jnp.transpose(weights[...].reshape(2 * tokens, -1))
    mixing_t = mix_picks(slots_t, weights_t, listed).astype(BF16)
    space = iota((owners * 2 * ROW_LIMIT, listed), 0)
    wide_a = hot(space == spot_a * (2 * ROW_LIMIT) + rank_a)
    wide_b = hot(space == spot_b * (2 * ROW_LIMIT) + (rank_b + ROW_LIMIT))
    tall_a = hot(iota((owners * ROW_LIMIT, listed), 0) == spot_a * ROW_LIMIT + rank_a)
    wide_list[...] = wide_a
    mix_tall[...] = contract(tall_a, mixing_t[:, :tokens], ((1,), (0,))).astype(BF16)

    signals = group - 1 + jnp.where(z > 0, 1, 0) + jnp.where(z < last, 1, 0)
    pl.semaphore_wait(pltpu.get_barrier_semaphore(), signals)

    drain(col.at[z], load.at[0])

    @pl.when(ahead_ok)
    def _():
        for c in range(PIECES):
            block = col.at[z, :, pl.ds(c * piece, piece)]
            remote(block, block, tab_send, tab_recv.at[z, c], sec, at(z + step_z, p_me))

    for hop in range(plane):
        q = peer(hop)
        for turn in range(sections):
            if hop or turn:
                remote(
                    message.at[q], asked.at[seat], ask_send, ask_recv,
                    other_section(turn), at(z, q),
                )
    pltpu.make_async_copy(message.at[p_me], asked.at[seat], ask_recv).start()

    drain(gate_a, load.at[1])
    drain(cot_a, load.at[2])
    for half in range(sections):

        @pl.loop(0, part // CHUNK)
        def _(c):
            inner = pl.ds(pl.multiple_of(c * CHUNK, CHUNK), CHUNK)
            cols = pl.ds(pl.multiple_of(half * part + c * CHUNK, CHUNK), CHUNK)
            gate = gate_a[:, cols].astype(F32)
            value = (cot_a[:, cols].astype(F32) * gate * jax.nn.sigmoid(gate)).astype(BF16)
            grad_memory[:, cols] = value
            rows = contract(mix_tall[...], value, ((1,), (0,))).astype(BF16)
            grads_out[half, :, :, :, inner] = rows.reshape(plane, LAYERS, ROW_LIMIT, CHUNK)

        for k in range(LAYERS):
            layer = need(k)
            for hop in range(1, plane):
                q = peer(hop)
                remote(
                    grads_out.at[half, q, layer], arrived.at[layer, seat],
                    grad_send, grad_recv.at[layer], half, at(z, q),
                )

            @pl.when(sec == half)
            def _():
                pltpu.make_async_copy(
                    grads_out.at[half, p_me, layer], arrived.at[layer, seat], grad_recv.at[layer]
                ).start()

            @pl.when(sec != half)
            def _():
                remote(
                    grads_out.at[half, p_me, layer], arrived.at[layer, seat],
                    grad_send, grad_recv.at[layer], half, me,
                )

    drain(asked, ask_recv)
    serving, summing = asked[sec * plane, :, :width], asked[0, :, width:]
    for q in range(1, plane):
        serving = serving + asked[sec * plane + q, :, :width]
    for q in range(1, group):
        summing = summing + asked[q, :, width:]
    for layer in range(LAYERS):
        codes[layer, :, :width] = serving[layer : layer + 1]
        codes[layer, :, width:] = summing[layer : layer + 1]

    def lookup(layer):
        code = codes[layer, :, :width]
        pick = (iota((rows_dev, width), 0).astype(F32) == code - 1.0).astype(F32)
        return jnp.transpose(pick)[: plane * 2 * ROW_LIMIT].astype(BF16)

    def serve(layer, pick, c):
        for k in range(piece // CHUNK):
            cols = pl.ds(c * piece + k * CHUNK, CHUNK)
            rows = contract(pick, col[layer, :, cols], ((1,), (0,))).astype(BF16)
            rows_out[layer, :, :, cols] = rows.reshape(plane, 2 * ROW_LIMIT, CHUNK)
        cols = pl.ds(c * piece, piece)
        for hop in range(1, plane):
            q = peer(hop)
            remote(
                rows_out.at[layer, q, :, cols], fetched.at[p_me, layer, :, cols],
                row_send, row_recv.at[c], sec, at(z, q),
            )
        pltpu.make_async_copy(
            rows_out.at[layer, p_me, :, cols], fetched.at[p_me, layer, :, cols], row_recv.at[c]
        ).start()

    def summed(layer, cols):
        code = codes[layer, :, width:][:, : group * ROW_LIMIT]
        pick = hot(iota((rows_dev, group * ROW_LIMIT), 0).astype(F32) == code - 1.0)
        block = arrived[layer, :, :, cols].reshape(group * ROW_LIMIT, -1)
        return contract(pick, block, ((1,), (0,)))

    def table_hop(h):
        behind, ahead = z - step_z * h, z + step_z * h

        @pl.when((behind >= 0) & (behind <= last))
        def _():
            pick = lookup(behind)
            for c in range(PIECES):
                block = col.at[behind, :, pl.ds(c * piece, piece)]
                drain(block, tab_recv.at[behind, c])

                @pl.when(ahead_ok)
                def _():
                    remote(
                        block, block, tab_send, tab_recv.at[behind, c],
                        sec, at(z + step_z, p_me),
                    )

                remote(block, block, par_send, par_recv.at[behind, c], partner, me)
                serve(behind, pick, c)

        @pl.when((ahead >= 0) & (ahead <= last))
        def _():
            pick = lookup(ahead)
            for c in range(PIECES):
                drain(col.at[ahead, :, pl.ds(c * piece, piece)], par_recv.at[ahead, c])
                serve(ahead, pick, c)

    def reduce_step(k):
        for way in range(2):
            place = z if way == 0 else last - z
            far = last - (k - place)
            layer = far if way == 0 else last - far
            target = z + 1 if way == 0 else z - 1

            def pass_on(earlier):
                for c in range(2):
                    cols = pl.ds(c * (part // 2), part // 2)
                    if earlier:
                        drain(rs_in.at[way, k - 1, :, cols], rs_recv.at[way, k - 1, c])
                    total = summed(layer, cols)
                    if earlier:
                        total = total + rs_in[way, k - 1, :, cols].astype(F32)
                    rs_out[way, k, :, cols] = total.astype(BF16)
                    remote(
                        rs_out.at[way, k, :, cols], rs_in.at[way, k, :, cols],
                        rs_send, rs_recv.at[way, k, c], sec, at(target, p_me),
                    )

            @pl.when(place <= k)
            def _():
                drain(arrived.at[layer], grad_recv.at[layer])

            @pl.when(place == 0)
            def _():
                pass_on(False)

            if k:

                @pl.when((place > 0) & (place <= k))
                def _():
                    pass_on(True)

    pick = lookup(z)
    for c in range(PIECES):
        serve(z, pick, c)
    reduce_step(0)
    table_hop(1)

    mix_wide[:tokens] = contract(mixing_t[:, :tokens], wide_a, ((0,), (1,))).astype(BF16)
    mix_wide[tokens:] = contract(mixing_t[:, tokens:], wide_b, ((0,), (1,))).astype(BF16)
    scores[...] = jnp.zeros_like(scores)

    for h in range(2, LAYERS):
        table_hop(h)
        reduce_step(h - 1)

    drain(arrived.at[z], grad_recv.at[z])

    @pl.loop(0, part // CHUNK)
    def _(c):
        cols = pl.ds(pl.multiple_of(c * CHUNK, CHUNK), CHUNK)
        grad_table[:, cols] = summed(z, cols)

    drain(gate_b, load.at[3])
    for c in range(PIECES):
        drain(fetched.at[:, :, :, pl.ds(c * piece, piece)], row_recv.at[c])
        for k in range(piece // CHUNK):
            cols = pl.ds(c * piece + k * CHUNK, CHUNK)
            rows = fetched[:, :, :, cols].reshape(owners * 2 * ROW_LIMIT, CHUNK)
            memory = contract(mix_wide[...], rows, ((1,), (0,)))
            gate = gate_a[:, cols].astype(F32)
            sig = jax.nn.sigmoid(gate)
            incoming = cot_a[:, cols].astype(F32)
            grad_gate[:, cols] = (
                incoming * memory[:tokens] * sig * (1.0 + gate * (1.0 - sig))
            ).astype(BF16)
            scores[...] += contract(grad_memory[:, cols], rows, ((1,), (1,)))
            gate = gate_b[:, cols].astype(F32)
            mixed_b[:, cols] = (gate * jax.nn.sigmoid(gate) * memory[tokens:]).astype(BF16)

    found = contract(
        scores[...], wide_list[...].astype(F32), ((1,), (0,)), precision=lax.Precision.HIGHEST
    )
    grad_weights[...] = jnp.take_along_axis(found, slots[0], axis=1)

    for way in range(2):

        @pl.when((z > 0) if way == 0 else (z < last))
        def _():
            for c in range(2):
                cols = pl.ds(c * (part // 2), part // 2)
                drain(rs_in.at[way, last - 1, :, cols], rs_recv.at[way, last - 1, c])
                grad_table[:, cols] += rs_in[way, last - 1, :, cols].astype(F32)

    drain(asked.at[pl.ds(0, group - 1)], ask_send)
    drain(arrived.at[:, pl.ds(0, group - 1)], grad_send)
    drain(rows_out.at[:, pl.ds(0, plane - 1)], row_send)

    @pl.when(ahead_ok)
    def _():
        drain(col.at[z], tab_send)

    for h in range(1, LAYERS):
        behind = z - step_z * h

        @pl.when((behind >= 0) & (behind <= last))
        def _():
            drain(col.at[behind], par_send)

            @pl.when(ahead_ok)
            def _():
                drain(col.at[behind], tab_send)

    for k in range(last):
        for way in range(2):

            @pl.when(k >= (z if way == 0 else last - z))
            def _():
                drain(rs_out.at[way, k], rs_send)


def store(mixed_b, grad_gate, grad_weights, grad_table, *refs):
    outs, sems = refs[:4], refs[4]
    copies = [
        pltpu.make_async_copy(source, target, sems.at[n])
        for n, (source, target) in enumerate(zip((mixed_b, grad_gate, grad_weights, grad_table), outs))
    ]
    for copy in copies:
        copy.start()
    for copy in copies:
        copy.wait()


def asked_width(group):
    return -(-group * ROW_LIMIT // 128) * 128


def local(gate_a, cotangent_a, gate_b, table, row_ids, slots, weights):
    owners = lax.axis_size("table")
    sections = lax.axis_size("section")
    plane = owners // LAYERS
    group = sections * plane
    rows_dev, features = table.shape
    tokens = gate_a.shape[1]
    listed = row_ids.shape[-1]
    picks = slots.shape[-1]
    part = features // sections
    lanes = -(-plane * 2 * ROW_LIMIT // 128) * 128 + asked_width(group)
    slot_rows = owners * 2 * ROW_LIMIT
    vmem = pl.BlockSpec(memory_space=pltpu.VMEM)
    hbm = pl.BlockSpec(memory_space=pl.ANY)
    dma = pltpu.SemaphoreType.DMA
    mixed_b, grad_gate, grad_weights, grad_table = pl.pallas_call(
        exchange,
        out_shape=(
            pltpu.VMEM((tokens, features), BF16),
            pltpu.VMEM((tokens, features), BF16),
            pltpu.VMEM((tokens, picks), F32),
            pltpu.VMEM((rows_dev, part), F32),
        ),
        in_specs=[hbm] * 4 + [vmem] * 3,
        out_specs=(vmem,) * 4,
        scratch_shapes=[
            pltpu.VMEM((tokens, features), BF16),
            pltpu.VMEM((tokens, features), BF16),
            pltpu.VMEM((tokens, features), BF16),
            pltpu.VMEM((LAYERS, rows_dev, features), BF16),
            pltpu.VMEM((picks, 2 * tokens), F32),
            pltpu.VMEM((picks, 2 * tokens), F32),
            pltpu.VMEM((2 * tokens, slot_rows), BF16),
            pltpu.VMEM((owners * ROW_LIMIT, tokens), BF16),
            pltpu.VMEM((slot_rows, listed), BF16),
            pltpu.VMEM((plane, LAYERS, lanes), F32),
            pltpu.VMEM((group, LAYERS, lanes), F32),
            pltpu.VMEM((LAYERS, 1, lanes), F32),
            pltpu.VMEM((sections, plane, LAYERS, ROW_LIMIT, part), BF16),
            pltpu.VMEM((LAYERS, group, ROW_LIMIT, part), BF16),
            pltpu.VMEM((LAYERS, plane, 2 * ROW_LIMIT, features), BF16),
            pltpu.VMEM((plane, LAYERS, 2 * ROW_LIMIT, features), BF16),
            pltpu.VMEM((tokens, features), BF16),
            pltpu.VMEM((tokens, slot_rows), F32),
            pltpu.VMEM((2, LAYERS - 1, rows_dev, part), BF16),
            pltpu.VMEM((2, LAYERS - 1, rows_dev, part), BF16),
            dma((4,)),
            dma, dma,
            dma, dma((LAYERS, PIECES)),
            dma, dma((LAYERS, PIECES)),
            dma, dma((LAYERS,)),
            dma, dma((PIECES,)),
            dma, dma((2, LAYERS - 1, 2)),
        ],
        compiler_params=pltpu.CompilerParams(
            collective_id=0, has_side_effects=True, vmem_limit_bytes=60 * 1024 * 1024
        ),
    )(
        gate_a[0], cotangent_a[0], gate_b[0], table, row_ids[0, :, 0], slots[0], weights[0]
    )
    results = (mixed_b, grad_gate, grad_weights, grad_table)
    mixed_b, grad_gate, grad_weights, grad_table = pl.pallas_call(
        store,
        out_shape=tuple(jax.ShapeDtypeStruct(r.shape, r.dtype) for r in results),
        in_specs=[vmem] * 4,
        out_specs=(hbm,) * 4,
        scratch_shapes=[dma((4,))],
    )(*(pltpu.with_memory_space_constraint(r, pltpu.VMEM) for r in results))
    return mixed_b[None], grad_gate[None], grad_weights[None], grad_table


def solution(mesh):
    return jax.shard_map(
        local,
        mesh=mesh,
        in_specs=(
            P("section", "table", None),
            P("section", "table", None),
            P("section", "table", None),
            P("table", None),
            P("section", None, "table", None),
            P("section", None, "table", None),
            P("section", None, "table", None),
        ),
        out_specs=(
            P("section", "table", None),
            P("section", "table", None),
            P("section", "table", None),
            P("table", "section"),
        ),
        check_vma=False,
    )
```

```python
import jax
import jax.numpy as jnp
from jax import lax
from jax.experimental import pallas as pl
from jax.experimental.pallas import tpu as pltpu
from jax.sharding import PartitionSpec as P

ROW_LIMIT = 8
CHUNK = 512
LAYERS = 4
PIECES = 4
UNROLL = 8
MESH = pl.DeviceIdType.MESH
BF16, F32 = jnp.bfloat16, jnp.float32


def iota(shape, axis):
    return lax.broadcasted_iota(jnp.int32, shape, axis)


def hot(mask):
    return mask.astype(F32).astype(BF16)


def contract(lhs, rhs, dims, **options):
    return lax.dot_general(lhs, rhs, (dims, ((), ())), preferred_element_type=F32, **options)


def locate(ids, owners, plane, rows_dev):
    listed = ids.shape[1]
    line = iota((owners, listed), 0)
    layer = line & (LAYERS - 1)
    column = lax.shift_right_logical(line, LAYERS.bit_length() - 1)
    first = (layer * plane + column) * rows_dev
    member = ((ids >= first) & (ids < first + rows_dev)).astype(F32)
    before = iota((listed, listed), 0) < iota((listed, listed), 1)
    earlier = contract(member.astype(BF16), hot(before), ((1,), (0,)))
    rank = jnp.sum(member * earlier, axis=0, keepdims=True).astype(jnp.int32)
    spot = jnp.sum(member * line.astype(F32), axis=0, keepdims=True).astype(jnp.int32)
    start = jnp.sum(member * first.astype(F32), axis=0, keepdims=True).astype(jnp.int32)
    held = (member * (ids - start + 1).astype(F32)).astype(BF16)
    return rank, spot, held


def mix_picks(slots_t, weights_t, listed):
    picks, tokens = slots_t.shape
    position = iota((listed, tokens), 0).astype(F32)

    def group(g, total):
        base = pl.multiple_of(g * UNROLL, UNROLL)
        slot = slots_t[pl.ds(base, UNROLL), :]
        weight = weights_t[pl.ds(base, UNROLL), :]
        for p in range(UNROLL):
            hit = slot[p : p + 1] == position
            total = total + jnp.where(hit, weight[p : p + 1], 0.0)
        return total

    start = jnp.zeros((listed, tokens), F32)
    return lax.fori_loop(0, picks // UNROLL, group, start)


def drain(block, sem):
    pltpu.make_async_copy(block, block, sem).wait()


def exchange(
    gate_a_in, cot_a_in, gate_b_in, table_in, row_ids, slots, weights,
    mixed_b, grad_gate, grad_weights, grad_table,
    gate_a, cot_a, gate_b, col, aux, slots_t, weights_t, mix_wide, mix_tall, wide_list,
    message, asked, asked_far, codes, codes_aux, grads_out, arrived, rows_out, rows_aux, fetched,
    grad_memory, scores,
    rs_out, rs_in,
    load, ask_send, ask_recv, far_recv, tab_send, tab_recv, par_send, par_recv, aux_recv,
    grad_send, grad_recv, row_send, row_recv, rs_send, rs_recv,
):
    sections = lax.axis_size("section")
    owners = lax.axis_size("table")
    plane = owners // LAYERS
    rows_dev, features = table_in.shape
    tokens = gate_a.shape[0]
    listed = row_ids.shape[1]
    part = features // sections
    group = sections * plane
    width = codes.shape[2] - asked_width(group)
    piece = features // PIECES
    last = LAYERS - 1

    sec = lax.axis_index("section")
    me = lax.axis_index("table")
    z = me // plane
    p_me = lax.rem(me, plane)
    seat = sec * plane + p_me
    parity = lax.rem(sec, 2)
    partner = sec + 1 - 2 * parity
    step_z = 1 - 2 * parity
    ahead_ok = (z + step_z >= 0) & (z + step_z <= last)

    def peer(hop):
        other, bit = p_me, 1
        while bit < plane:
            if hop & bit:
                other = other + bit - 2 * bit * lax.rem(p_me // bit, 2)
            bit *= 2
        return other

    x_side, y_side, corner = peer(1), peer(2), peer(3)

    def strip(c):
        if isinstance(c, int):
            return pl.ds(c * piece, piece)
        return pl.ds(pl.multiple_of(c * piece, piece), piece)

    def other_section(hop):
        return lax.rem(sec + hop, sections)

    def need(k):
        return jnp.where(z < LAYERS // 2, last - k, k)

    def at(layer, place):
        return layer * plane + place

    def greet(s, t):
        pl.semaphore_signal(
            pltpu.get_barrier_semaphore(), inc=1,
            device_id={"section": s, "table": t}, device_id_type=MESH,
        )

    def remote(source, target, send, recv, s, t):
        pltpu.make_async_remote_copy(
            src_ref=source, dst_ref=target, send_sem=send, recv_sem=recv,
            device_id={"section": s, "table": t}, device_id_type=MESH,
        ).start()

    for hop in range(plane):
        for turn in range(sections):
            if hop or turn:
                greet(other_section(turn), at(z, peer(hop)))

    @pl.when(z > 0)
    def _():
        greet(sec, at(z - 1, p_me))

    @pl.when(z < last)
    def _():
        greet(sec, at(z + 1, p_me))

    pltpu.make_async_copy(table_in, col.at[z], load.at[0]).start()
    pltpu.make_async_copy(gate_a_in, gate_a, load.at[1]).start()
    pltpu.make_async_copy(cot_a_in, cot_a, load.at[2]).start()
    pltpu.make_async_copy(gate_b_in, gate_b, load.at[3]).start()

    ids = row_ids[...]
    rank_a, spot_a, held_a = locate(ids[0:1], owners, plane, rows_dev)
    rank_b, spot_b, held_b = locate(ids[1:2], owners, plane, rows_dev)
    lane = iota((codes.shape[2], listed), 0)
    base = p_me * (2 * ROW_LIMIT)
    lanes_a = hot((lane == rank_a + base) | (lane == rank_a + (seat * ROW_LIMIT + width)))
    lanes_b = hot(lane == rank_b + (base + ROW_LIMIT))
    asking = contract(held_a, lanes_a, ((1,), (1,))) + contract(held_b, lanes_b, ((1,), (1,)))
    for q in range(plane):
        message[q] = asking[q * LAYERS : (q + 1) * LAYERS]

    slots_t[...] = jnp.transpose(slots[...].reshape(2 * tokens, -1).astype(F32))
    weights_t[...] = jnp.transpose(weights[...].reshape(2 * tokens, -1))
    mixing_t = mix_picks(slots_t, weights_t, listed).astype(BF16)
    space = iota((owners * 2 * ROW_LIMIT, listed), 0)
    wide_a = hot(space == spot_a * (2 * ROW_LIMIT) + rank_a)
    wide_b = hot(space == spot_b * (2 * ROW_LIMIT) + (rank_b + ROW_LIMIT))
    tall_a = hot(iota((owners * ROW_LIMIT, listed), 0) == spot_a * ROW_LIMIT + rank_a)
    wide_list[...] = wide_a
    mix_tall[...] = contract(tall_a, mixing_t[:, :tokens], ((1,), (0,))).astype(BF16)

    signals = group - 1 + jnp.where(z > 0, 1, 0) + jnp.where(z < last, 1, 0)
    pl.semaphore_wait(pltpu.get_barrier_semaphore(), signals)

    drain(col.at[z], load.at[0])

    @pl.when(ahead_ok)
    def _():
        for c in range(PIECES):
            block = col.at[z, :, pl.ds(c * piece, piece)]
            remote(block, block, tab_send, tab_recv.at[z, c], sec, at(z + step_z, p_me))

    for j, side in enumerate((x_side, y_side)):
        cols = strip(2 * j + parity)
        remote(
            col.at[z, :, cols], aux.at[z, :, cols], tab_send, aux_recv.at[z, 2 * j + parity],
            sec, at(z, side),
        )
        remote(
            message.at[corner], asked_far.at[1 - j], ask_send, far_recv, sec, at(z, side)
        )

    for hop in range(plane):
        q = peer(hop)
        for turn in range(sections):
            if hop or turn:
                remote(
                    message.at[q], asked.at[seat], ask_send, ask_recv,
                    other_section(turn), at(z, q),
                )
    pltpu.make_async_copy(message.at[p_me], asked.at[seat], ask_recv).start()

    drain(gate_a, load.at[1])
    drain(cot_a, load.at[2])
    for half in range(sections):

        @pl.loop(0, part // CHUNK)
        def _(c):
            inner = pl.ds(pl.multiple_of(c * CHUNK, CHUNK), CHUNK)
            cols = pl.ds(pl.multiple_of(half * part + c * CHUNK, CHUNK), CHUNK)
            gate = gate_a[:, cols].astype(F32)
            value = (cot_a[:, cols].astype(F32) * gate * jax.nn.sigmoid(gate)).astype(BF16)
            grad_memory[:, cols] = value
            rows = contract(mix_tall[...], value, ((1,), (0,))).astype(BF16)
            grads_out[half, :, :, :, inner] = rows.reshape(plane, LAYERS, ROW_LIMIT, CHUNK)

        for k in range(LAYERS):
            layer = need(k)
            for hop in range(1, plane):
                q = peer(hop)
                remote(
                    grads_out.at[half, q, layer], arrived.at[layer, seat],
                    grad_send, grad_recv.at[layer], half, at(z, q),
                )

            @pl.when(sec == half)
            def _():
                pltpu.make_async_copy(
                    grads_out.at[half, p_me, layer], arrived.at[layer, seat], grad_recv.at[layer]
                ).start()

            @pl.when(sec != half)
            def _():
                remote(
                    grads_out.at[half, p_me, layer], arrived.at[layer, seat],
                    grad_send, grad_recv.at[layer], half, me,
                )

    drain(asked, ask_recv)
    serving, summing = asked[sec * plane, :, :width], asked[0, :, width:]
    for q in range(1, plane):
        serving = serving + asked[sec * plane + q, :, :width]
    for q in range(1, group):
        summing = summing + asked[q, :, width:]
    for layer in range(LAYERS):
        codes[layer, :, :width] = serving[layer : layer + 1]
        codes[layer, :, width:] = summing[layer : layer + 1]

    drain(asked_far, far_recv)
    for j, side in enumerate((x_side, y_side)):
        serving = message[side, :, :width] + asked_far[j, :, :width]
        for layer in range(LAYERS):
            codes_aux[j, layer] = serving[layer : layer + 1]

    def lookup(code):
        pick = (iota((rows_dev, width), 0).astype(F32) == code - 1.0).astype(F32)
        return jnp.transpose(pick)[: plane * 2 * ROW_LIMIT].astype(BF16)

    def look_aside(layer):
        return [lookup(codes_aux[j, layer]) for j in range(2)]

    def find(pick, held, found, layer, c):
        for k in range(piece // CHUNK):
            cols = pl.ds(c * piece + k * CHUNK, CHUNK)
            rows = contract(pick, held[layer, :, cols], ((1,), (0,))).astype(BF16)
            found[layer, :, :, cols] = rows.reshape(plane, 2 * ROW_LIMIT, CHUNK)

    def give(found, layer, c, q, column):
        remote(
            found.at[layer, q, :, strip(c)], fetched.at[column, layer, :, strip(c)],
            row_send, row_recv.at[c], sec, at(z, q),
        )

    def keep(found, layer, c, column):
        pltpu.make_async_copy(
            found.at[layer, p_me, :, strip(c)], fetched.at[column, layer, :, strip(c)],
            row_recv.at[c],
        ).start()

    def serve(layer, pick, c, shared):
        find(pick, col, rows_out, layer, c)
        hops = [2 if c < PIECES // 2 else 1, *range(4, plane)] if shared else range(1, plane)
        for hop in hops:
            give(rows_out, layer, c, peer(hop), p_me)
        keep(rows_out, layer, c, p_me)

    def serve_aside(layer, picks, c):
        j = 2 * c // PIECES
        column, target = ((x_side, y_side), (y_side, x_side))[j]
        find(picks[j], aux, rows_aux, layer, c)
        give(rows_aux, layer, c, target, column)
        keep(rows_aux, layer, c, column)

    def summed(layer, cols):
        code = codes[layer, :, width:][:, : group * ROW_LIMIT]
        pick = hot(iota((rows_dev, group * ROW_LIMIT), 0).astype(F32) == code - 1.0)
        block = arrived[layer, :, :, cols].reshape(group * ROW_LIMIT, -1)
        return contract(pick, block, ((1,), (0,)))

    def table_hop(h):
        behind, ahead = z - step_z * h, z + step_z * h

        @pl.when((behind >= 0) & (behind <= last))
        def _():
            pick = lookup(codes[behind, :, :width])
            for c in range(PIECES):
                block = col.at[behind, :, pl.ds(c * piece, piece)]
                drain(block, tab_recv.at[behind, c])

                @pl.when(ahead_ok)
                def _():
                    remote(
                        block, block, tab_send, tab_recv.at[behind, c],
                        sec, at(z + step_z, p_me),
                    )

                remote(block, block, par_send, par_recv.at[behind, c], partner, me)
                serve(behind, pick, c, h == 1)

        @pl.when((ahead >= 0) & (ahead <= last))
        def _():
            pick = lookup(codes[ahead, :, :width])
            for c in range(PIECES):
                drain(col.at[ahead, :, pl.ds(c * piece, piece)], par_recv.at[ahead, c])
                serve(ahead, pick, c, h == 1)

    def own_aside():
        for j in range(2):
            c = 2 * j + parity
            block = aux.at[z, :, strip(c)]
            drain(block, aux_recv.at[z, c])
            remote(block, block, par_send, aux_recv.at[z, c], partner, me)

    def near_aside():
        behind, ahead = z - step_z, z + step_z

        @pl.when((behind >= 0) & (behind <= last))
        def _():
            picks = look_aside(behind)
            for c in range(PIECES):
                block = aux.at[behind, :, strip(c)]
                drain(block, aux_recv.at[behind, c])
                remote(block, block, par_send, aux_recv.at[behind, c], partner, me)
                serve_aside(behind, picks, c)

        @pl.when(ahead_ok)
        def _():
            picks = look_aside(ahead)
            for c in range(PIECES):
                drain(aux.at[ahead, :, strip(c)], aux_recv.at[ahead, c])
                serve_aside(ahead, picks, c)

    def reduce_step(k):
        for way in range(2):
            place = z if way == 0 else last - z
            far = last - (k - place)
            layer = far if way == 0 else last - far
            target = z + 1 if way == 0 else z - 1

            def pass_on(earlier):
                for c in range(2):
                    cols = pl.ds(c * (part // 2), part // 2)
                    if earlier:
                        drain(rs_in.at[way, k - 1, :, cols], rs_recv.at[way, k - 1, c])
                    total = summed(layer, cols)
                    if earlier:
                        total = total + rs_in[way, k - 1, :, cols].astype(F32)
                    rs_out[way, k, :, cols] = total.astype(BF16)
                    remote(
                        rs_out.at[way, k, :, cols], rs_in.at[way, k, :, cols],
                        rs_send, rs_recv.at[way, k, c], sec, at(target, p_me),
                    )

            @pl.when(place <= k)
            def _():
                drain(arrived.at[layer], grad_recv.at[layer])

            @pl.when(place == 0)
            def _():
                pass_on(False)

            if k:

                @pl.when((place > 0) & (place <= k))
                def _():
                    pass_on(True)

    own_aside()
    pick = lookup(codes[z, :, :width])
    for c in range(PIECES):
        serve(z, pick, c, True)
    for j in range(2):
        c = 2 * j + 1 - parity
        drain(aux.at[z, :, strip(c)], aux_recv.at[z, c])
    picks = look_aside(z)
    for c in range(PIECES):
        serve_aside(z, picks, c)
    reduce_step(0)
    table_hop(1)

    @pl.when(ahead_ok)
    def _():
        for c in range(PIECES):
            block = aux.at[z, :, strip(c)]
            remote(block, block, tab_send, aux_recv.at[z, c], sec, at(z + step_z, p_me))

    mix_wide[:tokens] = contract(mixing_t[:, :tokens], wide_a, ((0,), (1,))).astype(BF16)
    mix_wide[tokens:] = contract(mixing_t[:, tokens:], wide_b, ((0,), (1,))).astype(BF16)
    scores[...] = jnp.zeros_like(scores)

    for h in range(2, LAYERS):
        table_hop(h)
        reduce_step(h - 1)
        if h == 2:
            near_aside()

    drain(arrived.at[z], grad_recv.at[z])

    @pl.loop(0, part // CHUNK)
    def _(c):
        cols = pl.ds(pl.multiple_of(c * CHUNK, CHUNK), CHUNK)
        grad_table[:, cols] = summed(z, cols)

    drain(gate_b, load.at[3])
    for c in range(PIECES):
        drain(fetched.at[:, :, :, pl.ds(c * piece, piece)], row_recv.at[c])
        for k in range(piece // CHUNK):
            cols = pl.ds(c * piece + k * CHUNK, CHUNK)
            rows = fetched[:, :, :, cols].reshape(owners * 2 * ROW_LIMIT, CHUNK)
            memory = contract(mix_wide[...], rows, ((1,), (0,)))
            gate = gate_a[:, cols].astype(F32)
            sig = jax.nn.sigmoid(gate)
            incoming = cot_a[:, cols].astype(F32)
            grad_gate[:, cols] = (
                incoming * memory[:tokens] * sig * (1.0 + gate * (1.0 - sig))
            ).astype(BF16)
            scores[...] += contract(grad_memory[:, cols], rows, ((1,), (1,)))
            gate = gate_b[:, cols].astype(F32)
            mixed_b[:, cols] = (gate * jax.nn.sigmoid(gate) * memory[tokens:]).astype(BF16)

    found = contract(
        scores[...], wide_list[...].astype(F32), ((1,), (0,)), precision=lax.Precision.HIGHEST
    )
    grad_weights[...] = jnp.take_along_axis(found, slots[0], axis=1)

    for way in range(2):

        @pl.when((z > 0) if way == 0 else (z < last))
        def _():
            for c in range(2):
                cols = pl.ds(c * (part // 2), part // 2)
                drain(rs_in.at[way, last - 1, :, cols], rs_recv.at[way, last - 1, c])
                grad_table[:, cols] += rs_in[way, last - 1, :, cols].astype(F32)

    drain(asked.at[pl.ds(0, group - 1)], ask_send)
    drain(arrived.at[:, pl.ds(0, group - 1)], grad_send)
    drain(asked_far, ask_send)
    drain(rows_out.at[0, pl.ds(0, plane - 2)], row_send)
    for c in range(2):
        drain(col.at[z, :, strip(c)], tab_send)
        drain(col.at[z, :, strip(c)], par_send)

    @pl.when(ahead_ok)
    def _():
        drain(col.at[z], tab_send)
        drain(col.at[z], tab_send)

    for h in range(1, LAYERS):
        behind, ahead = z - step_z * h, z + step_z * h

        @pl.when((behind >= 0) & (behind <= last))
        def _():
            drain(rows_out.at[0, pl.ds(0, plane - (2 if h == 1 else 1))], row_send)
            drain(col.at[behind], par_send)
            if h == 1:
                drain(col.at[behind], par_send)

            @pl.when(ahead_ok)
            def _():
                drain(col.at[behind], tab_send)

        @pl.when((ahead >= 0) & (ahead <= last))
        def _():
            drain(rows_out.at[0, pl.ds(0, plane - (2 if h == 1 else 1))], row_send)

    for k in range(last):
        for way in range(2):

            @pl.when(k >= (z if way == 0 else last - z))
            def _():
                drain(rs_out.at[way, k], rs_send)


def store(mixed_b, grad_gate, grad_weights, grad_table, *refs):
    outs, sems = refs[:4], refs[4]
    copies = [
        pltpu.make_async_copy(source, target, sems.at[n])
        for n, (source, target) in enumerate(zip((mixed_b, grad_gate, grad_weights, grad_table), outs))
    ]
    for copy in copies:
        copy.start()
    for copy in copies:
        copy.wait()


def asked_width(group):
    return -(-group * ROW_LIMIT // 128) * 128


def local(gate_a, cotangent_a, gate_b, table, row_ids, slots, weights):
    owners = lax.axis_size("table")
    sections = lax.axis_size("section")
    plane = owners // LAYERS
    group = sections * plane
    rows_dev, features = table.shape
    tokens = gate_a.shape[1]
    listed = row_ids.shape[-1]
    picks = slots.shape[-1]
    part = features // sections
    lanes = -(-plane * 2 * ROW_LIMIT // 128) * 128 + asked_width(group)
    slot_rows = owners * 2 * ROW_LIMIT
    vmem = pl.BlockSpec(memory_space=pltpu.VMEM)
    hbm = pl.BlockSpec(memory_space=pl.ANY)
    dma = pltpu.SemaphoreType.DMA
    mixed_b, grad_gate, grad_weights, grad_table = pl.pallas_call(
        exchange,
        out_shape=(
            pltpu.VMEM((tokens, features), BF16),
            pltpu.VMEM((tokens, features), BF16),
            pltpu.VMEM((tokens, picks), F32),
            pltpu.VMEM((rows_dev, part), F32),
        ),
        in_specs=[hbm] * 4 + [vmem] * 3,
        out_specs=(vmem,) * 4,
        scratch_shapes=[
            pltpu.VMEM((tokens, features), BF16),
            pltpu.VMEM((tokens, features), BF16),
            pltpu.VMEM((tokens, features), BF16),
            pltpu.VMEM((LAYERS, rows_dev, features), BF16),
            pltpu.VMEM((LAYERS, rows_dev, features), BF16),
            pltpu.VMEM((picks, 2 * tokens), F32),
            pltpu.VMEM((picks, 2 * tokens), F32),
            pltpu.VMEM((2 * tokens, slot_rows), BF16),
            pltpu.VMEM((owners * ROW_LIMIT, tokens), BF16),
            pltpu.VMEM((slot_rows, listed), BF16),
            pltpu.VMEM((plane, LAYERS, lanes), F32),
            pltpu.VMEM((group, LAYERS, lanes), F32),
            pltpu.VMEM((2, LAYERS, lanes), F32),
            pltpu.VMEM((LAYERS, 1, lanes), F32),
            pltpu.VMEM((2, LAYERS, 1, lanes - asked_width(group)), F32),
            pltpu.VMEM((sections, plane, LAYERS, ROW_LIMIT, part), BF16),
            pltpu.VMEM((LAYERS, group, ROW_LIMIT, part), BF16),
            pltpu.VMEM((LAYERS, plane, 2 * ROW_LIMIT, features), BF16),
            pltpu.VMEM((LAYERS, plane, 2 * ROW_LIMIT, features), BF16),
            pltpu.VMEM((plane, LAYERS, 2 * ROW_LIMIT, features), BF16),
            pltpu.VMEM((tokens, features), BF16),
            pltpu.VMEM((tokens, slot_rows), F32),
            pltpu.VMEM((2, LAYERS - 1, rows_dev, part), BF16),
            pltpu.VMEM((2, LAYERS - 1, rows_dev, part), BF16),
            dma((4,)),
            dma, dma, dma,
            dma, dma((LAYERS, PIECES)),
            dma, dma((LAYERS, PIECES)), dma((LAYERS, PIECES)),
            dma, dma((LAYERS,)),
            dma, dma((PIECES,)),
            dma, dma((2, LAYERS - 1, 2)),
        ],
        compiler_params=pltpu.CompilerParams(
            collective_id=0, has_side_effects=True, vmem_limit_bytes=60 * 1024 * 1024
        ),
    )(
        gate_a[0], cotangent_a[0], gate_b[0], table, row_ids[0, :, 0], slots[0], weights[0]
    )
    results = (mixed_b, grad_gate, grad_weights, grad_table)
    mixed_b, grad_gate, grad_weights, grad_table = pl.pallas_call(
        store,
        out_shape=tuple(jax.ShapeDtypeStruct(r.shape, r.dtype) for r in results),
        in_specs=[vmem] * 4,
        out_specs=(hbm,) * 4,
        scratch_shapes=[dma((4,))],
    )(*(pltpu.with_memory_space_constraint(r, pltpu.VMEM) for r in results))
    return mixed_b[None], grad_gate[None], grad_weights[None], grad_table


def solution(mesh):
    return jax.shard_map(
        local,
        mesh=mesh,
        in_specs=(
            P("section", "table", None),
            P("section", "table", None),
            P("section", "table", None),
            P("table", None),
            P("section", None, "table", None),
            P("section", None, "table", None),
            P("section", None, "table", None),
        ),
        out_specs=(
            P("section", "table", None),
            P("section", "table", None),
            P("section", "table", None),
            P("table", "section"),
        ),
        check_vma=False,
    )
```

```python
import jax
import jax.numpy as jnp
from jax import lax
from jax.experimental import pallas as pl
from jax.experimental.pallas import tpu as pltpu
from jax.sharding import PartitionSpec as P

ROW_LIMIT = 8
CHUNK = 512
LAYERS = 4
PIECES = 4
HALVES = 2
UNROLL = 8
MESH = pl.DeviceIdType.MESH
BF16, F32 = jnp.bfloat16, jnp.float32


def iota(shape, axis):
    return lax.broadcasted_iota(jnp.int32, shape, axis)


def hot(mask):
    return mask.astype(F32).astype(BF16)


def contract(lhs, rhs, dims, **options):
    return lax.dot_general(lhs, rhs, (dims, ((), ())), preferred_element_type=F32, **options)


def locate(ids, owners, plane, rows_dev):
    listed = ids.shape[1]
    line = iota((owners, listed), 0)
    layer = line & (LAYERS - 1)
    column = lax.shift_right_logical(line, LAYERS.bit_length() - 1)
    first = (layer * plane + column) * rows_dev
    member = ((ids >= first) & (ids < first + rows_dev)).astype(F32)
    before = iota((listed, listed), 0) < iota((listed, listed), 1)
    earlier = contract(member.astype(BF16), hot(before), ((1,), (0,)))
    rank = jnp.sum(member * earlier, axis=0, keepdims=True).astype(jnp.int32)
    spot = jnp.sum(member * line.astype(F32), axis=0, keepdims=True).astype(jnp.int32)
    start = jnp.sum(member * first.astype(F32), axis=0, keepdims=True).astype(jnp.int32)
    held = (member * (ids - start + 1).astype(F32)).astype(BF16)
    return rank, spot, held


def mix_picks(slots_t, weights_t, listed):
    picks, tokens = slots_t.shape
    position = iota((listed, tokens), 0).astype(F32)

    def group(g, total):
        base = pl.multiple_of(g * UNROLL, UNROLL)
        slot = slots_t[pl.ds(base, UNROLL), :]
        weight = weights_t[pl.ds(base, UNROLL), :]
        for p in range(UNROLL):
            hit = slot[p : p + 1] == position
            total = total + jnp.where(hit, weight[p : p + 1], 0.0)
        return total

    start = jnp.zeros((listed, tokens), F32)
    return lax.fori_loop(0, picks // UNROLL, group, start)


def drain(block, sem):
    pltpu.make_async_copy(block, block, sem).wait()


def exchange(
    gate_a_in, cot_a_in, gate_b_in, table_in, row_ids_in, slots_in, weights_in,
    mixed_b, grad_gate, grad_weights, grad_table,
    gate_a, cot_a, gate_b, row_ids, slots, weights, col, aux, slots_t, weights_t, mix_wide, mix_tall, wide_list,
    message, asked, codes, codes_sum, codes_aux, grads_out, arrived, rows_out, rows_aux, fetched,
    grad_memory, scores,
    rs_out, rs_in,
    load, send, ask_recv, tab_recv, par_recv, aux_recv, grad_recv, row_recv, rs_recv,
):
    sections = lax.axis_size("section")
    owners = lax.axis_size("table")
    plane = owners // LAYERS
    rows_dev, features = table_in.shape
    tokens = gate_a.shape[0]
    listed = row_ids.shape[1]
    part = features // sections
    group = sections * plane
    width = group * ROW_LIMIT
    piece = features // PIECES
    last = LAYERS - 1

    sec = lax.axis_index("section")
    me = lax.axis_index("table")
    z = me // plane
    p_me = lax.rem(me, plane)
    seat = sec * plane + p_me
    parity = lax.rem(sec, 2)
    partner = sec + 1 - 2 * parity
    step_z = 1 - 2 * parity
    ahead_ok = (z + step_z >= 0) & (z + step_z <= last)

    def peer(hop):
        other, bit = p_me, 1
        while bit < plane:
            if hop & bit:
                other = other + bit - 2 * bit * lax.rem(p_me // bit, 2)
            bit *= 2
        return other

    x_side, y_side, corner = peer(1), peer(2), peer(3)

    def strip(c):
        if isinstance(c, int):
            return pl.ds(c * piece, piece)
        return pl.ds(pl.multiple_of(c * piece, piece), piece)

    def half(n):
        return pl.ds(n * (features // HALVES), features // HALVES)

    def other_section(hop):
        return lax.rem(sec + hop, sections)

    def need(k):
        return jnp.where(z < LAYERS // 2, last - k, k)

    def at(layer, place):
        return layer * plane + place

    def greet(s, t):
        pl.semaphore_signal(
            pltpu.get_barrier_semaphore(), inc=1,
            device_id={"section": s, "table": t}, device_id_type=MESH,
        )

    def remote(source, target, send, recv, s, t):
        pltpu.make_async_remote_copy(
            src_ref=source, dst_ref=target, send_sem=send, recv_sem=recv,
            device_id={"section": s, "table": t}, device_id_type=MESH,
        ).start()

    for hop in range(plane):
        for turn in range(sections):
            if hop or turn:
                greet(other_section(turn), at(z, peer(hop)))

    @pl.when(z > 0)
    def _():
        greet(sec, at(z - 1, p_me))

    @pl.when(z < last)
    def _():
        greet(sec, at(z + 1, p_me))

    pltpu.make_async_copy(row_ids_in, row_ids, load.at[4]).start()
    pltpu.make_async_copy(table_in, col.at[z], load.at[0]).start()
    pltpu.make_async_copy(slots_in, slots, load.at[5]).start()
    pltpu.make_async_copy(weights_in, weights, load.at[6]).start()
    pltpu.make_async_copy(gate_a_in, gate_a, load.at[1]).start()
    pltpu.make_async_copy(cot_a_in, cot_a, load.at[2]).start()
    pltpu.make_async_copy(gate_b_in, gate_b, load.at[3]).start()

    drain(row_ids, load.at[4])
    ids = row_ids[...]
    rank_a, spot_a, held_a = locate(ids[0:1], owners, plane, rows_dev)
    rank_b, spot_b, held_b = locate(ids[1:2], owners, plane, rows_dev)
    lane = iota((codes.shape[2], listed), 0)
    base = p_me * (2 * ROW_LIMIT) + width
    lanes_a = hot((lane == rank_a + base) | (lane == rank_a + seat * ROW_LIMIT))
    lanes_b = hot(lane == rank_b + (base + ROW_LIMIT))
    asking = contract(held_a, lanes_a, ((1,), (1,))) + contract(held_b, lanes_b, ((1,), (1,)))
    for q in range(plane):
        message[q] = asking[q * LAYERS : (q + 1) * LAYERS]

    signals = group - 1 + jnp.where(z > 0, 1, 0) + jnp.where(z < last, 1, 0)
    pl.semaphore_wait(pltpu.get_barrier_semaphore(), signals)

    for hop in range(plane):
        q = peer(hop)
        for turn in range(sections):
            if hop or turn:
                remote(
                    message.at[q], asked.at[seat], send, ask_recv,
                    other_section(turn), at(z, q),
                )
    pltpu.make_async_copy(message.at[p_me], asked.at[seat], ask_recv).start()

    for j, side in enumerate((x_side, y_side)):
        remote(
            message.at[corner], asked.at[group + 1 - j], send, ask_recv, sec, at(z, side)
        )

    drain(col.at[z], load.at[0])

    @pl.when(ahead_ok)
    def _():
        for n in range(HALVES):
            block = col.at[z, :, half(n)]
            remote(block, block, send, tab_recv.at[0, n], sec, at(z + step_z, p_me))

    for j, side in enumerate((x_side, y_side)):
        cols = strip(2 * j + parity)
        remote(
            col.at[z, :, cols], aux.at[z, :, cols], send, aux_recv.at[0], sec, at(z, side),
        )

    drain(slots, load.at[5])
    drain(weights, load.at[6])
    slots_t[...] = jnp.transpose(slots[...].reshape(2 * tokens, -1).astype(F32))
    weights_t[...] = jnp.transpose(weights[...].reshape(2 * tokens, -1))
    mixing_t = mix_picks(slots_t, weights_t, listed).astype(BF16)
    space = iota((owners * 2 * ROW_LIMIT, listed), 0)
    wide_a = hot(space == spot_a * (2 * ROW_LIMIT) + rank_a)
    wide_b = hot(space == spot_b * (2 * ROW_LIMIT) + (rank_b + ROW_LIMIT))
    tall_a = hot(iota((owners * ROW_LIMIT, listed), 0) == spot_a * ROW_LIMIT + rank_a)
    wide_list[...] = wide_a
    mix_tall[...] = contract(tall_a, mixing_t[:, :tokens], ((1,), (0,))).astype(BF16)

    drain(gate_a, load.at[1])
    drain(cot_a, load.at[2])

    @pl.loop(0, features // CHUNK)
    def _(c):
        per = part // CHUNK
        inner = pl.ds(pl.multiple_of(lax.rem(c, per) * CHUNK, CHUNK), CHUNK)
        cols = pl.ds(pl.multiple_of(c * CHUNK, CHUNK), CHUNK)
        gate = gate_a[:, cols].astype(F32)
        value = (cot_a[:, cols].astype(F32) * gate * jax.nn.sigmoid(gate)).astype(BF16)
        grad_memory[:, cols] = value
        rows = contract(mix_tall[...], value, ((1,), (0,))).astype(BF16)
        grads_out[c // per, :, :, :, inner] = rows.reshape(plane, LAYERS, ROW_LIMIT, CHUNK)

    for k in range(LAYERS):
        layer = need(k)
        for hop in range(plane):
            q = peer(hop)
            for turn in range(sections):
                if hop or turn:
                    other = other_section(turn)
                    remote(
                        grads_out.at[other, q, layer], arrived.at[layer, seat],
                        send, grad_recv.at[layer], other, at(z, q),
                    )
        pltpu.make_async_copy(
            grads_out.at[sec, p_me, layer], arrived.at[layer, seat], grad_recv.at[layer]
        ).start()

    drain(asked, ask_recv)
    served, summing = asked[sec * plane], asked[0]
    for q in range(1, plane):
        served = served + asked[sec * plane + q]
    for q in range(1, group):
        summing = summing + asked[q]
    for layer in range(LAYERS):
        codes[layer] = served[layer : layer + 1]
        codes_sum[layer] = summing[layer : layer + 1]

    for j, side in enumerate((x_side, y_side)):
        served = message[side] + asked[group + j]
        for layer in range(LAYERS):
            codes_aux[j, layer] = served[layer : layer + 1]

    def lookup(code):
        pick = (iota((rows_dev, code.shape[1]), 0).astype(F32) == code - 1.0).astype(F32)
        return jnp.transpose(pick)[width : width + plane * 2 * ROW_LIMIT].astype(BF16)

    def look_aside(layer):
        return [lookup(codes_aux[j, layer]) for j in range(2)]

    def find(pick, held, found, layer, c):
        for k in range(piece // CHUNK):
            cols = pl.ds(c * piece + k * CHUNK, CHUNK)
            rows = contract(pick, held[layer, :, cols], ((1,), (0,))).astype(BF16)
            found[layer, :, :, cols] = rows.reshape(plane, 2 * ROW_LIMIT, CHUNK)

    def give(found, layer, c, q, column):
        remote(
            found.at[layer, q, :, strip(c)], fetched.at[column, layer, :, strip(c)],
            send, row_recv.at[c], sec, at(z, q),
        )

    def keep(found, layer, c, column):
        pltpu.make_async_copy(
            found.at[layer, p_me, :, strip(c)], fetched.at[column, layer, :, strip(c)],
            row_recv.at[c],
        ).start()

    def shared(layer):
        return (layer > 0) & (layer < last)

    def serve(layer, pick, c, near):
        find(pick, col, rows_out, layer, c)
        first = 2 if c < PIECES // 2 else 1
        for hop in (first, *range(4, plane)):
            give(rows_out, layer, c, peer(hop), p_me)

        @pl.when(~shared(layer) if near else z >= 0)
        def _():
            for hop in (3 - first, 3):
                give(rows_out, layer, c, peer(hop), p_me)

        keep(rows_out, layer, c, p_me)

    def serve_aside(layer, picks, c):
        j = 2 * c // PIECES
        column, target = ((x_side, y_side), (y_side, x_side))[j]
        find(picks[j], aux, rows_aux, layer, c)
        give(rows_aux, layer, c, target, column)
        keep(rows_aux, layer, c, column)

    def summed(layer, cols):
        code = codes_sum[layer][:, :width]
        pick = hot(iota((rows_dev, width), 0).astype(F32) == code - 1.0)
        block = arrived[layer, :, :, cols].reshape(width, -1)
        return contract(pick, block, ((1,), (0,)))

    each = PIECES // HALVES

    def table_hop(h):
        behind, ahead = z - step_z * h, z + step_z * h

        @pl.when((behind >= 0) & (behind <= last))
        def _():
            pick = lookup(codes[behind])
            for n in range(HALVES):
                block = col.at[behind, :, half(n)]
                drain(block, tab_recv.at[h - 1, n])

                if h < last:

                    @pl.when(ahead_ok)
                    def _():
                        remote(
                            block, block, send, tab_recv.at[h, n], sec, at(z + step_z, p_me)
                        )

                remote(block, block, send, par_recv.at[h - 1, n], partner, me)
                for c in range(n * each, (n + 1) * each):
                    serve(behind, pick, c, h == 1)

        @pl.when((ahead >= 0) & (ahead <= last))
        def _():
            pick = lookup(codes[ahead])
            for n in range(HALVES):
                drain(col.at[ahead, :, half(n)], par_recv.at[h - 1, n])
                for c in range(n * each, (n + 1) * each):
                    serve(ahead, pick, c, h == 1)

    def own_aside():
        drain(col.at[z, :, half(0)], aux_recv.at[0])
        for j in range(2):
            block = aux.at[z, :, strip(2 * j + parity)]
            remote(block, block, send, aux_recv.at[1], partner, me)

    def near_aside():
        behind, ahead = z - step_z, z + step_z

        @pl.when(shared(behind))
        def _():
            picks = look_aside(behind)
            for n in range(HALVES):
                block = aux.at[behind, :, half(n)]
                drain(block, aux_recv.at[2 + n])
                remote(block, block, send, aux_recv.at[2 + HALVES + n], partner, me)
                for c in range(n * each, (n + 1) * each):
                    serve_aside(behind, picks, c)

        @pl.when(shared(ahead))
        def _():
            picks = look_aside(ahead)
            for n in range(HALVES):
                drain(aux.at[ahead, :, half(n)], aux_recv.at[2 + HALVES + n])
                for c in range(n * each, (n + 1) * each):
                    serve_aside(ahead, picks, c)

    def reduce_step(k):
        for turn in range(2):
            way = jnp.where(z < LAYERS // 2, 1 - turn, turn)
            up = way == 0
            place = jnp.where(up, z, last - z)
            layer = jnp.where(up, last - (k - place), k - place)
            target = jnp.where(up, z + 1, z - 1)

            def pass_on(earlier):
                for c in range(2):
                    cols = pl.ds(c * (part // 2), part // 2)
                    if earlier:
                        drain(rs_in.at[way, k - 1, :, cols], rs_recv.at[way, k - 1, c])
                    total = summed(layer, cols)
                    if earlier:
                        total = total + rs_in[way, k - 1, :, cols].astype(F32)
                    rs_out[way, k, :, cols] = total.astype(BF16)
                    remote(
                        rs_out.at[way, k, :, cols], rs_in.at[way, k, :, cols],
                        send, rs_recv.at[way, k, c], sec, at(target, p_me),
                    )

            @pl.when(place <= k)
            def _():
                drain(arrived.at[layer], grad_recv.at[layer])

            @pl.when(place == 0)
            def _():
                pass_on(False)

            if k:

                @pl.when((place > 0) & (place <= k))
                def _():
                    pass_on(True)

    own_aside()
    pick = lookup(codes[z])
    for c in range(PIECES):
        find(pick, col, rows_out, z, c)
        for hop in (2 if c < PIECES // 2 else 1, *range(4, plane)):
            give(rows_out, z, c, peer(hop), p_me)
        keep(rows_out, z, c, p_me)
    drain(col.at[z, :, half(0)], aux_recv.at[1])
    picks = look_aside(z)
    for c in range(PIECES):
        serve_aside(z, picks, c)
    reduce_step(0)
    table_hop(1)

    @pl.when(ahead_ok & shared(z))
    def _():
        for n in range(HALVES):
            block = aux.at[z, :, half(n)]
            remote(block, block, send, aux_recv.at[2 + n], sec, at(z + step_z, p_me))

    mix_wide[:tokens] = contract(mixing_t[:, :tokens], wide_a, ((0,), (1,))).astype(BF16)
    mix_wide[tokens:] = contract(mixing_t[:, tokens:], wide_b, ((0,), (1,))).astype(BF16)
    scores[...] = jnp.zeros_like(scores)

    for h in range(2, LAYERS):
        table_hop(h)
        reduce_step(h - 1)
        if h == 2:
            near_aside()

    drain(arrived.at[z], grad_recv.at[z])

    @pl.loop(0, part // CHUNK)
    def _(c):
        cols = pl.ds(pl.multiple_of(c * CHUNK, CHUNK), CHUNK)
        grad_table[:, cols] = summed(z, cols)

    drain(gate_b, load.at[3])
    for c in range(PIECES):
        drain(fetched.at[:, :, :, pl.ds(c * piece, piece)], row_recv.at[c])
        for k in range(piece // CHUNK):
            cols = pl.ds(c * piece + k * CHUNK, CHUNK)
            rows = fetched[:, :, :, cols].reshape(owners * 2 * ROW_LIMIT, CHUNK)
            memory = contract(mix_wide[...], rows, ((1,), (0,)))
            gate = gate_a[:, cols].astype(F32)
            sig = jax.nn.sigmoid(gate)
            incoming = cot_a[:, cols].astype(F32)
            grad_gate[:, cols] = (
                incoming * memory[:tokens] * sig * (1.0 + gate * (1.0 - sig))
            ).astype(BF16)
            scores[...] += contract(grad_memory[:, cols], rows, ((1,), (1,)))
            gate = gate_b[:, cols].astype(F32)
            mixed_b[:, cols] = (gate * jax.nn.sigmoid(gate) * memory[tokens:]).astype(BF16)

    found = contract(
        scores[...], wide_list[...].astype(F32), ((1,), (0,)), precision=lax.Precision.HIGHEST
    )
    grad_weights[...] = jnp.take_along_axis(found, slots[0], axis=1)

    for way in range(2):

        @pl.when((z > 0) if way == 0 else (z < last))
        def _():
            for c in range(2):
                cols = pl.ds(c * (part // 2), part // 2)
                drain(rs_in.at[way, last - 1, :, cols], rs_recv.at[way, last - 1, c])
                grad_table[:, cols] += rs_in[way, last - 1, :, cols].astype(F32)

    drain(asked.at[pl.ds(0, group + 1)], send)
    drain(arrived.at[:, pl.ds(0, group - 1)], send)
    drain(rows_out.at[0, pl.ds(0, plane - 2)], send)
    for c in range(2):
        drain(col.at[z, :, strip(c)], send)
        drain(col.at[z, :, strip(c)], send)

    @pl.when(ahead_ok)
    def _():
        drain(col.at[z], send)

    @pl.when(ahead_ok & shared(z))
    def _():
        drain(col.at[z], send)

    for h in range(1, LAYERS):
        behind, ahead = z - step_z * h, z + step_z * h

        @pl.when((behind >= 0) & (behind <= last))
        def _():
            drain(col.at[behind], send)

            @pl.when(ahead_ok)
            def _():
                drain(col.at[behind], send)

        for layer in (behind, ahead):

            @pl.when((layer >= 0) & (layer <= last))
            def _():
                drain(rows_out.at[0, pl.ds(0, plane - 2)], send)

                @pl.when(~shared(layer) if h == 1 else z >= 0)
                def _():
                    drain(rows_out.at[0, pl.ds(0, 1)], send)

    @pl.when(shared(z - step_z))
    def _():
        drain(col.at[z], send)

    for k in range(last):
        for way in range(2):

            @pl.when(k >= (z if way == 0 else last - z))
            def _():
                drain(rs_out.at[way, k], send)


def store(mixed_b, grad_gate, grad_weights, grad_table, *refs):
    outs, sems = refs[:4], refs[4]
    copies = [
        pltpu.make_async_copy(source, target, sems.at[n])
        for n, (source, target) in enumerate(zip((mixed_b, grad_gate, grad_weights, grad_table), outs))
    ]
    for copy in copies:
        copy.start()
    for copy in copies:
        copy.wait()


def local(gate_a, cotangent_a, gate_b, table, row_ids, slots, weights):
    owners = lax.axis_size("table")
    sections = lax.axis_size("section")
    plane = owners // LAYERS
    group = sections * plane
    rows_dev, features = table.shape
    tokens = gate_a.shape[1]
    listed = row_ids.shape[-1]
    picks = slots.shape[-1]
    part = features // sections
    lanes = -(-(2 * plane + group) * ROW_LIMIT // 128) * 128
    slot_rows = owners * 2 * ROW_LIMIT
    vmem = pl.BlockSpec(memory_space=pltpu.VMEM)
    hbm = pl.BlockSpec(memory_space=pl.ANY)
    dma = pltpu.SemaphoreType.DMA
    mixed_b, grad_gate, grad_weights, grad_table = pl.pallas_call(
        exchange,
        out_shape=(
            pltpu.VMEM((tokens, features), BF16),
            pltpu.VMEM((tokens, features), BF16),
            pltpu.VMEM((tokens, picks), F32),
            pltpu.VMEM((rows_dev, part), F32),
        ),
        in_specs=[hbm] * 7,
        out_specs=(vmem,) * 4,
        scratch_shapes=[
            pltpu.VMEM((tokens, features), BF16),
            pltpu.VMEM((tokens, features), BF16),
            pltpu.VMEM((tokens, features), BF16),
            pltpu.VMEM((2, listed), jnp.int32),
            pltpu.VMEM((2, tokens, picks), jnp.int32),
            pltpu.VMEM((2, tokens, picks), F32),
            pltpu.VMEM((LAYERS, rows_dev, features), BF16),
            pltpu.VMEM((LAYERS, rows_dev, features), BF16),
            pltpu.VMEM((picks, 2 * tokens), F32),
            pltpu.VMEM((picks, 2 * tokens), F32),
            pltpu.VMEM((2 * tokens, slot_rows), BF16),
            pltpu.VMEM((owners * ROW_LIMIT, tokens), BF16),
            pltpu.VMEM((slot_rows, listed), BF16),
            pltpu.VMEM((plane, LAYERS, lanes), F32),
            pltpu.VMEM((group + 2, LAYERS, lanes), F32),
            pltpu.VMEM((LAYERS, 1, lanes), F32),
            pltpu.VMEM((LAYERS, 1, lanes), F32),
            pltpu.VMEM((2, LAYERS, 1, lanes), F32),
            pltpu.VMEM((sections, plane, LAYERS, ROW_LIMIT, part), BF16),
            pltpu.VMEM((LAYERS, group, ROW_LIMIT, part), BF16),
            pltpu.VMEM((LAYERS, plane, 2 * ROW_LIMIT, features), BF16),
            pltpu.VMEM((LAYERS, plane, 2 * ROW_LIMIT, features), BF16),
            pltpu.VMEM((plane, LAYERS, 2 * ROW_LIMIT, features), BF16),
            pltpu.VMEM((tokens, features), BF16),
            pltpu.VMEM((tokens, slot_rows), F32),
            pltpu.VMEM((2, LAYERS - 1, rows_dev, part), BF16),
            pltpu.VMEM((2, LAYERS - 1, rows_dev, part), BF16),
            dma((7,)),
            dma,
            dma,
            dma((LAYERS - 1, HALVES)),
            dma((LAYERS - 1, HALVES)),
            dma((2 + 2 * HALVES,)),
            dma((LAYERS,)),
            dma((PIECES,)),
            dma((2, LAYERS - 1, HALVES)),
        ],
        compiler_params=pltpu.CompilerParams(
            collective_id=0, has_side_effects=True, vmem_limit_bytes=60 * 1024 * 1024
        ),
    )(
        gate_a[0], cotangent_a[0], gate_b[0], table, row_ids[0, :, 0], slots[0], weights[0]
    )
    results = (mixed_b, grad_gate, grad_weights, grad_table)
    mixed_b, grad_gate, grad_weights, grad_table = pl.pallas_call(
        store,
        out_shape=tuple(jax.ShapeDtypeStruct(r.shape, r.dtype) for r in results),
        in_specs=[vmem] * 4,
        out_specs=(hbm,) * 4,
        scratch_shapes=[dma((4,))],
    )(*(pltpu.with_memory_space_constraint(r, pltpu.VMEM) for r in results))
    return mixed_b[None], grad_gate[None], grad_weights[None], grad_table


def solution(mesh):
    return jax.shard_map(
        local,
        mesh=mesh,
        in_specs=(
            P("section", "table", None),
            P("section", "table", None),
            P("section", "table", None),
            P("table", None),
            P("section", None, "table", None),
            P("section", None, "table", None),
            P("section", None, "table", None),
        ),
        out_specs=(
            P("section", "table", None),
            P("section", "table", None),
            P("section", "table", None),
            P("table", "section"),
        ),
        check_vma=False,
    )
```

```python
import jax
import jax.numpy as jnp
from jax import lax
from jax.experimental import pallas as pl
from jax.experimental.pallas import tpu as pltpu
from jax.sharding import PartitionSpec as P

ROW_LIMIT = 8
CHUNK = 512
LAYERS = 4
PIECES = 4
PARTIAL = (1, 3)
ORDER = (0, 2, 1, 3)
HALVES = 2
FAR_SHARE = 2
UNROLL = 8
MESH = pl.DeviceIdType.MESH
BF16, F32 = jnp.bfloat16, jnp.float32


def iota(shape, axis):
    return lax.broadcasted_iota(jnp.int32, shape, axis)


def hot(mask):
    return mask.astype(F32).astype(BF16)


def contract(lhs, rhs, dims, **options):
    return lax.dot_general(lhs, rhs, (dims, ((), ())), preferred_element_type=F32, **options)


def locate(ids, owners, plane, rows_dev):
    listed = ids.shape[1]
    line = iota((owners, listed), 0)
    layer = line & (LAYERS - 1)
    column = lax.shift_right_logical(line, LAYERS.bit_length() - 1)
    first = (layer * plane + column) * rows_dev
    member = ((ids >= first) & (ids < first + rows_dev)).astype(F32)
    before = iota((listed, listed), 0) < iota((listed, listed), 1)
    earlier = contract(member.astype(BF16), hot(before), ((1,), (0,)))
    rank = jnp.sum(member * earlier, axis=0, keepdims=True).astype(jnp.int32)
    spot = jnp.sum(member * line.astype(F32), axis=0, keepdims=True).astype(jnp.int32)
    start = jnp.sum(member * first.astype(F32), axis=0, keepdims=True).astype(jnp.int32)
    held = (member * (ids - start + 1).astype(F32)).astype(BF16)
    return rank, spot, held


def mix_picks(slots_t, weights_t, listed):
    picks, tokens = slots_t.shape
    position = iota((listed, tokens), 0).astype(F32)

    def group(g, total):
        base = pl.multiple_of(g * UNROLL, UNROLL)
        slot = slots_t[pl.ds(base, UNROLL), :]
        weight = weights_t[pl.ds(base, UNROLL), :]
        for p in range(UNROLL):
            hit = slot[p : p + 1] == position
            total = total + jnp.where(hit, weight[p : p + 1], 0.0)
        return total

    start = jnp.zeros((listed, tokens), F32)
    return lax.fori_loop(0, picks // UNROLL, group, start)


def drain(block, sem):
    pltpu.make_async_copy(block, block, sem).wait()


def exchange(
    gate_a_in, cot_a_in, gate_b_in, table_in, row_ids_in, slots_in, weights_in,
    mixed_b, grad_gate, grad_table, scores, wide_list, slots,
    gate_a, cot_a, gate_b, row_ids, weights, col, aux, slots_t, weights_t, mix_wide, mix_tall,
    message, asked, codes, codes_sum, codes_aux, grads_out, arrived, rows_out, rows_aux, fetched,
    grad_memory,
    rs_out, rs_in,
    load, send, ask_recv, tab_recv, par_recv, aux_recv, grad_recv, row_recv, rs_recv,
):
    sections = lax.axis_size("section")
    owners = lax.axis_size("table")
    plane = owners // LAYERS
    rows_dev, features = table_in.shape
    tokens = gate_a.shape[0]
    listed = row_ids.shape[1]
    part = features // sections
    group = sections * plane
    width = group * ROW_LIMIT
    piece = features // PIECES
    far = piece // FAR_SHARE
    last = LAYERS - 1

    sec = lax.axis_index("section")
    me = lax.axis_index("table")
    z = me // plane
    p_me = lax.rem(me, plane)
    seat = sec * plane + p_me
    parity = lax.rem(sec, 2)
    partner = sec + 1 - 2 * parity
    step_z = 1 - 2 * parity
    ahead_ok = (z + step_z >= 0) & (z + step_z <= last)

    def peer(hop):
        other, bit = p_me, 1
        while bit < plane:
            if hop & bit:
                other = other + bit - 2 * bit * lax.rem(p_me // bit, 2)
            bit *= 2
        return other

    x_side, y_side, corner = peer(1), peer(2), peer(3)

    def strip(c):
        if isinstance(c, int):
            return pl.ds(c * piece, piece)
        return pl.ds(pl.multiple_of(c * piece, piece), piece)

    def half(n):
        return pl.ds(n * (features // HALVES), features // HALVES)

    def other_section(hop):
        return lax.rem(sec + hop, sections)

    def need(k):
        return jnp.where(z < LAYERS // 2, last - k, k)

    def at(layer, place):
        return layer * plane + place

    def greet(s, t):
        pl.semaphore_signal(
            pltpu.get_barrier_semaphore(), inc=1,
            device_id={"section": s, "table": t}, device_id_type=MESH,
        )

    def remote(source, target, send, recv, s, t):
        pltpu.make_async_remote_copy(
            src_ref=source, dst_ref=target, send_sem=send, recv_sem=recv,
            device_id={"section": s, "table": t}, device_id_type=MESH,
        ).start()

    for hop in range(plane):
        for turn in range(sections):
            if hop or turn:
                greet(other_section(turn), at(z, peer(hop)))

    @pl.when(z > 0)
    def _():
        greet(sec, at(z - 1, p_me))

    @pl.when(z < last)
    def _():
        greet(sec, at(z + 1, p_me))

    pltpu.make_async_copy(row_ids_in, row_ids, load.at[4]).start()
    pltpu.make_async_copy(table_in, col.at[z], load.at[0]).start()
    pltpu.make_async_copy(slots_in, slots, load.at[5]).start()
    pltpu.make_async_copy(weights_in, weights, load.at[6]).start()
    pltpu.make_async_copy(gate_a_in, gate_a, load.at[1]).start()
    pltpu.make_async_copy(cot_a_in, cot_a, load.at[2]).start()
    pltpu.make_async_copy(gate_b_in, gate_b, load.at[3]).start()

    drain(row_ids, load.at[4])
    ids = row_ids[...]
    rank_a, spot_a, held_a = locate(ids[0:1], owners, plane, rows_dev)
    rank_b, spot_b, held_b = locate(ids[1:2], owners, plane, rows_dev)
    lane = iota((codes.shape[2], listed), 0)
    base = p_me * (2 * ROW_LIMIT) + width
    lanes_a = hot((lane == rank_a + base) | (lane == rank_a + seat * ROW_LIMIT))
    lanes_b = hot(lane == rank_b + (base + ROW_LIMIT))
    asking = contract(held_a, lanes_a, ((1,), (1,))) + contract(held_b, lanes_b, ((1,), (1,)))
    for q in range(plane):
        message[q] = asking[q * LAYERS : (q + 1) * LAYERS]

    signals = group - 1 + jnp.where(z > 0, 1, 0) + jnp.where(z < last, 1, 0)
    pl.semaphore_wait(pltpu.get_barrier_semaphore(), signals)

    for hop in range(plane):
        q = peer(hop)
        for turn in range(sections):
            if hop or turn:
                remote(
                    message.at[q], asked.at[seat], send, ask_recv,
                    other_section(turn), at(z, q),
                )
    pltpu.make_async_copy(message.at[p_me], asked.at[seat], ask_recv).start()

    for j, side in enumerate((x_side, y_side)):
        remote(
            message.at[corner], asked.at[group + 1 - j], send, ask_recv, sec, at(z, side)
        )

    drain(col.at[z], load.at[0])

    @pl.when(ahead_ok)
    def _():
        for n in range(HALVES):
            block = col.at[z, :, half(n)]
            remote(block, block, send, tab_recv.at[0, n], sec, at(z + step_z, p_me))

    for j, side in enumerate((x_side, y_side)):
        cols = strip(2 * j + parity)
        remote(
            col.at[z, :, cols], aux.at[z, :, cols], send, aux_recv.at[0], sec, at(z, side),
        )

    drain(slots, load.at[5])
    drain(weights, load.at[6])
    slots_t[...] = jnp.transpose(slots[...].reshape(2 * tokens, -1).astype(F32))
    weights_t[...] = jnp.transpose(weights[...].reshape(2 * tokens, -1))
    mixing_t = mix_picks(slots_t, weights_t, listed).astype(BF16)
    space = iota((owners * 2 * ROW_LIMIT, listed), 0)
    wide_a = hot(space == spot_a * (2 * ROW_LIMIT) + rank_a)
    wide_b = hot(space == spot_b * (2 * ROW_LIMIT) + (rank_b + ROW_LIMIT))
    tall_a = hot(iota((owners * ROW_LIMIT, listed), 0) == spot_a * ROW_LIMIT + rank_a)
    wide_list[...] = wide_a
    mix_tall[...] = contract(tall_a, mixing_t[:, :tokens], ((1,), (0,))).astype(BF16)

    drain(gate_a, load.at[1])
    drain(cot_a, load.at[2])

    @pl.loop(0, features // CHUNK)
    def _(c):
        per = part // CHUNK
        inner = pl.ds(pl.multiple_of(lax.rem(c, per) * CHUNK, CHUNK), CHUNK)
        cols = pl.ds(pl.multiple_of(c * CHUNK, CHUNK), CHUNK)
        gate = gate_a[:, cols].astype(F32)
        value = (cot_a[:, cols].astype(F32) * gate * jax.nn.sigmoid(gate)).astype(BF16)
        grad_memory[:, cols] = value
        rows = contract(mix_tall[...], value, ((1,), (0,))).astype(BF16)
        grads_out[c // per, :, :, :, inner] = rows.reshape(plane, LAYERS, ROW_LIMIT, CHUNK)

    for k in range(LAYERS):
        layer = need(k)
        for hop in range(plane):
            q = peer(hop)
            for turn in range(sections):
                if hop or turn:
                    other = other_section(turn)
                    remote(
                        grads_out.at[other, q, layer], arrived.at[layer, seat],
                        send, grad_recv.at[layer], other, at(z, q),
                    )
        pltpu.make_async_copy(
            grads_out.at[sec, p_me, layer], arrived.at[layer, seat], grad_recv.at[layer]
        ).start()

    drain(asked, ask_recv)
    served, summing = asked[sec * plane], asked[0]
    for q in range(1, plane):
        served = served + asked[sec * plane + q]
    for q in range(1, group):
        summing = summing + asked[q]
    for layer in range(LAYERS):
        codes[layer] = served[layer : layer + 1]
        codes_sum[layer] = summing[layer : layer + 1]

    for j, side in enumerate((x_side, y_side)):
        served = message[side] + asked[group + j]
        for layer in range(LAYERS):
            codes_aux[j, layer] = served[layer : layer + 1]

    def lookup(code):
        pick = (iota((rows_dev, code.shape[1]), 0).astype(F32) == code - 1.0).astype(F32)
        return jnp.transpose(pick)[width : width + plane * 2 * ROW_LIMIT].astype(BF16)

    def look_aside(layer):
        return [lookup(codes_aux[j, layer]) for j in range(2)]

    def span(block):
        return pl.ds(*block[1:])

    def whole(c):
        return c, c * piece, piece

    def tail(c):
        return c, (c + 1) * piece - far, far

    def find(pick, held, found, layer, block):
        _, first, size = block
        for k in range(0, size, CHUNK):
            cols = pl.ds(first + k, min(CHUNK, size - k))
            rows = contract(pick, held[layer, :, cols], ((1,), (0,))).astype(BF16)
            found[layer, :, :, cols] = rows.reshape(plane, 2 * ROW_LIMIT, -1)

    def give(found, layer, block, q, column):
        cols = span(block)
        remote(
            found.at[layer, q, :, cols], fetched.at[column, layer, :, cols],
            send, row_recv.at[block[0]], sec, at(z, q),
        )

    def keep(found, layer, block, column):
        cols = span(block)
        pltpu.make_async_copy(
            found.at[layer, p_me, :, cols], fetched.at[column, layer, :, cols],
            row_recv.at[block[0]],
        ).start()

    def valid(layer):
        return (layer >= 0) & (layer <= last)

    def inner(layer):
        return (layer > 0) & (layer < last)

    def blocks(h, c):
        if h == 0 or (h == 1 and c in PARTIAL):
            return [(whole(c), True)]
        if h == 2 and c in PARTIAL:
            return [((c, c * piece, piece - far), False), (tail(c), None)]
        return [(whole(c), None if h == 1 else False)]

    def serve(layer, pick, c, h):
        first = 2 if c < PIECES // 2 else 1
        for block, shared in blocks(h, c):
            find(pick, col, rows_out, layer, block)
            for hop in (first, *range(4, plane)):
                give(rows_out, layer, block, peer(hop), p_me)
            if shared is not True:

                @pl.when(~inner(layer) if shared is None else z >= 0)
                def _():
                    for hop in (3 - first, 3):
                        give(rows_out, layer, block, peer(hop), p_me)

            keep(rows_out, layer, block, p_me)

    def serve_aside(layer, picks, block):
        j = 2 * block[0] // PIECES
        column, target = ((x_side, y_side), (y_side, x_side))[j]
        find(picks[j], aux, rows_aux, layer, block)
        give(rows_aux, layer, block, target, column)
        keep(rows_aux, layer, block, column)

    def summed(layer, cols):
        code = codes_sum[layer][:, :width]
        pick = hot(iota((rows_dev, width), 0).astype(F32) == code - 1.0)
        block = arrived[layer, :, :, cols].reshape(width, -1)
        return contract(pick, block, ((1,), (0,)))

    each = PIECES // HALVES

    def pass_table(h, n):
        behind = z - step_z * h

        @pl.when(valid(behind))
        def _():
            block = col.at[behind, :, half(n)]
            drain(block, tab_recv.at[h - 1, n])
            if h < last:

                @pl.when(ahead_ok)
                def _():
                    remote(block, block, send, tab_recv.at[h, n], sec, at(z + step_z, p_me))

            remote(block, block, send, par_recv.at[h - 1, n], partner, me)

    def serve_layer(h, passing):
        behind, ahead = z - step_z * h, z + step_z * h

        @pl.when(valid(behind))
        def _():
            pick = lookup(codes[behind])
            for n in range(HALVES):
                if passing:
                    pass_table(h, n)
                for c in range(n * each, (n + 1) * each):
                    serve(behind, pick, c, h)

        @pl.when(valid(ahead))
        def _():
            pick = lookup(codes[ahead])
            for n in range(HALVES):
                drain(col.at[ahead, :, half(n)], par_recv.at[h - 1, n])
                for c in range(n * each, (n + 1) * each):
                    serve(ahead, pick, c, h)

    def own_aside():
        drain(col.at[z, :, half(0)], aux_recv.at[0])
        for j in range(2):
            block = aux.at[z, :, strip(2 * j + parity)]
            remote(block, block, send, aux_recv.at[1], partner, me)

    def landing(h, way, c):
        if h == 1:
            return 2 + way * PIECES + c
        return 2 + 2 * PIECES + way * len(PARTIAL) + PARTIAL.index(c)

    def near_aside(h):
        behind, ahead = z - step_z * h, z + step_z * h

        def each_block(layer, use):
            for c in sorted(range(PIECES), key=lambda c: c not in PARTIAL):
                for block, shared in blocks(h, c):
                    if shared is True:
                        use(block)
                    elif shared is None:

                        @pl.when(inner(layer))
                        def _():
                            use(block)

        @pl.when(valid(behind))
        def _():
            picks = look_aside(behind)

            def use(block):
                c = block[0]
                part = aux.at[behind, :, span(block)]
                drain(part, aux_recv.at[landing(h, 0, c)])
                if h == 1 and c in PARTIAL:

                    @pl.when(inner(behind) & ahead_ok)
                    def _():
                        onward = aux.at[behind, :, span(tail(c))]
                        remote(
                            onward, onward, send, aux_recv.at[landing(2, 0, c)],
                            sec, at(z + step_z, p_me),
                        )

                remote(part, part, send, aux_recv.at[landing(h, 1, c)], partner, me)
                serve_aside(behind, picks, block)

            each_block(behind, use)

        @pl.when(valid(ahead))
        def _():
            picks = look_aside(ahead)

            def use(block):
                drain(aux.at[ahead, :, span(block)], aux_recv.at[landing(h, 1, block[0])])
                serve_aside(ahead, picks, block)

            each_block(ahead, use)

    def reduce_step(k, starts, follows):
        for turn in range(2):
            way = jnp.where(z < LAYERS // 2, 1 - turn, turn)
            up = way == 0
            place = jnp.where(up, z, last - z)
            layer = jnp.where(up, last - (k - place), k - place)
            target = jnp.where(up, z + 1, z - 1)

            def pass_on(earlier):
                for c in range(2):
                    cols = pl.ds(c * (part // 2), part // 2)
                    if earlier:
                        drain(rs_in.at[way, k - 1, :, cols], rs_recv.at[way, k - 1, c])
                    total = summed(layer, cols)
                    if earlier:
                        total = total + rs_in[way, k - 1, :, cols].astype(F32)
                    rs_out[way, k, :, cols] = total.astype(BF16)
                    remote(
                        rs_out.at[way, k, :, cols], rs_in.at[way, k, :, cols],
                        send, rs_recv.at[way, k, c], sec, at(target, p_me),
                    )

            if starts:

                @pl.when(place == 0)
                def _():
                    drain(arrived.at[layer], grad_recv.at[layer])
                    pass_on(False)

            if follows:

                @pl.when((place > 0) & (place <= k))
                def _():
                    drain(arrived.at[layer], grad_recv.at[layer])
                    pass_on(True)

    own_aside()
    pick = lookup(codes[z])
    for c in range(PIECES):
        serve(z, pick, c, 0)
    pass_table(1, 0)
    drain(col.at[z, :, half(0)], aux_recv.at[1])
    picks = look_aside(z)
    for c in range(PIECES):
        serve_aside(z, picks, whole(c))
    for n in range(1, HALVES):
        pass_table(1, n)

    def pass_aside(c):
        block = aux.at[z, :, strip(c)]
        remote(block, block, send, aux_recv.at[landing(1, 0, c)], sec, at(z + step_z, p_me))

    @pl.when(ahead_ok)
    def _():
        for c in PARTIAL:
            pass_aside(c)

    @pl.when(ahead_ok & inner(z))
    def _():
        for c in range(PIECES):
            if c not in PARTIAL:
                pass_aside(c)

    reduce_step(0, True, False)
    serve_layer(1, False)

    mix_wide[:tokens] = contract(mixing_t[:, :tokens], wide_a, ((0,), (1,))).astype(BF16)
    mix_wide[tokens:] = contract(mixing_t[:, tokens:], wide_b, ((0,), (1,))).astype(BF16)
    scores[...] = jnp.zeros_like(scores)

    serve_layer(2, True)
    reduce_step(1, True, True)
    for k in range(2, last):
        reduce_step(k, True, False)
    near_aside(1)
    for h in range(3, LAYERS):
        serve_layer(h, True)
    near_aside(2)
    for k in range(2, last):
        reduce_step(k, False, True)

    drain(arrived.at[z], grad_recv.at[z])

    @pl.loop(0, part // CHUNK)
    def _(c):
        cols = pl.ds(pl.multiple_of(c * CHUNK, CHUNK), CHUNK)
        grad_table[:, cols] = summed(z, cols)

    drain(gate_b, load.at[3])
    for c in ORDER:
        drain(fetched.at[:, :, :, strip(c)], row_recv.at[c])
        for k in range(piece // CHUNK):
            cols = pl.ds(c * piece + k * CHUNK, CHUNK)
            rows = fetched[:, :, :, cols].reshape(owners * 2 * ROW_LIMIT, CHUNK)
            memory = contract(mix_wide[...], rows, ((1,), (0,)))
            gate = gate_a[:, cols].astype(F32)
            sig = jax.nn.sigmoid(gate)
            incoming = cot_a[:, cols].astype(F32)
            grad_gate[:, cols] = (
                incoming * memory[:tokens] * sig * (1.0 + gate * (1.0 - sig))
            ).astype(BF16)
            scores[...] += contract(grad_memory[:, cols], rows, ((1,), (1,)))
            gate = gate_b[:, cols].astype(F32)
            mixed_b[:, cols] = (gate * jax.nn.sigmoid(gate) * memory[tokens:]).astype(BF16)

    for way in range(2):

        @pl.when((z > 0) if way == 0 else (z < last))
        def _():
            for c in range(2):
                cols = pl.ds(c * (part // 2), part // 2)
                drain(rs_in.at[way, last - 1, :, cols], rs_recv.at[way, last - 1, c])
                grad_table[:, cols] += rs_in[way, last - 1, :, cols].astype(F32)

    drain(asked.at[pl.ds(0, group + 1)], send)
    drain(arrived.at[:, pl.ds(0, group - 1)], send)
    drain(rows_out.at[0, pl.ds(0, plane - 2)], send)
    for c in range(2):
        drain(col.at[z, :, strip(c)], send)
        drain(col.at[z, :, strip(c)], send)

    @pl.when(ahead_ok)
    def _():
        drain(col.at[z], send)
        drain(col.at[z, :, half(0)], send)

    @pl.when(ahead_ok & inner(z))
    def _():
        drain(col.at[z, :, half(0)], send)

    for h in range(1, LAYERS):
        behind, ahead = z - step_z * h, z + step_z * h

        @pl.when(valid(behind))
        def _():
            drain(col.at[behind], send)

            @pl.when(ahead_ok)
            def _():
                drain(col.at[behind], send)

            for c in range(PIECES):
                for block, shared in blocks(h, c):
                    if shared is True:
                        drain(aux.at[z, :, span(block)], send)
                    elif shared is None:

                        @pl.when(inner(behind))
                        def _():
                            drain(aux.at[z, :, span(block)], send)

                if h == 1 and c in PARTIAL:

                    @pl.when(inner(behind) & ahead_ok)
                    def _():
                        drain(aux.at[z, :, span(tail(c))], send)

        for layer in (behind, ahead):

            @pl.when(valid(layer))
            def _():
                drain(rows_out.at[0, pl.ds(0, plane - 2)], send)
                for c in range(PIECES):
                    for block, shared in blocks(h, c):
                        if shared is not True:

                            @pl.when(~inner(layer) if shared is None else z >= 0)
                            def _():
                                drain(rows_out.at[0, 0, :, span(block)], send)

    for k in range(last):
        for way in range(2):

            @pl.when(k >= (z if way == 0 else last - z))
            def _():
                drain(rs_out.at[way, k], send)


def store(mixed_b, grad_gate, grad_table, scores, wide_list, slots, *refs):
    outs, grad_weights, sems = refs[:4], refs[4], refs[5]
    copies = [
        pltpu.make_async_copy(source, target, sems.at[n])
        for n, (source, target) in enumerate(
            zip((mixed_b, grad_gate, grad_table, grad_weights), outs)
        )
    ]
    for copy in copies[:3]:
        copy.start()
    found = contract(
        scores[...], wide_list[...].astype(F32), ((1,), (0,)), precision=lax.Precision.HIGHEST
    )
    grad_weights[...] = jnp.take_along_axis(found, slots[0], axis=1)
    copies[3].start()
    for copy in copies:
        copy.wait()


def local(gate_a, cotangent_a, gate_b, table, row_ids, slots, weights):
    owners = lax.axis_size("table")
    sections = lax.axis_size("section")
    plane = owners // LAYERS
    group = sections * plane
    rows_dev, features = table.shape
    tokens = gate_a.shape[1]
    listed = row_ids.shape[-1]
    picks = slots.shape[-1]
    part = features // sections
    lanes = -(-(2 * plane + group) * ROW_LIMIT // 128) * 128
    slot_rows = owners * 2 * ROW_LIMIT
    vmem = pl.BlockSpec(memory_space=pltpu.VMEM)
    hbm = pl.BlockSpec(memory_space=pl.ANY)
    dma = pltpu.SemaphoreType.DMA
    results = pl.pallas_call(
        exchange,
        out_shape=(
            pltpu.VMEM((tokens, features), BF16),
            pltpu.VMEM((tokens, features), BF16),
            pltpu.VMEM((rows_dev, part), F32),
            pltpu.VMEM((tokens, slot_rows), F32),
            pltpu.VMEM((slot_rows, listed), BF16),
            pltpu.VMEM((2, tokens, picks), jnp.int32),
        ),
        in_specs=[hbm] * 7,
        out_specs=(vmem,) * 6,
        scratch_shapes=[
            pltpu.VMEM((tokens, features), BF16),
            pltpu.VMEM((tokens, features), BF16),
            pltpu.VMEM((tokens, features), BF16),
            pltpu.VMEM((2, listed), jnp.int32),
            pltpu.VMEM((2, tokens, picks), F32),
            pltpu.VMEM((LAYERS, rows_dev, features), BF16),
            pltpu.VMEM((LAYERS, rows_dev, features), BF16),
            pltpu.VMEM((picks, 2 * tokens), F32),
            pltpu.VMEM((picks, 2 * tokens), F32),
            pltpu.VMEM((2 * tokens, slot_rows), BF16),
            pltpu.VMEM((owners * ROW_LIMIT, tokens), BF16),
            pltpu.VMEM((plane, LAYERS, lanes), F32),
            pltpu.VMEM((group + 2, LAYERS, lanes), F32),
            pltpu.VMEM((LAYERS, 1, lanes), F32),
            pltpu.VMEM((LAYERS, 1, lanes), F32),
            pltpu.VMEM((2, LAYERS, 1, lanes), F32),
            pltpu.VMEM((sections, plane, LAYERS, ROW_LIMIT, part), BF16),
            pltpu.VMEM((LAYERS, group, ROW_LIMIT, part), BF16),
            pltpu.VMEM((LAYERS, plane, 2 * ROW_LIMIT, features), BF16),
            pltpu.VMEM((LAYERS, plane, 2 * ROW_LIMIT, features), BF16),
            pltpu.VMEM((plane, LAYERS, 2 * ROW_LIMIT, features), BF16),
            pltpu.VMEM((tokens, features), BF16),
            pltpu.VMEM((2, LAYERS - 1, rows_dev, part), BF16),
            pltpu.VMEM((2, LAYERS - 1, rows_dev, part), BF16),
            dma((7,)),
            dma,
            dma,
            dma((LAYERS - 1, HALVES)),
            dma((LAYERS - 1, HALVES)),
            dma((2 + 2 * PIECES + 2 * len(PARTIAL),)),
            dma((LAYERS,)),
            dma((PIECES,)),
            dma((2, LAYERS - 1, HALVES)),
        ],
        compiler_params=pltpu.CompilerParams(
            collective_id=0, has_side_effects=True, vmem_limit_bytes=60 * 1024 * 1024
        ),
    )(
        gate_a[0], cotangent_a[0], gate_b[0], table, row_ids[0, :, 0], slots[0], weights[0]
    )
    mixed_b, grad_gate, grad_table, grad_weights = pl.pallas_call(
        store,
        out_shape=(
            jax.ShapeDtypeStruct((tokens, features), BF16),
            jax.ShapeDtypeStruct((tokens, features), BF16),
            jax.ShapeDtypeStruct((rows_dev, part), F32),
            jax.ShapeDtypeStruct((tokens, picks), F32),
        ),
        in_specs=[vmem] * 6,
        out_specs=(hbm,) * 4,
        scratch_shapes=[pltpu.VMEM((tokens, picks), F32), dma((4,))],
    )(*(pltpu.with_memory_space_constraint(r, pltpu.VMEM) for r in results))
    return mixed_b[None], grad_gate[None], grad_weights[None], grad_table


def solution(mesh):
    return jax.shard_map(
        local,
        mesh=mesh,
        in_specs=(
            P("section", "table", None),
            P("section", "table", None),
            P("section", "table", None),
            P("table", None),
            P("section", None, "table", None),
            P("section", None, "table", None),
            P("section", None, "table", None),
        ),
        out_specs=(
            P("section", "table", None),
            P("section", "table", None),
            P("section", "table", None),
            P("table", "section"),
        ),
        check_vma=False,
    )
```

```python
import jax
import jax.numpy as jnp
from jax import lax
from jax.experimental import pallas as pl
from jax.experimental.pallas import tpu as pltpu
from jax.sharding import PartitionSpec as P

ROW_LIMIT = 8
CHUNK = 512
LAYERS = 4
PIECES = 4
PARTIAL = (1, 3)
ORDER = (0, 2, 1, 3)
HALVES = 2
FAR_EIGHTHS = 5
UNROLL = 8
MESH = pl.DeviceIdType.MESH
BF16, F32 = jnp.bfloat16, jnp.float32


def iota(shape, axis):
    return lax.broadcasted_iota(jnp.int32, shape, axis)


def hot(mask):
    return mask.astype(F32).astype(BF16)


def contract(lhs, rhs, dims, **options):
    return lax.dot_general(lhs, rhs, (dims, ((), ())), preferred_element_type=F32, **options)


def locate(ids, owners, plane, rows_dev):
    listed = ids.shape[1]
    line = iota((owners, listed), 0)
    layer = line & (LAYERS - 1)
    column = lax.shift_right_logical(line, LAYERS.bit_length() - 1)
    first = (layer * plane + column) * rows_dev
    member = ((ids >= first) & (ids < first + rows_dev)).astype(F32)
    before = iota((listed, listed), 0) < iota((listed, listed), 1)
    earlier = contract(member.astype(BF16), hot(before), ((1,), (0,)))
    rank = jnp.sum(member * earlier, axis=0, keepdims=True).astype(jnp.int32)
    spot = jnp.sum(member * line.astype(F32), axis=0, keepdims=True).astype(jnp.int32)
    start = jnp.sum(member * first.astype(F32), axis=0, keepdims=True).astype(jnp.int32)
    held = (member * (ids - start + 1).astype(F32)).astype(BF16)
    return rank, spot, held


def mix_picks(slots_t, weights_t, listed):
    picks, tokens = slots_t.shape
    position = iota((listed, tokens), 0).astype(F32)

    def group(g, total):
        base = pl.multiple_of(g * UNROLL, UNROLL)
        slot = slots_t[pl.ds(base, UNROLL), :]
        weight = weights_t[pl.ds(base, UNROLL), :]
        for p in range(UNROLL):
            hit = slot[p : p + 1] == position
            total = total + jnp.where(hit, weight[p : p + 1], 0.0)
        return total

    start = jnp.zeros((listed, tokens), F32)
    return lax.fori_loop(0, picks // UNROLL, group, start)


def finish(c, gate_a, cot_a, gate_b, fetched, mix_wide, grad_memory, mixed_b, grad_gate, scores):
    tokens, features = gate_a.shape
    slot_rows = mix_wide.shape[1]
    piece = features // PIECES
    for k in range(piece // CHUNK):
        cols = pl.ds(c * piece + k * CHUNK, CHUNK)
        rows = fetched[:, :, :, cols].reshape(slot_rows, CHUNK)
        memory = contract(mix_wide[...], rows, ((1,), (0,)))
        gate = gate_a[:, cols].astype(F32)
        sig = jax.nn.sigmoid(gate)
        incoming = cot_a[:, cols].astype(F32)
        grad_gate[:, cols] = (
            incoming * memory[:tokens] * sig * (1.0 + gate * (1.0 - sig))
        ).astype(BF16)
        scores[...] += contract(grad_memory[:, cols], rows, ((1,), (1,)))
        gate = gate_b[:, cols].astype(F32)
        mixed_b[:, cols] = (gate * jax.nn.sigmoid(gate) * memory[tokens:]).astype(BF16)


def drain(block, sem):
    pltpu.make_async_copy(block, block, sem).wait()


def exchange(
    gate_a_in, cot_a_in, gate_b_in, table_in, row_ids_in, slots_in, weights_in,
    mixed_b, grad_gate, grad_table, scores, wide_list, slots,
    gate_a, cot_a, gate_b, fetched, mix_wide, grad_memory,
    row_ids, weights, col, aux, slots_t, weights_t, mix_tall,
    message, asked, codes, codes_sum, codes_aux, grads_out, arrived, rows_out, rows_aux,
    rs_out, rs_in,
    load, send, ask_recv, tab_recv, par_recv, aux_recv, grad_recv, row_recv, rs_recv,
):
    sections = lax.axis_size("section")
    owners = lax.axis_size("table")
    plane = owners // LAYERS
    rows_dev, features = table_in.shape
    tokens = gate_a.shape[0]
    listed = row_ids.shape[1]
    part = features // sections
    group = sections * plane
    width = group * ROW_LIMIT
    piece = features // PIECES
    far = FAR_EIGHTHS * piece // 8
    last = LAYERS - 1

    sec = lax.axis_index("section")
    me = lax.axis_index("table")
    z = me // plane
    p_me = lax.rem(me, plane)
    seat = sec * plane + p_me
    parity = lax.rem(sec, 2)
    partner = sec + 1 - 2 * parity
    step_z = 1 - 2 * parity
    ahead_ok = (z + step_z >= 0) & (z + step_z <= last)

    def peer(hop):
        other, bit = p_me, 1
        while bit < plane:
            if hop & bit:
                other = other + bit - 2 * bit * lax.rem(p_me // bit, 2)
            bit *= 2
        return other

    x_side, y_side, corner = peer(1), peer(2), peer(3)

    def strip(c):
        if isinstance(c, int):
            return pl.ds(c * piece, piece)
        return pl.ds(pl.multiple_of(c * piece, piece), piece)

    def half(n):
        return pl.ds(n * (features // HALVES), features // HALVES)

    def other_section(hop):
        return lax.rem(sec + hop, sections)

    def need(k):
        return jnp.where(z < LAYERS // 2, last - k, k)

    def at(layer, place):
        return layer * plane + place

    def greet(s, t):
        pl.semaphore_signal(
            pltpu.get_barrier_semaphore(), inc=1,
            device_id={"section": s, "table": t}, device_id_type=MESH,
        )

    def remote(source, target, send, recv, s, t):
        pltpu.make_async_remote_copy(
            src_ref=source, dst_ref=target, send_sem=send, recv_sem=recv,
            device_id={"section": s, "table": t}, device_id_type=MESH,
        ).start()

    for hop in range(plane):
        for turn in range(sections):
            if hop or turn:
                greet(other_section(turn), at(z, peer(hop)))

    @pl.when(z > 0)
    def _():
        greet(sec, at(z - 1, p_me))

    @pl.when(z < last)
    def _():
        greet(sec, at(z + 1, p_me))

    pltpu.make_async_copy(row_ids_in, row_ids, load.at[4]).start()
    pltpu.make_async_copy(table_in, col.at[z], load.at[0]).start()
    pltpu.make_async_copy(slots_in, slots, load.at[5]).start()
    pltpu.make_async_copy(weights_in, weights, load.at[6]).start()
    pltpu.make_async_copy(gate_a_in, gate_a, load.at[1]).start()
    pltpu.make_async_copy(cot_a_in, cot_a, load.at[2]).start()
    pltpu.make_async_copy(gate_b_in, gate_b, load.at[3]).start()

    drain(row_ids, load.at[4])
    ids = row_ids[...]
    rank_a, spot_a, held_a = locate(ids[0:1], owners, plane, rows_dev)
    rank_b, spot_b, held_b = locate(ids[1:2], owners, plane, rows_dev)
    lane = iota((codes.shape[2], listed), 0)
    base = p_me * (2 * ROW_LIMIT) + width
    lanes_a = hot((lane == rank_a + base) | (lane == rank_a + seat * ROW_LIMIT))
    lanes_b = hot(lane == rank_b + (base + ROW_LIMIT))
    asking = contract(held_a, lanes_a, ((1,), (1,))) + contract(held_b, lanes_b, ((1,), (1,)))
    for q in range(plane):
        message[q] = asking[q * LAYERS : (q + 1) * LAYERS]

    signals = group - 1 + jnp.where(z > 0, 1, 0) + jnp.where(z < last, 1, 0)
    pl.semaphore_wait(pltpu.get_barrier_semaphore(), signals)

    for hop in range(plane):
        q = peer(hop)
        for turn in range(sections):
            if hop or turn:
                remote(
                    message.at[q], asked.at[seat], send, ask_recv,
                    other_section(turn), at(z, q),
                )
    pltpu.make_async_copy(message.at[p_me], asked.at[seat], ask_recv).start()

    for j, side in enumerate((x_side, y_side)):
        remote(
            message.at[corner], asked.at[group + 1 - j], send, ask_recv, sec, at(z, side)
        )

    drain(col.at[z], load.at[0])

    @pl.when(ahead_ok)
    def _():
        for n in range(HALVES):
            block = col.at[z, :, half(n)]
            remote(block, block, send, tab_recv.at[0, n], sec, at(z + step_z, p_me))

    for j, side in enumerate((x_side, y_side)):
        cols = strip(2 * j + parity)
        remote(
            col.at[z, :, cols], aux.at[z, :, cols], send, aux_recv.at[0], sec, at(z, side),
        )

    drain(slots, load.at[5])
    drain(weights, load.at[6])
    slots_t[...] = jnp.transpose(slots[...].reshape(2 * tokens, -1).astype(F32))
    weights_t[...] = jnp.transpose(weights[...].reshape(2 * tokens, -1))
    mixing_t = mix_picks(slots_t, weights_t, listed).astype(BF16)
    space = iota((owners * 2 * ROW_LIMIT, listed), 0)
    wide_a = hot(space == spot_a * (2 * ROW_LIMIT) + rank_a)
    wide_b = hot(space == spot_b * (2 * ROW_LIMIT) + (rank_b + ROW_LIMIT))
    tall_a = hot(iota((owners * ROW_LIMIT, listed), 0) == spot_a * ROW_LIMIT + rank_a)
    wide_list[...] = wide_a
    mix_tall[...] = contract(tall_a, mixing_t[:, :tokens], ((1,), (0,))).astype(BF16)

    drain(gate_a, load.at[1])
    drain(cot_a, load.at[2])

    @pl.loop(0, features // CHUNK)
    def _(c):
        per = part // CHUNK
        inner = pl.ds(pl.multiple_of(lax.rem(c, per) * CHUNK, CHUNK), CHUNK)
        cols = pl.ds(pl.multiple_of(c * CHUNK, CHUNK), CHUNK)
        gate = gate_a[:, cols].astype(F32)
        value = (cot_a[:, cols].astype(F32) * gate * jax.nn.sigmoid(gate)).astype(BF16)
        grad_memory[:, cols] = value
        rows = contract(mix_tall[...], value, ((1,), (0,))).astype(BF16)
        grads_out[c // per, :, :, :, inner] = rows.reshape(plane, LAYERS, ROW_LIMIT, CHUNK)

    for k in range(LAYERS):
        layer = need(k)
        for hop in range(plane):
            q = peer(hop)
            for turn in range(sections):
                if hop or turn:
                    other = other_section(turn)
                    remote(
                        grads_out.at[other, q, layer], arrived.at[layer, seat],
                        send, grad_recv.at[layer], other, at(z, q),
                    )
        pltpu.make_async_copy(
            grads_out.at[sec, p_me, layer], arrived.at[layer, seat], grad_recv.at[layer]
        ).start()

    drain(asked, ask_recv)
    served, summing = asked[sec * plane], asked[0]
    for q in range(1, plane):
        served = served + asked[sec * plane + q]
    for q in range(1, group):
        summing = summing + asked[q]
    for layer in range(LAYERS):
        codes[layer] = served[layer : layer + 1]
        codes_sum[layer] = summing[layer : layer + 1]

    for j, side in enumerate((x_side, y_side)):
        served = message[side] + asked[group + j]
        for layer in range(LAYERS):
            codes_aux[j, layer] = served[layer : layer + 1]

    def lookup(code):
        pick = (iota((rows_dev, code.shape[1]), 0).astype(F32) == code - 1.0).astype(F32)
        return jnp.transpose(pick)[width : width + plane * 2 * ROW_LIMIT].astype(BF16)

    def look_aside(layer):
        return [lookup(codes_aux[j, layer]) for j in range(2)]

    def span(block):
        return pl.ds(*block[1:])

    def whole(c):
        return c, c * piece, piece

    def tail(c):
        return c, (c + 1) * piece - far, far

    def find(pick, held, found, layer, block):
        _, first, size = block
        for k in range(0, size, CHUNK):
            cols = pl.ds(first + k, min(CHUNK, size - k))
            rows = contract(pick, held[layer, :, cols], ((1,), (0,))).astype(BF16)
            found[layer, :, :, cols] = rows.reshape(plane, 2 * ROW_LIMIT, -1)

    def give(found, layer, block, q, column):
        cols = span(block)
        remote(
            found.at[layer, q, :, cols], fetched.at[column, layer, :, cols],
            send, row_recv.at[block[0]], sec, at(z, q),
        )

    def keep(found, layer, block, column):
        cols = span(block)
        pltpu.make_async_copy(
            found.at[layer, p_me, :, cols], fetched.at[column, layer, :, cols],
            row_recv.at[block[0]],
        ).start()

    def valid(layer):
        return (layer >= 0) & (layer <= last)

    def inner(layer):
        return (layer > 0) & (layer < last)

    def blocks(h, c):
        if h == 0 or (h == 1 and c in PARTIAL):
            return [(whole(c), True)]
        if h == 2 and c in PARTIAL:
            return [((c, c * piece, piece - far), False), (tail(c), None)]
        return [(whole(c), None if h == 1 else False)]

    def serve(layer, pick, c, h):
        first = 2 if c < PIECES // 2 else 1
        for block, shared in blocks(h, c):
            find(pick, col, rows_out, layer, block)
            for hop in (first, *range(4, plane)):
                give(rows_out, layer, block, peer(hop), p_me)
            if shared is not True:

                @pl.when(~inner(layer) if shared is None else z >= 0)
                def _():
                    for hop in (3 - first, 3):
                        give(rows_out, layer, block, peer(hop), p_me)

            keep(rows_out, layer, block, p_me)

    def serve_aside(layer, picks, block):
        j = 2 * block[0] // PIECES
        column, target = ((x_side, y_side), (y_side, x_side))[j]
        find(picks[j], aux, rows_aux, layer, block)
        give(rows_aux, layer, block, target, column)
        keep(rows_aux, layer, block, column)

    def summed(layer, cols):
        code = codes_sum[layer][:, :width]
        pick = hot(iota((rows_dev, width), 0).astype(F32) == code - 1.0)
        block = arrived[layer, :, :, cols].reshape(width, -1)
        return contract(pick, block, ((1,), (0,)))

    each = PIECES // HALVES

    def pass_table(h, n):
        behind = z - step_z * h

        @pl.when(valid(behind))
        def _():
            block = col.at[behind, :, half(n)]
            drain(block, tab_recv.at[h - 1, n])
            if h < last:

                @pl.when(ahead_ok)
                def _():
                    remote(block, block, send, tab_recv.at[h, n], sec, at(z + step_z, p_me))

            remote(block, block, send, par_recv.at[h - 1, n], partner, me)

    def serve_layer(h, passing):
        behind, ahead = z - step_z * h, z + step_z * h

        @pl.when(valid(behind))
        def _():
            pick = lookup(codes[behind])
            for n in range(HALVES):
                if passing:
                    pass_table(h, n)
                for c in range(n * each, (n + 1) * each):
                    serve(behind, pick, c, h)

        @pl.when(valid(ahead))
        def _():
            pick = lookup(codes[ahead])
            for n in range(HALVES):
                drain(col.at[ahead, :, half(n)], par_recv.at[h - 1, n])
                for c in range(n * each, (n + 1) * each):
                    serve(ahead, pick, c, h)

    def own_aside():
        drain(col.at[z, :, half(0)], aux_recv.at[0])
        for j in range(2):
            block = aux.at[z, :, strip(2 * j + parity)]
            remote(block, block, send, aux_recv.at[1], partner, me)

    def landing(h, way, c):
        if h == 1:
            return 2 + way * PIECES + c
        return 2 + 2 * PIECES + way * len(PARTIAL) + PARTIAL.index(c)

    def near_aside(h):
        behind, ahead = z - step_z * h, z + step_z * h

        def each_block(layer, use):
            for c in sorted(range(PIECES), key=lambda c: c not in PARTIAL):
                for block, shared in blocks(h, c):
                    if shared is True:
                        use(block)
                    elif shared is None:

                        @pl.when(inner(layer))
                        def _():
                            use(block)

        @pl.when(valid(behind))
        def _():
            picks = look_aside(behind)

            def use(block):
                c = block[0]
                part = aux.at[behind, :, span(block)]
                drain(part, aux_recv.at[landing(h, 0, c)])
                if h == 1 and c in PARTIAL:

                    @pl.when(inner(behind) & ahead_ok)
                    def _():
                        onward = aux.at[behind, :, span(tail(c))]
                        remote(
                            onward, onward, send, aux_recv.at[landing(2, 0, c)],
                            sec, at(z + step_z, p_me),
                        )

                remote(part, part, send, aux_recv.at[landing(h, 1, c)], partner, me)
                serve_aside(behind, picks, block)

            each_block(behind, use)

        @pl.when(valid(ahead))
        def _():
            picks = look_aside(ahead)

            def use(block):
                drain(aux.at[ahead, :, span(block)], aux_recv.at[landing(h, 1, block[0])])
                serve_aside(ahead, picks, block)

            each_block(ahead, use)

    def reduce_step(k, starts, follows):
        for turn in range(2):
            way = jnp.where(z < LAYERS // 2, 1 - turn, turn)
            up = way == 0
            place = jnp.where(up, z, last - z)
            layer = jnp.where(up, last - (k - place), k - place)
            target = jnp.where(up, z + 1, z - 1)

            def pass_on(earlier):
                for c in range(2):
                    cols = pl.ds(c * (part // 2), part // 2)
                    if earlier:
                        drain(rs_in.at[way, k - 1, :, cols], rs_recv.at[way, k - 1, c])
                    total = summed(layer, cols)
                    if earlier:
                        total = total + rs_in[way, k - 1, :, cols].astype(F32)
                    rs_out[way, k, :, cols] = total.astype(BF16)
                    remote(
                        rs_out.at[way, k, :, cols], rs_in.at[way, k, :, cols],
                        send, rs_recv.at[way, k, c], sec, at(target, p_me),
                    )

            if starts:

                @pl.when(place == 0)
                def _():
                    drain(arrived.at[layer], grad_recv.at[layer])
                    pass_on(False)

            if follows:

                @pl.when((place > 0) & (place <= k))
                def _():
                    drain(arrived.at[layer], grad_recv.at[layer])
                    pass_on(True)

    own_aside()
    pick = lookup(codes[z])
    for c in range(PIECES):
        serve(z, pick, c, 0)
    pass_table(1, 0)
    drain(col.at[z, :, half(0)], aux_recv.at[1])
    picks = look_aside(z)
    for c in range(PIECES):
        serve_aside(z, picks, whole(c))
    for n in range(1, HALVES):
        pass_table(1, n)

    def pass_aside(c):
        block = aux.at[z, :, strip(c)]
        remote(block, block, send, aux_recv.at[landing(1, 0, c)], sec, at(z + step_z, p_me))

    @pl.when(ahead_ok)
    def _():
        for c in PARTIAL:
            pass_aside(c)

    @pl.when(ahead_ok & inner(z))
    def _():
        for c in range(PIECES):
            if c not in PARTIAL:
                pass_aside(c)

    reduce_step(0, True, False)
    serve_layer(1, False)

    mix_wide[:tokens] = contract(mixing_t[:, :tokens], wide_a, ((0,), (1,))).astype(BF16)
    mix_wide[tokens:] = contract(mixing_t[:, tokens:], wide_b, ((0,), (1,))).astype(BF16)
    scores[...] = jnp.zeros_like(scores)

    serve_layer(2, True)
    reduce_step(1, True, True)
    for k in range(2, last):
        reduce_step(k, True, False)
    near_aside(1)
    for h in range(3, LAYERS):
        serve_layer(h, True)
    near_aside(2)
    for k in range(2, last):
        reduce_step(k, False, True)

    drain(arrived.at[z], grad_recv.at[z])

    @pl.loop(0, part // CHUNK)
    def _(c):
        cols = pl.ds(pl.multiple_of(c * CHUNK, CHUNK), CHUNK)
        grad_table[:, cols] = summed(z, cols)

    drain(gate_b, load.at[3])
    for c in ORDER[:-1]:
        drain(fetched.at[:, :, :, strip(c)], row_recv.at[c])
        finish(c, gate_a, cot_a, gate_b, fetched, mix_wide, grad_memory, mixed_b, grad_gate, scores)

    for way in range(2):

        @pl.when((z > 0) if way == 0 else (z < last))
        def _():
            for c in range(2):
                cols = pl.ds(c * (part // 2), part // 2)
                drain(rs_in.at[way, last - 1, :, cols], rs_recv.at[way, last - 1, c])
                grad_table[:, cols] += rs_in[way, last - 1, :, cols].astype(F32)

    drain(fetched.at[:, :, :, strip(ORDER[-1])], row_recv.at[ORDER[-1]])
    drain(asked.at[pl.ds(0, group + 1)], send)
    drain(arrived.at[:, pl.ds(0, group - 1)], send)
    drain(rows_out.at[0, pl.ds(0, plane - 2)], send)
    for c in range(2):
        drain(col.at[z, :, strip(c)], send)
        drain(col.at[z, :, strip(c)], send)

    @pl.when(ahead_ok)
    def _():
        drain(col.at[z], send)
        drain(col.at[z, :, half(0)], send)

    @pl.when(ahead_ok & inner(z))
    def _():
        drain(col.at[z, :, half(0)], send)

    for h in range(1, LAYERS):
        behind, ahead = z - step_z * h, z + step_z * h

        @pl.when(valid(behind))
        def _():
            drain(col.at[behind], send)

            @pl.when(ahead_ok)
            def _():
                drain(col.at[behind], send)

            for c in range(PIECES):
                for block, shared in blocks(h, c):
                    if shared is True:
                        drain(aux.at[z, :, span(block)], send)
                    elif shared is None:

                        @pl.when(inner(behind))
                        def _():
                            drain(aux.at[z, :, span(block)], send)

                if h == 1 and c in PARTIAL:

                    @pl.when(inner(behind) & ahead_ok)
                    def _():
                        drain(aux.at[z, :, span(tail(c))], send)

        for layer in (behind, ahead):

            @pl.when(valid(layer))
            def _():
                drain(rows_out.at[0, pl.ds(0, plane - 2)], send)
                for c in range(PIECES):
                    for block, shared in blocks(h, c):
                        if shared is not True:

                            @pl.when(~inner(layer) if shared is None else z >= 0)
                            def _():
                                drain(rows_out.at[0, 0, :, span(block)], send)

    for k in range(last):
        for way in range(2):

            @pl.when(k >= (z if way == 0 else last - z))
            def _():
                drain(rs_out.at[way, k], send)


def store(
    mixed_b, grad_gate, grad_table, scores, wide_list, slots,
    gate_a, cot_a, gate_b, fetched, mix_wide, grad_memory,
    mixed_out, grad_gate_out, grad_table_out, grad_weights_out, grad_weights, sems,
):
    features = gate_a.shape[1]
    done = pl.ds(0, features - features // PIECES)
    rest = pl.ds(features - features // PIECES, features // PIECES)

    def put(source, target, n):
        copy = pltpu.make_async_copy(source, target, sems.at[n])
        copy.start()
        return copy

    copies = [
        put(mixed_b.at[:, done], mixed_out.at[:, done], 0),
        put(grad_gate.at[:, done], grad_gate_out.at[:, done], 1),
        put(grad_table, grad_table_out, 2),
    ]
    finish(
        ORDER[-1], gate_a, cot_a, gate_b, fetched, mix_wide, grad_memory,
        mixed_b, grad_gate, scores,
    )
    copies.append(put(mixed_b.at[:, rest], mixed_out.at[:, rest], 3))
    copies.append(put(grad_gate.at[:, rest], grad_gate_out.at[:, rest], 4))
    found = contract(
        scores[...], wide_list[...].astype(F32), ((1,), (0,)), precision=lax.Precision.HIGHEST
    )
    grad_weights[...] = jnp.take_along_axis(found, slots[0], axis=1)
    copies.append(put(grad_weights, grad_weights_out, 5))
    for copy in copies:
        copy.wait()


def local(gate_a, cotangent_a, gate_b, table, row_ids, slots, weights):
    owners = lax.axis_size("table")
    sections = lax.axis_size("section")
    plane = owners // LAYERS
    group = sections * plane
    rows_dev, features = table.shape
    tokens = gate_a.shape[1]
    listed = row_ids.shape[-1]
    picks = slots.shape[-1]
    part = features // sections
    lanes = -(-(2 * plane + group) * ROW_LIMIT // 128) * 128
    slot_rows = owners * 2 * ROW_LIMIT
    vmem = pl.BlockSpec(memory_space=pltpu.VMEM)
    hbm = pl.BlockSpec(memory_space=pl.ANY)
    dma = pltpu.SemaphoreType.DMA
    results = pl.pallas_call(
        exchange,
        out_shape=(
            pltpu.VMEM((tokens, features), BF16),
            pltpu.VMEM((tokens, features), BF16),
            pltpu.VMEM((rows_dev, part), F32),
            pltpu.VMEM((tokens, slot_rows), F32),
            pltpu.VMEM((slot_rows, listed), BF16),
            pltpu.VMEM((2, tokens, picks), jnp.int32),
            pltpu.VMEM((tokens, features), BF16),
            pltpu.VMEM((tokens, features), BF16),
            pltpu.VMEM((tokens, features), BF16),
            pltpu.VMEM((plane, LAYERS, 2 * ROW_LIMIT, features), BF16),
            pltpu.VMEM((2 * tokens, slot_rows), BF16),
            pltpu.VMEM((tokens, features), BF16),
        ),
        in_specs=[pl.BlockSpec(memory_space=pltpu.HBM)] * 7,
        out_specs=(vmem,) * 12,
        scratch_shapes=[
            pltpu.VMEM((2, listed), jnp.int32),
            pltpu.VMEM((2, tokens, picks), F32),
            pltpu.VMEM((LAYERS, rows_dev, features), BF16),
            pltpu.VMEM((LAYERS, rows_dev, features), BF16),
            pltpu.VMEM((picks, 2 * tokens), F32),
            pltpu.VMEM((picks, 2 * tokens), F32),
            pltpu.VMEM((owners * ROW_LIMIT, tokens), BF16),
            pltpu.VMEM((plane, LAYERS, lanes), F32),
            pltpu.VMEM((group + 2, LAYERS, lanes), F32),
            pltpu.VMEM((LAYERS, 1, lanes), F32),
            pltpu.VMEM((LAYERS, 1, lanes), F32),
            pltpu.VMEM((2, LAYERS, 1, lanes), F32),
            pltpu.VMEM((sections, plane, LAYERS, ROW_LIMIT, part), BF16),
            pltpu.VMEM((LAYERS, group, ROW_LIMIT, part), BF16),
            pltpu.VMEM((LAYERS, plane, 2 * ROW_LIMIT, features), BF16),
            pltpu.VMEM((LAYERS, plane, 2 * ROW_LIMIT, features), BF16),
            pltpu.VMEM((2, LAYERS - 1, rows_dev, part), BF16),
            pltpu.VMEM((2, LAYERS - 1, rows_dev, part), BF16),
            dma((7,)),
            dma,
            dma,
            dma((LAYERS - 1, HALVES)),
            dma((LAYERS - 1, HALVES)),
            dma((2 + 2 * PIECES + 2 * len(PARTIAL),)),
            dma((LAYERS,)),
            dma((PIECES,)),
            dma((2, LAYERS - 1, HALVES)),
        ],
        compiler_params=pltpu.CompilerParams(
            collective_id=0, has_side_effects=True, vmem_limit_bytes=44 * 1024 * 1024
        ),
    )(
        *(
            pltpu.with_memory_space_constraint(x, pltpu.HBM)
            for x in (
                gate_a[0], cotangent_a[0], gate_b[0], table, row_ids[0, :, 0], slots[0], weights[0]
            )
        )
    )
    mixed_b, grad_gate, grad_table, grad_weights = pl.pallas_call(
        store,
        out_shape=(
            jax.ShapeDtypeStruct((tokens, features), BF16),
            jax.ShapeDtypeStruct((tokens, features), BF16),
            jax.ShapeDtypeStruct((rows_dev, part), F32),
            jax.ShapeDtypeStruct((tokens, picks), F32),
        ),
        in_specs=[vmem] * 12,
        out_specs=(hbm,) * 4,
        scratch_shapes=[pltpu.VMEM((tokens, picks), F32), dma((6,))],
        compiler_params=pltpu.CompilerParams(vmem_limit_bytes=8 * 1024 * 1024),
    )(*(pltpu.with_memory_space_constraint(r, pltpu.VMEM) for r in results))
    return mixed_b[None], grad_gate[None], grad_weights[None], grad_table


def solution(mesh):
    return jax.shard_map(
        local,
        mesh=mesh,
        in_specs=(
            P("section", "table", None),
            P("section", "table", None),
            P("section", "table", None),
            P("table", None),
            P("section", None, "table", None),
            P("section", None, "table", None),
            P("section", None, "table", None),
        ),
        out_specs=(
            P("section", "table", None),
            P("section", "table", None),
            P("section", "table", None),
            P("table", "section"),
        ),
        check_vma=False,
    )
```

```python
import jax
import jax.numpy as jnp
from jax import lax
from jax.experimental import pallas as pl
from jax.experimental.pallas import tpu as pltpu
from jax.sharding import PartitionSpec as P

ROW_LIMIT = 8
CHUNK = 512
LAYERS = 4
PIECES = 4
PARTIAL = (1, 3)
ORDER = (0, 2, 1, 3)
HALVES = 2
FAR_EIGHTHS = 5
UNROLL = 8
MESH = pl.DeviceIdType.MESH
BF16, F32 = jnp.bfloat16, jnp.float32


def iota(shape, axis):
    return lax.broadcasted_iota(jnp.int32, shape, axis)


def hot(mask):
    return mask.astype(F32).astype(BF16)


def contract(lhs, rhs, dims, **options):
    return lax.dot_general(lhs, rhs, (dims, ((), ())), preferred_element_type=F32, **options)


def locate(ids, owners, plane, rows_dev):
    listed = ids.shape[1]
    line = iota((owners, listed), 0)
    layer = line & (LAYERS - 1)
    column = lax.shift_right_logical(line, LAYERS.bit_length() - 1)
    first = (layer * plane + column) * rows_dev
    member = ((ids >= first) & (ids < first + rows_dev)).astype(F32)
    before = iota((listed, listed), 0) < iota((listed, listed), 1)
    earlier = contract(member.astype(BF16), hot(before), ((1,), (0,)))
    rank = jnp.sum(member * earlier, axis=0, keepdims=True).astype(jnp.int32)
    spot = jnp.sum(member * line.astype(F32), axis=0, keepdims=True).astype(jnp.int32)
    start = jnp.sum(member * first.astype(F32), axis=0, keepdims=True).astype(jnp.int32)
    held = (member * (ids - start + 1).astype(F32)).astype(BF16)
    return rank, spot, held


def mix_picks(slots_t, weights_t, listed):
    picks, tokens = slots_t.shape
    position = iota((listed, tokens), 0).astype(F32)

    def group(g, total):
        base = pl.multiple_of(g * UNROLL, UNROLL)
        slot = slots_t[pl.ds(base, UNROLL), :]
        weight = weights_t[pl.ds(base, UNROLL), :]
        for p in range(UNROLL):
            hit = slot[p : p + 1] == position
            total = total + jnp.where(hit, weight[p : p + 1], 0.0)
        return total

    start = jnp.zeros((listed, tokens), F32)
    return lax.fori_loop(0, picks // UNROLL, group, start)


def finish(c, gate_a, cot_a, gate_b, fetched, mix_wide, grad_memory, mixed_b, grad_gate, scores):
    tokens, features = gate_a.shape
    slot_rows = mix_wide.shape[1]
    piece = features // PIECES
    for k in range(piece // CHUNK):
        cols = pl.ds(c * piece + k * CHUNK, CHUNK)
        rows = fetched[:, :, :, cols].reshape(slot_rows, CHUNK)
        memory = contract(mix_wide[...], rows, ((1,), (0,)))
        gate = gate_a[:, cols].astype(F32)
        sig = jax.nn.sigmoid(gate)
        incoming = cot_a[:, cols].astype(F32)
        grad_gate[:, cols] = (
            incoming * memory[:tokens] * sig * (1.0 + gate * (1.0 - sig))
        ).astype(BF16)
        scores[...] += contract(grad_memory[:, cols], rows, ((1,), (1,)))
        gate = gate_b[:, cols].astype(F32)
        mixed_b[:, cols] = (gate * jax.nn.sigmoid(gate) * memory[tokens:]).astype(BF16)


def drain(block, sem):
    pltpu.make_async_copy(block, block, sem).wait()


def exchange(
    gate_a_in, cot_a_in, gate_b_in, table_in, row_ids_in, slots_in, weights_in,
    mixed_b, grad_gate, grad_table, scores, spots,
    gate_a, cot_a, gate_b, fetched, mix_wide, grad_memory,
    row_ids, slots, weights, col, aux, slots_t, weights_t, mix_tall,
    message, asked, codes, codes_sum, codes_aux, grads_out, arrived, rows_out, rows_aux,
    rs_out, rs_in,
    load, send, ask_recv, tab_recv, par_recv, aux_recv, grad_recv, row_recv, rs_recv,
):
    sections = lax.axis_size("section")
    owners = lax.axis_size("table")
    plane = owners // LAYERS
    rows_dev, features = table_in.shape
    tokens = gate_a.shape[0]
    listed = row_ids.shape[1]
    part = features // sections
    group = sections * plane
    width = group * ROW_LIMIT
    piece = features // PIECES
    far = FAR_EIGHTHS * piece // 8
    last = LAYERS - 1

    sec = lax.axis_index("section")
    me = lax.axis_index("table")
    z = me // plane
    p_me = lax.rem(me, plane)
    seat = sec * plane + p_me
    parity = lax.rem(sec, 2)
    partner = sec + 1 - 2 * parity
    step_z = 1 - 2 * parity
    ahead_ok = (z + step_z >= 0) & (z + step_z <= last)

    def peer(hop):
        other, bit = p_me, 1
        while bit < plane:
            if hop & bit:
                other = other + bit - 2 * bit * lax.rem(p_me // bit, 2)
            bit *= 2
        return other

    x_side, y_side, corner = peer(1), peer(2), peer(3)

    def strip(c):
        if isinstance(c, int):
            return pl.ds(c * piece, piece)
        return pl.ds(pl.multiple_of(c * piece, piece), piece)

    def half(n):
        return pl.ds(n * (features // HALVES), features // HALVES)

    def other_section(hop):
        return lax.rem(sec + hop, sections)

    def need(k):
        return jnp.where(z < LAYERS // 2, last - k, k)

    def at(layer, place):
        return layer * plane + place

    def greet(s, t):
        pl.semaphore_signal(
            pltpu.get_barrier_semaphore(), inc=1,
            device_id={"section": s, "table": t}, device_id_type=MESH,
        )

    def remote(source, target, send, recv, s, t):
        pltpu.make_async_remote_copy(
            src_ref=source, dst_ref=target, send_sem=send, recv_sem=recv,
            device_id={"section": s, "table": t}, device_id_type=MESH,
        ).start()

    for hop in range(plane):
        for turn in range(sections):
            if hop or turn:
                greet(other_section(turn), at(z, peer(hop)))

    @pl.when(z > 0)
    def _():
        greet(sec, at(z - 1, p_me))

    @pl.when(z < last)
    def _():
        greet(sec, at(z + 1, p_me))

    pltpu.make_async_copy(row_ids_in, row_ids, load.at[4]).start()
    pltpu.make_async_copy(table_in, col.at[z], load.at[0]).start()
    pltpu.make_async_copy(slots_in, slots, load.at[5]).start()
    pltpu.make_async_copy(weights_in, weights, load.at[6]).start()
    pltpu.make_async_copy(gate_a_in, gate_a, load.at[1]).start()
    pltpu.make_async_copy(cot_a_in, cot_a, load.at[2]).start()
    pltpu.make_async_copy(gate_b_in, gate_b, load.at[3]).start()

    drain(row_ids, load.at[4])
    ids = row_ids[...]
    rank_a, spot_a, held_a = locate(ids[0:1], owners, plane, rows_dev)
    rank_b, spot_b, held_b = locate(ids[1:2], owners, plane, rows_dev)
    lane = iota((codes.shape[2], listed), 0)
    base = p_me * (2 * ROW_LIMIT) + width
    lanes_a = hot((lane == rank_a + base) | (lane == rank_a + seat * ROW_LIMIT))
    lanes_b = hot(lane == rank_b + (base + ROW_LIMIT))
    asking = contract(held_a, lanes_a, ((1,), (1,))) + contract(held_b, lanes_b, ((1,), (1,)))
    for q in range(plane):
        message[q] = asking[q * LAYERS : (q + 1) * LAYERS]

    signals = group - 1 + jnp.where(z > 0, 1, 0) + jnp.where(z < last, 1, 0)
    pl.semaphore_wait(pltpu.get_barrier_semaphore(), signals)

    for hop in range(plane):
        q = peer(hop)
        for turn in range(sections):
            if hop or turn:
                remote(
                    message.at[q], asked.at[seat], send, ask_recv,
                    other_section(turn), at(z, q),
                )
    pltpu.make_async_copy(message.at[p_me], asked.at[seat], ask_recv).start()

    for j, side in enumerate((x_side, y_side)):
        remote(
            message.at[corner], asked.at[group + 1 - j], send, ask_recv, sec, at(z, side)
        )

    drain(col.at[z], load.at[0])

    @pl.when(ahead_ok)
    def _():
        for n in range(HALVES):
            block = col.at[z, :, half(n)]
            remote(block, block, send, tab_recv.at[0, n], sec, at(z + step_z, p_me))

    for j, side in enumerate((x_side, y_side)):
        cols = strip(2 * j + parity)
        remote(
            col.at[z, :, cols], aux.at[z, :, cols], send, aux_recv.at[0], sec, at(z, side),
        )

    drain(slots, load.at[5])
    drain(weights, load.at[6])
    slots_t[...] = jnp.transpose(slots[...].reshape(2 * tokens, -1).astype(F32))
    weights_t[...] = jnp.transpose(weights[...].reshape(2 * tokens, -1))
    mixing_t = mix_picks(slots_t, weights_t, listed).astype(BF16)
    space = iota((owners * 2 * ROW_LIMIT, listed), 0)
    wide_a = hot(space == spot_a * (2 * ROW_LIMIT) + rank_a)
    wide_b = hot(space == spot_b * (2 * ROW_LIMIT) + (rank_b + ROW_LIMIT))
    tall_a = hot(iota((owners * ROW_LIMIT, listed), 0) == spot_a * ROW_LIMIT + rank_a)
    mix_tall[...] = contract(tall_a, mixing_t[:, :tokens], ((1,), (0,))).astype(BF16)

    drain(gate_a, load.at[1])
    drain(cot_a, load.at[2])

    @pl.loop(0, features // CHUNK)
    def _(c):
        per = part // CHUNK
        inner = pl.ds(pl.multiple_of(lax.rem(c, per) * CHUNK, CHUNK), CHUNK)
        cols = pl.ds(pl.multiple_of(c * CHUNK, CHUNK), CHUNK)
        gate = gate_a[:, cols].astype(F32)
        value = (cot_a[:, cols].astype(F32) * gate * jax.nn.sigmoid(gate)).astype(BF16)
        grad_memory[:, cols] = value
        rows = contract(mix_tall[...], value, ((1,), (0,))).astype(BF16)
        grads_out[c // per, :, :, :, inner] = rows.reshape(plane, LAYERS, ROW_LIMIT, CHUNK)

    for k in range(LAYERS):
        layer = need(k)
        for hop in range(plane):
            q = peer(hop)
            for turn in range(sections):
                if hop or turn:
                    other = other_section(turn)
                    remote(
                        grads_out.at[other, q, layer], arrived.at[layer, seat],
                        send, grad_recv.at[layer], other, at(z, q),
                    )
        pltpu.make_async_copy(
            grads_out.at[sec, p_me, layer], arrived.at[layer, seat], grad_recv.at[layer]
        ).start()

    drain(asked, ask_recv)
    served, summing = asked[sec * plane], asked[0]
    for q in range(1, plane):
        served = served + asked[sec * plane + q]
    for q in range(1, group):
        summing = summing + asked[q]
    for layer in range(LAYERS):
        codes[layer] = served[layer : layer + 1]
        codes_sum[layer] = summing[layer : layer + 1]

    for j, side in enumerate((x_side, y_side)):
        served = message[side] + asked[group + j]
        for layer in range(LAYERS):
            codes_aux[j, layer] = served[layer : layer + 1]

    def lookup(code):
        pick = (iota((rows_dev, code.shape[1]), 0).astype(F32) == code - 1.0).astype(F32)
        return jnp.transpose(pick)[width : width + plane * 2 * ROW_LIMIT].astype(BF16)

    def look_aside(layer):
        return [lookup(codes_aux[j, layer]) for j in range(2)]

    def span(block):
        return pl.ds(*block[1:])

    def whole(c):
        return c, c * piece, piece

    def tail(c):
        return c, (c + 1) * piece - far, far

    def find(pick, held, found, layer, block):
        _, first, size = block
        for k in range(0, size, CHUNK):
            cols = pl.ds(first + k, min(CHUNK, size - k))
            rows = contract(pick, held[layer, :, cols], ((1,), (0,))).astype(BF16)
            found[layer, :, :, cols] = rows.reshape(plane, 2 * ROW_LIMIT, -1)

    def give(found, layer, block, q, column):
        cols = span(block)
        remote(
            found.at[layer, q, :, cols], fetched.at[column, layer, :, cols],
            send, row_recv.at[block[0]], sec, at(z, q),
        )

    def keep(found, layer, block, column):
        cols = span(block)
        pltpu.make_async_copy(
            found.at[layer, p_me, :, cols], fetched.at[column, layer, :, cols],
            row_recv.at[block[0]],
        ).start()

    def valid(layer):
        return (layer >= 0) & (layer <= last)

    def inner(layer):
        return (layer > 0) & (layer < last)

    def blocks(h, c):
        if h == 0 or (h == 1 and c in PARTIAL):
            return [(whole(c), True)]
        if h == 2 and c in PARTIAL:
            return [((c, c * piece, piece - far), False), (tail(c), None)]
        return [(whole(c), None if h == 1 else False)]

    def serve(layer, pick, c, h):
        first = 2 if c < PIECES // 2 else 1
        for block, shared in blocks(h, c):
            find(pick, col, rows_out, layer, block)
            for hop in (first, *range(4, plane)):
                give(rows_out, layer, block, peer(hop), p_me)
            if shared is not True:

                @pl.when(~inner(layer) if shared is None else z >= 0)
                def _():
                    for hop in (3 - first, 3):
                        give(rows_out, layer, block, peer(hop), p_me)

            keep(rows_out, layer, block, p_me)

    def serve_aside(layer, picks, block):
        j = 2 * block[0] // PIECES
        column, target = ((x_side, y_side), (y_side, x_side))[j]
        find(picks[j], aux, rows_aux, layer, block)
        give(rows_aux, layer, block, target, column)
        keep(rows_aux, layer, block, column)

    def summed(layer, cols):
        code = codes_sum[layer][:, :width]
        pick = hot(iota((rows_dev, width), 0).astype(F32) == code - 1.0)
        block = arrived[layer, :, :, cols].reshape(width, -1)
        return contract(pick, block, ((1,), (0,)))

    each = PIECES // HALVES

    def pass_table(h, n):
        behind = z - step_z * h

        @pl.when(valid(behind))
        def _():
            block = col.at[behind, :, half(n)]
            drain(block, tab_recv.at[h - 1, n])
            if h < last:

                @pl.when(ahead_ok)
                def _():
                    remote(block, block, send, tab_recv.at[h, n], sec, at(z + step_z, p_me))

            remote(block, block, send, par_recv.at[h - 1, n], partner, me)

    def serve_layer(h, passing):
        behind, ahead = z - step_z * h, z + step_z * h

        @pl.when(valid(behind))
        def _():
            pick = lookup(codes[behind])
            for n in range(HALVES):
                if passing:
                    pass_table(h, n)
                for c in range(n * each, (n + 1) * each):
                    serve(behind, pick, c, h)

        @pl.when(valid(ahead))
        def _():
            pick = lookup(codes[ahead])
            for n in range(HALVES):
                drain(col.at[ahead, :, half(n)], par_recv.at[h - 1, n])
                for c in range(n * each, (n + 1) * each):
                    serve(ahead, pick, c, h)

    def own_aside():
        drain(col.at[z, :, half(0)], aux_recv.at[0])
        for j in range(2):
            block = aux.at[z, :, strip(2 * j + parity)]
            remote(block, block, send, aux_recv.at[1], partner, me)

    def landing(h, way, c):
        if h == 1:
            return 2 + way * PIECES + c
        return 2 + 2 * PIECES + way * len(PARTIAL) + PARTIAL.index(c)

    def near_aside(h):
        behind, ahead = z - step_z * h, z + step_z * h

        def each_block(layer, use):
            for c in sorted(range(PIECES), key=lambda c: c not in PARTIAL):
                for block, shared in blocks(h, c):
                    if shared is True:
                        use(block)
                    elif shared is None:

                        @pl.when(inner(layer))
                        def _():
                            use(block)

        @pl.when(valid(behind))
        def _():
            picks = look_aside(behind)

            def use(block):
                c = block[0]
                part = aux.at[behind, :, span(block)]
                drain(part, aux_recv.at[landing(h, 0, c)])
                if h == 1 and c in PARTIAL:

                    @pl.when(inner(behind) & ahead_ok)
                    def _():
                        onward = aux.at[behind, :, span(tail(c))]
                        remote(
                            onward, onward, send, aux_recv.at[landing(2, 0, c)],
                            sec, at(z + step_z, p_me),
                        )

                remote(part, part, send, aux_recv.at[landing(h, 1, c)], partner, me)
                serve_aside(behind, picks, block)

            each_block(behind, use)

        @pl.when(valid(ahead))
        def _():
            picks = look_aside(ahead)

            def use(block):
                drain(aux.at[ahead, :, span(block)], aux_recv.at[landing(h, 1, block[0])])
                serve_aside(ahead, picks, block)

            each_block(ahead, use)

    def reduce_step(k, starts, follows):
        for turn in range(2):
            way = jnp.where(z < LAYERS // 2, 1 - turn, turn)
            up = way == 0
            place = jnp.where(up, z, last - z)
            layer = jnp.where(up, last - (k - place), k - place)
            target = jnp.where(up, z + 1, z - 1)

            def pass_on(earlier):
                for c in range(2):
                    cols = pl.ds(c * (part // 2), part // 2)
                    if earlier:
                        drain(rs_in.at[way, k - 1, :, cols], rs_recv.at[way, k - 1, c])
                    total = summed(layer, cols)
                    if earlier:
                        total = total + rs_in[way, k - 1, :, cols].astype(F32)
                    rs_out[way, k, :, cols] = total.astype(BF16)
                    remote(
                        rs_out.at[way, k, :, cols], rs_in.at[way, k, :, cols],
                        send, rs_recv.at[way, k, c], sec, at(target, p_me),
                    )

            if starts:

                @pl.when(place == 0)
                def _():
                    drain(arrived.at[layer], grad_recv.at[layer])
                    pass_on(False)

            if follows:

                @pl.when((place > 0) & (place <= k))
                def _():
                    drain(arrived.at[layer], grad_recv.at[layer])
                    pass_on(True)

    own_aside()
    pick = lookup(codes[z])
    for c in range(PIECES):
        serve(z, pick, c, 0)
    pass_table(1, 0)
    drain(col.at[z, :, half(0)], aux_recv.at[1])
    picks = look_aside(z)
    for c in range(PIECES):
        serve_aside(z, picks, whole(c))
    for n in range(1, HALVES):
        pass_table(1, n)

    def pass_aside(c):
        block = aux.at[z, :, strip(c)]
        remote(block, block, send, aux_recv.at[landing(1, 0, c)], sec, at(z + step_z, p_me))

    @pl.when(ahead_ok & inner(z))
    def _():
        for c in sorted(range(PIECES), key=lambda c: c not in PARTIAL):
            pass_aside(c)

    reduce_step(0, True, False)

    @pl.when(ahead_ok & ~inner(z))
    def _():
        for c in PARTIAL:
            pass_aside(c)

    serve_layer(1, False)

    mix_wide[:tokens] = contract(mixing_t[:, :tokens], wide_a, ((0,), (1,))).astype(BF16)
    mix_wide[tokens:] = contract(mixing_t[:, tokens:], wide_b, ((0,), (1,))).astype(BF16)
    scores[...] = jnp.zeros_like(scores)
    place_a = jnp.broadcast_to(spot_a * (2 * ROW_LIMIT) + rank_a, (tokens, listed))
    spots[...] = jnp.take_along_axis(place_a, slots[0], axis=1)

    serve_layer(2, True)
    reduce_step(1, True, True)
    near_aside(1)
    for k in range(2, last):
        reduce_step(k, True, False)
    for h in range(3, LAYERS):
        serve_layer(h, True)
    near_aside(2)
    for k in range(2, last):
        reduce_step(k, False, True)

    drain(arrived.at[z], grad_recv.at[z])

    @pl.loop(0, part // CHUNK)
    def _(c):
        cols = pl.ds(pl.multiple_of(c * CHUNK, CHUNK), CHUNK)
        grad_table[:, cols] = summed(z, cols)

    drain(gate_b, load.at[3])
    for c in ORDER[:-1]:
        drain(fetched.at[:, :, :, strip(c)], row_recv.at[c])
        finish(c, gate_a, cot_a, gate_b, fetched, mix_wide, grad_memory, mixed_b, grad_gate, scores)

    for way in range(2):

        @pl.when((z > 0) if way == 0 else (z < last))
        def _():
            for c in range(2):
                cols = pl.ds(c * (part // 2), part // 2)
                drain(rs_in.at[way, last - 1, :, cols], rs_recv.at[way, last - 1, c])
                grad_table[:, cols] += rs_in[way, last - 1, :, cols].astype(F32)

    drain(fetched.at[:, :, :, strip(ORDER[-1])], row_recv.at[ORDER[-1]])
    drain(asked.at[pl.ds(0, group + 1)], send)
    drain(arrived.at[:, pl.ds(0, group - 1)], send)
    drain(rows_out.at[0, pl.ds(0, plane - 2)], send)
    for c in range(2):
        drain(col.at[z, :, strip(c)], send)
        drain(col.at[z, :, strip(c)], send)

    @pl.when(ahead_ok)
    def _():
        drain(col.at[z], send)
        drain(col.at[z, :, half(0)], send)

    @pl.when(ahead_ok & inner(z))
    def _():
        drain(col.at[z, :, half(0)], send)

    for h in range(1, LAYERS):
        behind, ahead = z - step_z * h, z + step_z * h

        @pl.when(valid(behind))
        def _():
            drain(col.at[behind], send)

            @pl.when(ahead_ok)
            def _():
                drain(col.at[behind], send)

            for c in range(PIECES):
                for block, shared in blocks(h, c):
                    if shared is True:
                        drain(aux.at[z, :, span(block)], send)
                    elif shared is None:

                        @pl.when(inner(behind))
                        def _():
                            drain(aux.at[z, :, span(block)], send)

                if h == 1 and c in PARTIAL:

                    @pl.when(inner(behind) & ahead_ok)
                    def _():
                        drain(aux.at[z, :, span(tail(c))], send)

        for layer in (behind, ahead):

            @pl.when(valid(layer))
            def _():
                drain(rows_out.at[0, pl.ds(0, plane - 2)], send)
                for c in range(PIECES):
                    for block, shared in blocks(h, c):
                        if shared is not True:

                            @pl.when(~inner(layer) if shared is None else z >= 0)
                            def _():
                                drain(rows_out.at[0, 0, :, span(block)], send)

    for k in range(last):
        for way in range(2):

            @pl.when(k >= (z if way == 0 else last - z))
            def _():
                drain(rs_out.at[way, k], send)


def store(
    mixed_b, grad_gate, grad_table, scores, spots,
    gate_a, cot_a, gate_b, fetched, mix_wide, grad_memory,
    mixed_out, grad_gate_out, grad_table_out, grad_weights_out, grad_weights, sems,
):
    features = gate_a.shape[1]
    done = pl.ds(0, features - features // PIECES)
    rest = pl.ds(features - features // PIECES, features // PIECES)

    def put(source, target, n):
        copy = pltpu.make_async_copy(source, target, sems.at[n])
        copy.start()
        return copy

    copies = [
        put(mixed_b.at[:, done], mixed_out.at[:, done], 0),
        put(grad_gate.at[:, done], grad_gate_out.at[:, done], 1),
        put(grad_table, grad_table_out, 2),
    ]
    finish(
        ORDER[-1], gate_a, cot_a, gate_b, fetched, mix_wide, grad_memory,
        mixed_b, grad_gate, scores,
    )
    copies.append(put(mixed_b.at[:, rest], mixed_out.at[:, rest], 3))
    copies.append(put(grad_gate.at[:, rest], grad_gate_out.at[:, rest], 4))
    picks = grad_weights.shape[1]
    where = spots[...]
    found = jnp.zeros(grad_weights.shape, F32)
    for first in range(0, scores.shape[1], picks):
        near = where - first
        inside = (near >= 0) & (near < picks)
        got = jnp.take_along_axis(
            scores[:, first : first + picks], jnp.where(inside, near, 0), axis=1
        )
        found = jnp.where(inside, got, found)
    grad_weights[...] = found
    copies.append(put(grad_weights, grad_weights_out, 5))
    for copy in copies:
        copy.wait()


def local(gate_a, cotangent_a, gate_b, table, row_ids, slots, weights):
    owners = lax.axis_size("table")
    sections = lax.axis_size("section")
    plane = owners // LAYERS
    group = sections * plane
    rows_dev, features = table.shape
    tokens = gate_a.shape[1]
    listed = row_ids.shape[-1]
    picks = slots.shape[-1]
    part = features // sections
    lanes = -(-(2 * plane + group) * ROW_LIMIT // 128) * 128
    slot_rows = owners * 2 * ROW_LIMIT
    vmem = pl.BlockSpec(memory_space=pltpu.VMEM)
    hbm = pl.BlockSpec(memory_space=pl.ANY)
    dma = pltpu.SemaphoreType.DMA
    results = pl.pallas_call(
        exchange,
        out_shape=(
            pltpu.VMEM((tokens, features), BF16),
            pltpu.VMEM((tokens, features), BF16),
            pltpu.VMEM((rows_dev, part), F32),
            pltpu.VMEM((tokens, slot_rows), F32),
            pltpu.VMEM((tokens, picks), jnp.int32),
            pltpu.VMEM((tokens, features), BF16),
            pltpu.VMEM((tokens, features), BF16),
            pltpu.VMEM((tokens, features), BF16),
            pltpu.VMEM((plane, LAYERS, 2 * ROW_LIMIT, features), BF16),
            pltpu.VMEM((2 * tokens, slot_rows), BF16),
            pltpu.VMEM((tokens, features), BF16),
        ),
        in_specs=[pl.BlockSpec(memory_space=pltpu.HBM)] * 7,
        out_specs=(vmem,) * 11,
        scratch_shapes=[
            pltpu.VMEM((2, listed), jnp.int32),
            pltpu.VMEM((2, tokens, picks), jnp.int32),
            pltpu.VMEM((2, tokens, picks), F32),
            pltpu.VMEM((LAYERS, rows_dev, features), BF16),
            pltpu.VMEM((LAYERS, rows_dev, features), BF16),
            pltpu.VMEM((picks, 2 * tokens), F32),
            pltpu.VMEM((picks, 2 * tokens), F32),
            pltpu.VMEM((owners * ROW_LIMIT, tokens), BF16),
            pltpu.VMEM((plane, LAYERS, lanes), F32),
            pltpu.VMEM((group + 2, LAYERS, lanes), F32),
            pltpu.VMEM((LAYERS, 1, lanes), F32),
            pltpu.VMEM((LAYERS, 1, lanes), F32),
            pltpu.VMEM((2, LAYERS, 1, lanes), F32),
            pltpu.VMEM((sections, plane, LAYERS, ROW_LIMIT, part), BF16),
            pltpu.VMEM((LAYERS, group, ROW_LIMIT, part), BF16),
            pltpu.VMEM((LAYERS, plane, 2 * ROW_LIMIT, features), BF16),
            pltpu.VMEM((LAYERS, plane, 2 * ROW_LIMIT, features), BF16),
            pltpu.VMEM((2, LAYERS - 1, rows_dev, part), BF16),
            pltpu.VMEM((2, LAYERS - 1, rows_dev, part), BF16),
            dma((7,)),
            dma,
            dma,
            dma((LAYERS - 1, HALVES)),
            dma((LAYERS - 1, HALVES)),
            dma((2 + 2 * PIECES + 2 * len(PARTIAL),)),
            dma((LAYERS,)),
            dma((PIECES,)),
            dma((2, LAYERS - 1, HALVES)),
        ],
        compiler_params=pltpu.CompilerParams(
            collective_id=0, has_side_effects=True, vmem_limit_bytes=44 * 1024 * 1024
        ),
    )(
        *(
            pltpu.with_memory_space_constraint(x, pltpu.HBM)
            for x in (
                gate_a[0], cotangent_a[0], gate_b[0], table, row_ids[0, :, 0], slots[0], weights[0]
            )
        )
    )
    mixed_b, grad_gate, grad_table, grad_weights = pl.pallas_call(
        store,
        out_shape=(
            jax.ShapeDtypeStruct((tokens, features), BF16),
            jax.ShapeDtypeStruct((tokens, features), BF16),
            jax.ShapeDtypeStruct((rows_dev, part), F32),
            jax.ShapeDtypeStruct((tokens, picks), F32),
        ),
        in_specs=[vmem] * 11,
        out_specs=(hbm,) * 4,
        scratch_shapes=[pltpu.VMEM((tokens, picks), F32), dma((6,))],
        compiler_params=pltpu.CompilerParams(vmem_limit_bytes=8 * 1024 * 1024),
    )(*(pltpu.with_memory_space_constraint(r, pltpu.VMEM) for r in results))
    return mixed_b[None], grad_gate[None], grad_weights[None], grad_table


def solution(mesh):
    return jax.shard_map(
        local,
        mesh=mesh,
        in_specs=(
            P("section", "table", None),
            P("section", "table", None),
            P("section", "table", None),
            P("table", None),
            P("section", None, "table", None),
            P("section", None, "table", None),
            P("section", None, "table", None),
        ),
        out_specs=(
            P("section", "table", None),
            P("section", "table", None),
            P("section", "table", None),
            P("table", "section"),
        ),
        check_vma=False,
    )
```

```python
import jax
import jax.numpy as jnp
from jax import lax
from jax.experimental import pallas as pl
from jax.experimental.pallas import tpu as pltpu
from jax.sharding import PartitionSpec as P

ROW_LIMIT = 8
CHUNK = 512
LAYERS = 4
PIECES = 4
PARTIAL = (1, 3)
ORDER = (0, 2, 1, 3)
HALVES = 2
FAR_EIGHTHS = 6
UNROLL = 8
MESH = pl.DeviceIdType.MESH
BF16, F32 = jnp.bfloat16, jnp.float32


def iota(shape, axis):
    return lax.broadcasted_iota(jnp.int32, shape, axis)


def hot(mask):
    return mask.astype(F32).astype(BF16)


def contract(lhs, rhs, dims, **options):
    return lax.dot_general(lhs, rhs, (dims, ((), ())), preferred_element_type=F32, **options)


def locate(ids, owners, plane, rows_dev):
    listed = ids.shape[1]
    line = iota((owners, listed), 0)
    layer = line & (LAYERS - 1)
    column = lax.shift_right_logical(line, LAYERS.bit_length() - 1)
    first = (layer * plane + column) * rows_dev
    member = ((ids >= first) & (ids < first + rows_dev)).astype(F32)
    before = iota((listed, listed), 0) < iota((listed, listed), 1)
    earlier = contract(member.astype(BF16), hot(before), ((1,), (0,)))
    rank = jnp.sum(member * earlier, axis=0, keepdims=True).astype(jnp.int32)
    spot = jnp.sum(member * line.astype(F32), axis=0, keepdims=True).astype(jnp.int32)
    start = jnp.sum(member * first.astype(F32), axis=0, keepdims=True).astype(jnp.int32)
    held = (member * (ids - start + 1).astype(F32)).astype(BF16)
    return rank, spot, held


def mix_picks(slots_t, weights_t, listed):
    picks, tokens = slots_t.shape
    position = iota((listed, tokens), 0).astype(F32)

    def group(g, total):
        base = pl.multiple_of(g * UNROLL, UNROLL)
        slot = slots_t[pl.ds(base, UNROLL), :]
        weight = weights_t[pl.ds(base, UNROLL), :]
        for p in range(UNROLL):
            hit = slot[p : p + 1] == position
            total = total + jnp.where(hit, weight[p : p + 1], 0.0)
        return total

    start = jnp.zeros((listed, tokens), F32)
    return lax.fori_loop(0, picks // UNROLL, group, start)


def finish(c, gate_a, cot_a, gate_b, fetched, mix_wide, grad_memory, mixed_b, grad_gate, scores):
    tokens, features = gate_a.shape
    slot_rows = mix_wide.shape[1]
    piece = features // PIECES
    for k in range(piece // CHUNK):
        cols = pl.ds(c * piece + k * CHUNK, CHUNK)
        rows = fetched[:, :, :, cols].reshape(slot_rows, CHUNK)
        memory = contract(mix_wide[...], rows, ((1,), (0,)))
        gate = gate_a[:, cols].astype(F32)
        sig = jax.nn.sigmoid(gate)
        incoming = cot_a[:, cols].astype(F32)
        grad_gate[:, cols] = (
            incoming * memory[:tokens] * sig * (1.0 + gate * (1.0 - sig))
        ).astype(BF16)
        scores[...] += contract(grad_memory[:, cols], rows, ((1,), (1,)))
        gate = gate_b[:, cols].astype(F32)
        mixed_b[:, cols] = (gate * jax.nn.sigmoid(gate) * memory[tokens:]).astype(BF16)


def drain(block, sem):
    pltpu.make_async_copy(block, block, sem).wait()


def exchange(
    gate_a_in, cot_a_in, gate_b_in, table_in, row_ids_in, slots_in, weights_in,
    mixed_b, grad_gate, grad_table, scores, spots,
    gate_a, cot_a, gate_b, fetched, mix_wide, grad_memory,
    row_ids, slots, weights, col, aux, slots_t, weights_t, mix_tall,
    message, asked, codes, codes_sum, codes_aux, grads_out, arrived, rows_out, rows_aux,
    rs_out, rs_in,
    load, send, ask_recv, tab_recv, par_recv, aux_recv, grad_recv, row_recv, rs_recv,
    corner_in,
):
    sections = lax.axis_size("section")
    owners = lax.axis_size("table")
    plane = owners // LAYERS
    rows_dev, features = table_in.shape
    tokens = gate_a.shape[0]
    listed = row_ids.shape[1]
    part = features // sections
    group = sections * plane
    width = group * ROW_LIMIT
    piece = features // PIECES
    far = FAR_EIGHTHS * piece // 8
    last = LAYERS - 1

    sec = lax.axis_index("section")
    me = lax.axis_index("table")
    z = me // plane
    p_me = lax.rem(me, plane)
    seat = sec * plane + p_me
    parity = lax.rem(sec, 2)
    partner = sec + 1 - 2 * parity
    step_z = 1 - 2 * parity
    ahead_ok = (z + step_z >= 0) & (z + step_z <= last)

    def peer(hop):
        other, bit = p_me, 1
        while bit < plane:
            if hop & bit:
                other = other + bit - 2 * bit * lax.rem(p_me // bit, 2)
            bit *= 2
        return other

    x_side, y_side, corner = peer(1), peer(2), peer(3)

    def strip(c):
        if isinstance(c, int):
            return pl.ds(c * piece, piece)
        return pl.ds(pl.multiple_of(c * piece, piece), piece)

    def half(n):
        return pl.ds(n * (features // HALVES), features // HALVES)

    def other_section(hop):
        return lax.rem(sec + hop, sections)

    def need(k):
        return jnp.where(z < LAYERS // 2, last - k, k)

    def at(layer, place):
        return layer * plane + place

    def greet(s, t):
        pl.semaphore_signal(
            pltpu.get_barrier_semaphore(), inc=1,
            device_id={"section": s, "table": t}, device_id_type=MESH,
        )

    def remote(source, target, send, recv, s, t):
        pltpu.make_async_remote_copy(
            src_ref=source, dst_ref=target, send_sem=send, recv_sem=recv,
            device_id={"section": s, "table": t}, device_id_type=MESH,
        ).start()

    for hop in range(plane):
        for turn in range(sections):
            if (hop or turn) and hop != 3:
                greet(other_section(turn), at(z, peer(hop)))

    @pl.when(z > 0)
    def _():
        greet(sec, at(z - 1, p_me))

    @pl.when(z < last)
    def _():
        greet(sec, at(z + 1, p_me))

    pltpu.make_async_copy(row_ids_in, row_ids, load.at[4]).start()
    pltpu.make_async_copy(table_in, col.at[z], load.at[0]).start()
    pltpu.make_async_copy(slots_in, slots, load.at[5]).start()
    pltpu.make_async_copy(weights_in, weights, load.at[6]).start()
    pltpu.make_async_copy(gate_a_in, gate_a, load.at[1]).start()
    pltpu.make_async_copy(cot_a_in, cot_a, load.at[2]).start()
    pltpu.make_async_copy(gate_b_in, gate_b, load.at[3]).start()

    drain(row_ids, load.at[4])
    ids = row_ids[...]
    rank_a, spot_a, held_a = locate(ids[0:1], owners, plane, rows_dev)
    rank_b, spot_b, held_b = locate(ids[1:2], owners, plane, rows_dev)
    lane = iota((codes.shape[2], listed), 0)
    base = p_me * (2 * ROW_LIMIT) + width
    lanes_a = hot((lane == rank_a + base) | (lane == rank_a + seat * ROW_LIMIT))
    lanes_b = hot(lane == rank_b + (base + ROW_LIMIT))
    asking = contract(held_a, lanes_a, ((1,), (1,))) + contract(held_b, lanes_b, ((1,), (1,)))
    for q in range(plane):
        message[q] = asking[q * LAYERS : (q + 1) * LAYERS]

    signals = group - 1 - sections + jnp.where(z > 0, 1, 0) + jnp.where(z < last, 1, 0)
    pl.semaphore_wait(pltpu.get_barrier_semaphore(), signals)
    for side in (x_side, y_side):
        pl.semaphore_signal(
            corner_in, inc=1,
            device_id={"section": sec, "table": at(z, side)}, device_id_type=MESH,
        )

    def ask(hops):
        for hop in hops:
            q = peer(hop)
            for turn in range(sections):
                if hop or turn:
                    remote(
                        message.at[q], asked.at[seat], send, ask_recv,
                        other_section(turn), at(z, q),
                    )

    ask([hop for hop in range(plane) if hop != 3])
    pltpu.make_async_copy(message.at[p_me], asked.at[seat], ask_recv).start()

    for j, side in enumerate((x_side, y_side)):
        remote(
            message.at[corner], asked.at[group + 1 - j], send, ask_recv, sec, at(z, side)
        )

    drain(col.at[z], load.at[0])

    @pl.when(ahead_ok)
    def _():
        for n in range(HALVES):
            block = col.at[z, :, half(n)]
            remote(block, block, send, tab_recv.at[0, n], sec, at(z + step_z, p_me))

    for j, side in enumerate((x_side, y_side)):
        cols = strip(2 * j + parity)
        remote(
            col.at[z, :, cols], aux.at[z, :, cols], send, aux_recv.at[0], sec, at(z, side),
        )

    drain(slots, load.at[5])
    drain(weights, load.at[6])
    slots_t[...] = jnp.transpose(slots[...].reshape(2 * tokens, -1).astype(F32))
    weights_t[...] = jnp.transpose(weights[...].reshape(2 * tokens, -1))
    mixing_t = mix_picks(slots_t, weights_t, listed).astype(BF16)
    space = iota((owners * 2 * ROW_LIMIT, listed), 0)
    wide_a = hot(space == spot_a * (2 * ROW_LIMIT) + rank_a)
    wide_b = hot(space == spot_b * (2 * ROW_LIMIT) + (rank_b + ROW_LIMIT))
    tall_a = hot(iota((owners * ROW_LIMIT, listed), 0) == spot_a * ROW_LIMIT + rank_a)
    mix_tall[...] = contract(tall_a, mixing_t[:, :tokens], ((1,), (0,))).astype(BF16)

    pl.semaphore_wait(corner_in, 2)
    ask([3])
    drain(gate_a, load.at[1])
    drain(cot_a, load.at[2])

    @pl.loop(0, features // CHUNK)
    def _(c):
        per = part // CHUNK
        inner = pl.ds(pl.multiple_of(lax.rem(c, per) * CHUNK, CHUNK), CHUNK)
        cols = pl.ds(pl.multiple_of(c * CHUNK, CHUNK), CHUNK)
        gate = gate_a[:, cols].astype(F32)
        value = (cot_a[:, cols].astype(F32) * gate * jax.nn.sigmoid(gate)).astype(BF16)
        grad_memory[:, cols] = value
        rows = contract(mix_tall[...], value, ((1,), (0,))).astype(BF16)
        grads_out[c // per, :, :, :, inner] = rows.reshape(plane, LAYERS, ROW_LIMIT, CHUNK)

    for k in range(LAYERS):
        layer = need(k)
        for hop in range(plane):
            q = peer(hop)
            for turn in range(sections):
                if hop or turn:
                    other = other_section(turn)
                    remote(
                        grads_out.at[other, q, layer], arrived.at[layer, seat],
                        send, grad_recv.at[layer], other, at(z, q),
                    )
        pltpu.make_async_copy(
            grads_out.at[sec, p_me, layer], arrived.at[layer, seat], grad_recv.at[layer]
        ).start()

    def lookup(code):
        pick = (iota((rows_dev, code.shape[1]), 0).astype(F32) == code - 1.0).astype(F32)
        return jnp.transpose(pick)[width : width + plane * 2 * ROW_LIMIT].astype(BF16)

    def look_aside(layer):
        return [lookup(codes_aux[j, layer]) for j in range(2)]

    def span(block):
        return pl.ds(*block[1:])

    def whole(c):
        return c, c * piece, piece

    def tail(c):
        return c, (c + 1) * piece - far, far

    def find(pick, held, found, layer, block):
        _, first, size = block
        for k in range(0, size, CHUNK):
            cols = pl.ds(first + k, min(CHUNK, size - k))
            rows = contract(pick, held[layer, :, cols], ((1,), (0,))).astype(BF16)
            found[layer, :, :, cols] = rows.reshape(plane, 2 * ROW_LIMIT, -1)

    def give(found, layer, block, q, column):
        cols = span(block)
        remote(
            found.at[layer, q, :, cols], fetched.at[column, layer, :, cols],
            send, row_recv.at[block[0]], sec, at(z, q),
        )

    def keep(found, layer, block, column):
        cols = span(block)
        pltpu.make_async_copy(
            found.at[layer, p_me, :, cols], fetched.at[column, layer, :, cols],
            row_recv.at[block[0]],
        ).start()

    def valid(layer):
        return (layer >= 0) & (layer <= last)

    def inner(layer):
        return (layer > 0) & (layer < last)

    def blocks(h, c):
        if h == 0 or (h == 1 and c in PARTIAL):
            return [(whole(c), True)]
        if h == 2 and c in PARTIAL:
            return [((c, c * piece, piece - far), False), (tail(c), None)]
        return [(whole(c), None if h == 1 else False)]

    def serve(layer, pick, c, h):
        first = 2 if c < PIECES // 2 else 1
        for block, shared in blocks(h, c):
            find(pick, col, rows_out, layer, block)
            for hop in (first, *range(4, plane)):
                give(rows_out, layer, block, peer(hop), p_me)
            if shared is not True:

                @pl.when(~inner(layer) if shared is None else z >= 0)
                def _():
                    for hop in (3 - first, 3):
                        give(rows_out, layer, block, peer(hop), p_me)

            keep(rows_out, layer, block, p_me)

    def serve_aside(layer, picks, block):
        j = 2 * block[0] // PIECES
        column, target = ((x_side, y_side), (y_side, x_side))[j]
        find(picks[j], aux, rows_aux, layer, block)
        give(rows_aux, layer, block, target, column)
        keep(rows_aux, layer, block, column)

    def summed(layer, cols):
        code = codes_sum[layer][:, :width]
        pick = hot(iota((rows_dev, width), 0).astype(F32) == code - 1.0)
        block = arrived[layer, :, :, cols].reshape(width, -1)
        return contract(pick, block, ((1,), (0,)))

    each = PIECES // HALVES

    def pass_table(h, n):
        behind = z - step_z * h

        @pl.when(valid(behind))
        def _():
            block = col.at[behind, :, half(n)]
            drain(block, tab_recv.at[h - 1, n])
            if h < last:

                @pl.when(ahead_ok)
                def _():
                    remote(block, block, send, tab_recv.at[h, n], sec, at(z + step_z, p_me))

            remote(block, block, send, par_recv.at[h - 1, n], partner, me)

    def serve_layer(h, passing):
        behind, ahead = z - step_z * h, z + step_z * h

        @pl.when(valid(behind))
        def _():
            pick = lookup(codes[behind])
            for n in range(HALVES):
                if passing:
                    pass_table(h, n)
                for c in range(n * each, (n + 1) * each):
                    serve(behind, pick, c, h)

        @pl.when(valid(ahead))
        def _():
            pick = lookup(codes[ahead])
            for n in range(HALVES):
                drain(col.at[ahead, :, half(n)], par_recv.at[h - 1, n])
                for c in range(n * each, (n + 1) * each):
                    serve(ahead, pick, c, h)

    def own_aside():
        drain(col.at[z, :, half(0)], aux_recv.at[0])
        for j in range(2):
            block = aux.at[z, :, strip(2 * j + parity)]
            remote(block, block, send, aux_recv.at[1], partner, me)

    def landing(h, way, c):
        if h == 1:
            return 2 + way * PIECES + c
        return 2 + 2 * PIECES + way * len(PARTIAL) + PARTIAL.index(c)

    def near_aside(h):
        behind, ahead = z - step_z * h, z + step_z * h

        def each_block(layer, use):
            for c in sorted(range(PIECES), key=lambda c: c not in PARTIAL):
                for block, shared in blocks(h, c):
                    if shared is True:
                        use(block)
                    elif shared is None:

                        @pl.when(inner(layer))
                        def _():
                            use(block)

        @pl.when(valid(behind))
        def _():
            picks = look_aside(behind)

            def use(block):
                c = block[0]
                part = aux.at[behind, :, span(block)]
                drain(part, aux_recv.at[landing(h, 0, c)])
                if h == 1 and c in PARTIAL:

                    @pl.when(inner(behind) & ahead_ok)
                    def _():
                        onward = aux.at[behind, :, span(tail(c))]
                        remote(
                            onward, onward, send, aux_recv.at[landing(2, 0, c)],
                            sec, at(z + step_z, p_me),
                        )

                remote(part, part, send, aux_recv.at[landing(h, 1, c)], partner, me)
                serve_aside(behind, picks, block)

            each_block(behind, use)

        @pl.when(valid(ahead))
        def _():
            picks = look_aside(ahead)

            def use(block):
                drain(aux.at[ahead, :, span(block)], aux_recv.at[landing(h, 1, block[0])])
                serve_aside(ahead, picks, block)

            each_block(ahead, use)

    def reduce_step(k, starts, follows):
        for turn in range(2):
            way = jnp.where(z < LAYERS // 2, 1 - turn, turn)
            up = way == 0
            place = jnp.where(up, z, last - z)
            layer = jnp.where(up, last - (k - place), k - place)
            target = jnp.where(up, z + 1, z - 1)

            def pass_on(earlier):
                for c in range(2):
                    cols = pl.ds(c * (part // 2), part // 2)
                    if earlier:
                        drain(rs_in.at[way, k - 1, :, cols], rs_recv.at[way, k - 1, c])
                    total = summed(layer, cols)
                    if earlier:
                        total = total + rs_in[way, k - 1, :, cols].astype(F32)
                    rs_out[way, k, :, cols] = total.astype(BF16)
                    remote(
                        rs_out.at[way, k, :, cols], rs_in.at[way, k, :, cols],
                        send, rs_recv.at[way, k, c], sec, at(target, p_me),
                    )

            if starts:

                @pl.when(place == 0)
                def _():
                    drain(arrived.at[layer], grad_recv.at[layer])
                    pass_on(False)

            if follows:

                @pl.when((place > 0) & (place <= k))
                def _():
                    drain(arrived.at[layer], grad_recv.at[layer])
                    pass_on(True)

    own_aside()
    pass_table(1, 0)

    drain(asked, ask_recv)
    served, summing = asked[sec * plane], asked[0]
    for q in range(1, plane):
        served = served + asked[sec * plane + q]
    for q in range(1, group):
        summing = summing + asked[q]
    for layer in range(LAYERS):
        codes[layer] = served[layer : layer + 1]
        codes_sum[layer] = summing[layer : layer + 1]

    for j, side in enumerate((x_side, y_side)):
        served = message[side] + asked[group + j]
        for layer in range(LAYERS):
            codes_aux[j, layer] = served[layer : layer + 1]

    pick = lookup(codes[z])
    for c in range(PIECES):
        serve(z, pick, c, 0)
    drain(col.at[z, :, half(0)], aux_recv.at[1])
    picks = look_aside(z)
    for c in range(PIECES):
        serve_aside(z, picks, whole(c))
    for n in range(1, HALVES):
        pass_table(1, n)

    def pass_aside(c):
        block = aux.at[z, :, strip(c)]
        remote(block, block, send, aux_recv.at[landing(1, 0, c)], sec, at(z + step_z, p_me))

    @pl.when(ahead_ok & inner(z))
    def _():
        for c in sorted(range(PIECES), key=lambda c: c not in PARTIAL):
            pass_aside(c)

    reduce_step(0, True, False)

    @pl.when(ahead_ok & ~inner(z))
    def _():
        for c in PARTIAL:
            pass_aside(c)

    serve_layer(1, False)

    mix_wide[:tokens] = contract(mixing_t[:, :tokens], wide_a, ((0,), (1,))).astype(BF16)
    mix_wide[tokens:] = contract(mixing_t[:, tokens:], wide_b, ((0,), (1,))).astype(BF16)
    scores[...] = jnp.zeros_like(scores)
    place_a = jnp.broadcast_to(spot_a * (2 * ROW_LIMIT) + rank_a, (tokens, listed))
    spots[...] = jnp.take_along_axis(place_a, slots[0], axis=1)

    serve_layer(2, True)
    reduce_step(1, True, True)
    near_aside(1)
    for k in range(2, last):
        reduce_step(k, True, False)
    for h in range(3, LAYERS):
        serve_layer(h, True)
    near_aside(2)
    for k in range(2, last):
        reduce_step(k, False, True)

    drain(arrived.at[z], grad_recv.at[z])

    @pl.loop(0, part // CHUNK)
    def _(c):
        cols = pl.ds(pl.multiple_of(c * CHUNK, CHUNK), CHUNK)
        grad_table[:, cols] = summed(z, cols)

    drain(gate_b, load.at[3])
    for c in ORDER[:-1]:
        drain(fetched.at[:, :, :, strip(c)], row_recv.at[c])
        finish(c, gate_a, cot_a, gate_b, fetched, mix_wide, grad_memory, mixed_b, grad_gate, scores)

    for way in range(2):

        @pl.when((z > 0) if way == 0 else (z < last))
        def _():
            for c in range(2):
                cols = pl.ds(c * (part // 2), part // 2)
                drain(rs_in.at[way, last - 1, :, cols], rs_recv.at[way, last - 1, c])
                grad_table[:, cols] += rs_in[way, last - 1, :, cols].astype(F32)

    drain(fetched.at[:, :, :, strip(ORDER[-1])], row_recv.at[ORDER[-1]])
    drain(asked.at[pl.ds(0, group + 1)], send)
    drain(arrived.at[:, pl.ds(0, group - 1)], send)
    drain(rows_out.at[0, pl.ds(0, plane - 2)], send)
    for c in range(2):
        drain(col.at[z, :, strip(c)], send)
        drain(col.at[z, :, strip(c)], send)

    @pl.when(ahead_ok)
    def _():
        drain(col.at[z], send)
        drain(col.at[z, :, half(0)], send)

    @pl.when(ahead_ok & inner(z))
    def _():
        drain(col.at[z, :, half(0)], send)

    for h in range(1, LAYERS):
        behind, ahead = z - step_z * h, z + step_z * h

        @pl.when(valid(behind))
        def _():
            drain(col.at[behind], send)

            @pl.when(ahead_ok)
            def _():
                drain(col.at[behind], send)

            for c in range(PIECES):
                for block, shared in blocks(h, c):
                    if shared is True:
                        drain(aux.at[z, :, span(block)], send)
                    elif shared is None:

                        @pl.when(inner(behind))
                        def _():
                            drain(aux.at[z, :, span(block)], send)

                if h == 1 and c in PARTIAL:

                    @pl.when(inner(behind) & ahead_ok)
                    def _():
                        drain(aux.at[z, :, span(tail(c))], send)

        for layer in (behind, ahead):

            @pl.when(valid(layer))
            def _():
                drain(rows_out.at[0, pl.ds(0, plane - 2)], send)
                for c in range(PIECES):
                    for block, shared in blocks(h, c):
                        if shared is not True:

                            @pl.when(~inner(layer) if shared is None else z >= 0)
                            def _():
                                drain(rows_out.at[0, 0, :, span(block)], send)

    for k in range(last):
        for way in range(2):

            @pl.when(k >= (z if way == 0 else last - z))
            def _():
                drain(rs_out.at[way, k], send)


def store(
    mixed_b, grad_gate, grad_table, scores, spots,
    gate_a, cot_a, gate_b, fetched, mix_wide, grad_memory,
    mixed_out, grad_gate_out, grad_table_out, grad_weights_out, grad_weights, sems,
):
    features = gate_a.shape[1]
    done = pl.ds(0, features - features // PIECES)
    rest = pl.ds(features - features // PIECES, features // PIECES)

    def put(source, target, n):
        copy = pltpu.make_async_copy(source, target, sems.at[n])
        copy.start()
        return copy

    copies = [
        put(mixed_b.at[:, done], mixed_out.at[:, done], 0),
        put(grad_gate.at[:, done], grad_gate_out.at[:, done], 1),
        put(grad_table, grad_table_out, 2),
    ]
    finish(
        ORDER[-1], gate_a, cot_a, gate_b, fetched, mix_wide, grad_memory,
        mixed_b, grad_gate, scores,
    )
    copies.append(put(mixed_b.at[:, rest], mixed_out.at[:, rest], 3))
    copies.append(put(grad_gate.at[:, rest], grad_gate_out.at[:, rest], 4))
    picks = grad_weights.shape[1]
    where = spots[...]
    found = jnp.zeros(grad_weights.shape, F32)
    for first in range(0, scores.shape[1], picks):
        near = where - first
        inside = (near >= 0) & (near < picks)
        got = jnp.take_along_axis(
            scores[:, first : first + picks], jnp.where(inside, near, 0), axis=1
        )
        found = jnp.where(inside, got, found)
    grad_weights[...] = found
    copies.append(put(grad_weights, grad_weights_out, 5))
    for copy in copies:
        copy.wait()


def local(gate_a, cotangent_a, gate_b, table, row_ids, slots, weights):
    owners = lax.axis_size("table")
    sections = lax.axis_size("section")
    plane = owners // LAYERS
    group = sections * plane
    rows_dev, features = table.shape
    tokens = gate_a.shape[1]
    listed = row_ids.shape[-1]
    picks = slots.shape[-1]
    part = features // sections
    lanes = -(-(2 * plane + group) * ROW_LIMIT // 128) * 128
    slot_rows = owners * 2 * ROW_LIMIT
    vmem = pl.BlockSpec(memory_space=pltpu.VMEM)
    hbm = pl.BlockSpec(memory_space=pl.ANY)
    dma = pltpu.SemaphoreType.DMA
    results = pl.pallas_call(
        exchange,
        out_shape=(
            pltpu.VMEM((tokens, features), BF16),
            pltpu.VMEM((tokens, features), BF16),
            pltpu.VMEM((rows_dev, part), F32),
            pltpu.VMEM((tokens, slot_rows), F32),
            pltpu.VMEM((tokens, picks), jnp.int32),
            pltpu.VMEM((tokens, features), BF16),
            pltpu.VMEM((tokens, features), BF16),
            pltpu.VMEM((tokens, features), BF16),
            pltpu.VMEM((plane, LAYERS, 2 * ROW_LIMIT, features), BF16),
            pltpu.VMEM((2 * tokens, slot_rows), BF16),
            pltpu.VMEM((tokens, features), BF16),
        ),
        in_specs=[pl.BlockSpec(memory_space=pltpu.HBM)] * 7,
        out_specs=(vmem,) * 11,
        scratch_shapes=[
            pltpu.VMEM((2, listed), jnp.int32),
            pltpu.VMEM((2, tokens, picks), jnp.int32),
            pltpu.VMEM((2, tokens, picks), F32),
            pltpu.VMEM((LAYERS, rows_dev, features), BF16),
            pltpu.VMEM((LAYERS, rows_dev, features), BF16),
            pltpu.VMEM((picks, 2 * tokens), F32),
            pltpu.VMEM((picks, 2 * tokens), F32),
            pltpu.VMEM((owners * ROW_LIMIT, tokens), BF16),
            pltpu.VMEM((plane, LAYERS, lanes), F32),
            pltpu.VMEM((group + 2, LAYERS, lanes), F32),
            pltpu.VMEM((LAYERS, 1, lanes), F32),
            pltpu.VMEM((LAYERS, 1, lanes), F32),
            pltpu.VMEM((2, LAYERS, 1, lanes), F32),
            pltpu.VMEM((sections, plane, LAYERS, ROW_LIMIT, part), BF16),
            pltpu.VMEM((LAYERS, group, ROW_LIMIT, part), BF16),
            pltpu.VMEM((LAYERS, plane, 2 * ROW_LIMIT, features), BF16),
            pltpu.VMEM((LAYERS, plane, 2 * ROW_LIMIT, features), BF16),
            pltpu.VMEM((2, LAYERS - 1, rows_dev, part), BF16),
            pltpu.VMEM((2, LAYERS - 1, rows_dev, part), BF16),
            dma((7,)),
            dma,
            dma,
            dma((LAYERS - 1, HALVES)),
            dma((LAYERS - 1, HALVES)),
            dma((2 + 2 * PIECES + 2 * len(PARTIAL),)),
            dma((LAYERS,)),
            dma((PIECES,)),
            dma((2, LAYERS - 1, HALVES)),
            pltpu.SemaphoreType.REGULAR,
        ],
        compiler_params=pltpu.CompilerParams(
            collective_id=0, has_side_effects=True, vmem_limit_bytes=44 * 1024 * 1024
        ),
    )(
        *(
            pltpu.with_memory_space_constraint(x, pltpu.HBM)
            for x in (
                gate_a[0], cotangent_a[0], gate_b[0], table, row_ids[0, :, 0], slots[0], weights[0]
            )
        )
    )
    mixed_b, grad_gate, grad_table, grad_weights = pl.pallas_call(
        store,
        out_shape=(
            jax.ShapeDtypeStruct((tokens, features), BF16),
            jax.ShapeDtypeStruct((tokens, features), BF16),
            jax.ShapeDtypeStruct((rows_dev, part), F32),
            jax.ShapeDtypeStruct((tokens, picks), F32),
        ),
        in_specs=[vmem] * 11,
        out_specs=(hbm,) * 4,
        scratch_shapes=[pltpu.VMEM((tokens, picks), F32), dma((6,))],
        compiler_params=pltpu.CompilerParams(vmem_limit_bytes=8 * 1024 * 1024),
    )(*(pltpu.with_memory_space_constraint(r, pltpu.VMEM) for r in results))
    return mixed_b[None], grad_gate[None], grad_weights[None], grad_table


def solution(mesh):
    return jax.shard_map(
        local,
        mesh=mesh,
        in_specs=(
            P("section", "table", None),
            P("section", "table", None),
            P("section", "table", None),
            P("table", None),
            P("section", None, "table", None),
            P("section", None, "table", None),
            P("section", None, "table", None),
        ),
        out_specs=(
            P("section", "table", None),
            P("section", "table", None),
            P("section", "table", None),
            P("table", "section"),
        ),
        check_vma=False,
    )
```

```python
import jax
import jax.numpy as jnp
from jax import lax
from jax.experimental import pallas as pl
from jax.experimental.pallas import tpu as pltpu
from jax.sharding import PartitionSpec as P

ROW_LIMIT = 8
CHUNK = 512
LAYERS = 4
PIECES = 4
PARTIAL = (1, 3)
ORDER = (0, 2, 1, 3)
HALVES = 2
FAR_EIGHTHS = 6
UNROLL = 16
MESH = pl.DeviceIdType.MESH
BF16, F32 = jnp.bfloat16, jnp.float32


def iota(shape, axis):
    return lax.broadcasted_iota(jnp.int32, shape, axis)


def hot(mask):
    return mask.astype(F32).astype(BF16)


def contract(lhs, rhs, dims, **options):
    return lax.dot_general(lhs, rhs, (dims, ((), ())), preferred_element_type=F32, **options)


def locate(ids, owners, plane, rows_dev):
    listed = ids.shape[1]
    line = iota((owners, listed), 0)
    layer = line & (LAYERS - 1)
    column = lax.shift_right_logical(line, LAYERS.bit_length() - 1)
    first = (layer * plane + column) * rows_dev
    member = ((ids >= first) & (ids < first + rows_dev)).astype(F32)
    before = iota((listed, listed), 0) < iota((listed, listed), 1)
    earlier = contract(member.astype(BF16), hot(before), ((1,), (0,)))
    rank = jnp.sum(member * earlier, axis=0, keepdims=True).astype(jnp.int32)
    spot = jnp.sum(member * line.astype(F32), axis=0, keepdims=True).astype(jnp.int32)
    start = jnp.sum(member * first.astype(F32), axis=0, keepdims=True).astype(jnp.int32)
    held = (member * (ids - start + 1).astype(F32)).astype(BF16)
    return rank, spot, held


def mix_picks(slots_t, weights_t, listed):
    picks, tokens = slots_t.shape
    position = iota((listed, tokens), 0).astype(F32)

    def group(g, total):
        base = pl.multiple_of(g * UNROLL, UNROLL)
        slot = slots_t[pl.ds(base, UNROLL), :]
        weight = weights_t[pl.ds(base, UNROLL), :]
        for p in range(UNROLL):
            hit = slot[p : p + 1] == position
            total = total + jnp.where(hit, weight[p : p + 1], 0.0)
        return total

    start = jnp.zeros((listed, tokens), F32)
    return lax.fori_loop(0, picks // UNROLL, group, start)


def finish(c, gate_a, cot_a, gate_b, fetched, mix_wide, grad_memory, mixed_b, grad_gate, scores):
    tokens, features = gate_a.shape
    slot_rows = mix_wide.shape[1]
    piece = features // PIECES
    for k in range(piece // CHUNK):
        cols = pl.ds(c * piece + k * CHUNK, CHUNK)
        rows = fetched[:, :, :, cols].reshape(slot_rows, CHUNK)
        memory = contract(mix_wide[...], rows, ((1,), (0,)))
        gate = gate_a[:, cols].astype(F32)
        sig = jax.nn.sigmoid(gate)
        incoming = cot_a[:, cols].astype(F32)
        grad_gate[:, cols] = (
            incoming * memory[:tokens] * sig * (1.0 + gate * (1.0 - sig))
        ).astype(BF16)
        scores[...] += contract(grad_memory[:, cols], rows, ((1,), (1,)))
        gate = gate_b[:, cols].astype(F32)
        mixed_b[:, cols] = (gate * jax.nn.sigmoid(gate) * memory[tokens:]).astype(BF16)


def drain(block, sem):
    pltpu.make_async_copy(block, block, sem).wait()


def exchange(
    gate_a_in, cot_a_in, gate_b_in, table_in, row_ids_in, slots_in, weights_in,
    mixed_b, grad_gate, grad_table, scores, spots,
    gate_a, cot_a, gate_b, fetched, mix_wide, grad_memory,
    row_ids, slots, weights, col, aux, slots_t, weights_t, mix_tall,
    message, asked, codes, codes_sum, codes_aux, grads_out, arrived, rows_out, rows_aux,
    rs_out, rs_in,
    load, send, ask_recv, tab_recv, par_recv, aux_recv, grad_recv, row_recv, rs_recv,
    corner_in,
):
    sections = lax.axis_size("section")
    owners = lax.axis_size("table")
    plane = owners // LAYERS
    rows_dev, features = table_in.shape
    tokens = gate_a.shape[0]
    listed = row_ids.shape[1]
    part = features // sections
    group = sections * plane
    width = group * ROW_LIMIT
    piece = features // PIECES
    far = FAR_EIGHTHS * piece // 8
    last = LAYERS - 1

    sec = lax.axis_index("section")
    me = lax.axis_index("table")
    z = me // plane
    p_me = lax.rem(me, plane)
    seat = sec * plane + p_me
    parity = lax.rem(sec, 2)
    partner = sec + 1 - 2 * parity
    step_z = 1 - 2 * parity
    ahead_ok = (z + step_z >= 0) & (z + step_z <= last)

    def peer(hop):
        other, bit = p_me, 1
        while bit < plane:
            if hop & bit:
                other = other + bit - 2 * bit * lax.rem(p_me // bit, 2)
            bit *= 2
        return other

    x_side, y_side, corner = peer(1), peer(2), peer(3)

    def strip(c):
        if isinstance(c, int):
            return pl.ds(c * piece, piece)
        return pl.ds(pl.multiple_of(c * piece, piece), piece)

    def half(n):
        return pl.ds(n * (features // HALVES), features // HALVES)

    def other_section(hop):
        return lax.rem(sec + hop, sections)

    def need(k):
        return jnp.where(z < LAYERS // 2, last - k, k)

    def at(layer, place):
        return layer * plane + place

    def greet(s, t):
        pl.semaphore_signal(
            pltpu.get_barrier_semaphore(), inc=1,
            device_id={"section": s, "table": t}, device_id_type=MESH,
        )

    def remote(source, target, send, recv, s, t):
        pltpu.make_async_remote_copy(
            src_ref=source, dst_ref=target, send_sem=send, recv_sem=recv,
            device_id={"section": s, "table": t}, device_id_type=MESH,
        ).start()

    for hop in range(plane):
        for turn in range(sections):
            if (hop or turn) and hop != 3:
                greet(other_section(turn), at(z, peer(hop)))

    @pl.when(z > 0)
    def _():
        greet(sec, at(z - 1, p_me))

    @pl.when(z < last)
    def _():
        greet(sec, at(z + 1, p_me))

    pltpu.make_async_copy(row_ids_in, row_ids, load.at[4]).start()
    pltpu.make_async_copy(table_in, col.at[z], load.at[0]).start()
    pltpu.make_async_copy(slots_in, slots, load.at[5]).start()
    pltpu.make_async_copy(weights_in, weights, load.at[6]).start()
    pltpu.make_async_copy(gate_a_in, gate_a, load.at[1]).start()
    pltpu.make_async_copy(cot_a_in, cot_a, load.at[2]).start()
    pltpu.make_async_copy(gate_b_in, gate_b, load.at[3]).start()

    drain(row_ids, load.at[4])
    ids = row_ids[...]
    rank_a, spot_a, held_a = locate(ids[0:1], owners, plane, rows_dev)
    rank_b, spot_b, held_b = locate(ids[1:2], owners, plane, rows_dev)
    lane = iota((codes.shape[2], listed), 0)
    base = p_me * (2 * ROW_LIMIT) + width
    lanes_a = hot((lane == rank_a + base) | (lane == rank_a + seat * ROW_LIMIT))
    lanes_b = hot(lane == rank_b + (base + ROW_LIMIT))
    asking = contract(held_a, lanes_a, ((1,), (1,))) + contract(held_b, lanes_b, ((1,), (1,)))
    for q in range(plane):
        message[q] = asking[q * LAYERS : (q + 1) * LAYERS]

    signals = group - 1 - sections + jnp.where(z > 0, 1, 0) + jnp.where(z < last, 1, 0)
    pl.semaphore_wait(pltpu.get_barrier_semaphore(), signals)
    for side in (x_side, y_side):
        pl.semaphore_signal(
            corner_in, inc=1,
            device_id={"section": sec, "table": at(z, side)}, device_id_type=MESH,
        )

    def ask(hops):
        for hop in hops:
            q = peer(hop)
            for turn in range(sections):
                if hop or turn:
                    remote(
                        message.at[q], asked.at[seat], send, ask_recv,
                        other_section(turn), at(z, q),
                    )

    ask([hop for hop in range(plane) if hop != 3])
    pltpu.make_async_copy(message.at[p_me], asked.at[seat], ask_recv).start()

    for j, side in enumerate((x_side, y_side)):
        remote(
            message.at[corner], asked.at[group + 1 - j], send, ask_recv, sec, at(z, side)
        )

    drain(col.at[z], load.at[0])

    @pl.when(ahead_ok)
    def _():
        for n in range(HALVES):
            block = col.at[z, :, half(n)]
            remote(block, block, send, tab_recv.at[0, n], sec, at(z + step_z, p_me))

    for j, side in enumerate((x_side, y_side)):
        cols = strip(2 * j + parity)
        remote(
            col.at[z, :, cols], aux.at[z, :, cols], send, aux_recv.at[0], sec, at(z, side),
        )

    drain(slots, load.at[5])
    drain(weights, load.at[6])
    slots_t[...] = jnp.transpose(slots[...].reshape(2 * tokens, -1).astype(F32))
    weights_t[...] = jnp.transpose(weights[...].reshape(2 * tokens, -1))
    mixing_t = mix_picks(slots_t, weights_t, listed).astype(BF16)
    space = iota((owners * 2 * ROW_LIMIT, listed), 0)
    wide_a = hot(space == spot_a * (2 * ROW_LIMIT) + rank_a)
    wide_b = hot(space == spot_b * (2 * ROW_LIMIT) + (rank_b + ROW_LIMIT))
    tall_a = hot(iota((owners * ROW_LIMIT, listed), 0) == spot_a * ROW_LIMIT + rank_a)
    mix_tall[...] = contract(tall_a, mixing_t[:, :tokens], ((1,), (0,))).astype(BF16)

    pl.semaphore_wait(corner_in, 2)
    ask([3])
    drain(gate_a, load.at[1])
    drain(cot_a, load.at[2])

    @pl.loop(0, features // CHUNK)
    def _(c):
        per = part // CHUNK
        inner = pl.ds(pl.multiple_of(lax.rem(c, per) * CHUNK, CHUNK), CHUNK)
        cols = pl.ds(pl.multiple_of(c * CHUNK, CHUNK), CHUNK)
        gate = gate_a[:, cols].astype(F32)
        value = (cot_a[:, cols].astype(F32) * gate * jax.nn.sigmoid(gate)).astype(BF16)
        grad_memory[:, cols] = value
        rows = contract(mix_tall[...], value, ((1,), (0,))).astype(BF16)
        grads_out[c // per, :, :, :, inner] = rows.reshape(plane, LAYERS, ROW_LIMIT, CHUNK)

    for k in range(LAYERS):
        layer = need(k)
        for hop in range(plane):
            q = peer(hop)
            for turn in range(sections):
                if hop or turn:
                    other = other_section(turn)
                    remote(
                        grads_out.at[other, q, layer], arrived.at[layer, seat],
                        send, grad_recv.at[layer], other, at(z, q),
                    )
        pltpu.make_async_copy(
            grads_out.at[sec, p_me, layer], arrived.at[layer, seat], grad_recv.at[layer]
        ).start()

    def lookup(code):
        pick = (iota((rows_dev, code.shape[1]), 0).astype(F32) == code - 1.0).astype(F32)
        return jnp.transpose(pick)[width : width + plane * 2 * ROW_LIMIT].astype(BF16)

    def look_aside(layer):
        return [lookup(codes_aux[j, layer]) for j in range(2)]

    def span(block):
        return pl.ds(*block[1:])

    def whole(c):
        return c, c * piece, piece

    def tail(c):
        return c, (c + 1) * piece - far, far

    def find(pick, held, found, layer, block):
        _, first, size = block
        for k in range(0, size, CHUNK):
            cols = pl.ds(first + k, min(CHUNK, size - k))
            rows = contract(pick, held[layer, :, cols], ((1,), (0,))).astype(BF16)
            found[layer, :, :, cols] = rows.reshape(plane, 2 * ROW_LIMIT, -1)

    def give(found, layer, block, q, column):
        cols = span(block)
        remote(
            found.at[layer, q, :, cols], fetched.at[column, layer, :, cols],
            send, row_recv.at[block[0]], sec, at(z, q),
        )

    def keep(found, layer, block, column):
        cols = span(block)
        pltpu.make_async_copy(
            found.at[layer, p_me, :, cols], fetched.at[column, layer, :, cols],
            row_recv.at[block[0]],
        ).start()

    def valid(layer):
        return (layer >= 0) & (layer <= last)

    def inner(layer):
        return (layer > 0) & (layer < last)

    def blocks(h, c):
        if h == 0 or (h == 1 and c in PARTIAL):
            return [(whole(c), True)]
        if h == 2 and c in PARTIAL:
            return [((c, c * piece, piece - far), False), (tail(c), None)]
        return [(whole(c), None if h == 1 else False)]

    def serve(layer, pick, c, h):
        first = 2 if c < PIECES // 2 else 1
        for block, shared in blocks(h, c):
            find(pick, col, rows_out, layer, block)
            for hop in (first, *range(4, plane)):
                give(rows_out, layer, block, peer(hop), p_me)
            if shared is not True:

                @pl.when(~inner(layer) if shared is None else z >= 0)
                def _():
                    for hop in (3 - first, 3):
                        give(rows_out, layer, block, peer(hop), p_me)

            keep(rows_out, layer, block, p_me)

    def serve_aside(layer, picks, block):
        j = 2 * block[0] // PIECES
        column, target = ((x_side, y_side), (y_side, x_side))[j]
        find(picks[j], aux, rows_aux, layer, block)
        give(rows_aux, layer, block, target, column)
        keep(rows_aux, layer, block, column)

    def summed(layer, cols):
        code = codes_sum[layer][:, :width]
        pick = hot(iota((rows_dev, width), 0).astype(F32) == code - 1.0)
        block = arrived[layer, :, :, cols].reshape(width, -1)
        return contract(pick, block, ((1,), (0,)))

    each = PIECES // HALVES

    def pass_table(h, n):
        behind = z - step_z * h

        @pl.when(valid(behind))
        def _():
            block = col.at[behind, :, half(n)]
            drain(block, tab_recv.at[h - 1, n])
            if h < last:

                @pl.when(ahead_ok)
                def _():
                    remote(block, block, send, tab_recv.at[h, n], sec, at(z + step_z, p_me))

            remote(block, block, send, par_recv.at[h - 1, n], partner, me)

    def serve_layer(h, passing):
        behind, ahead = z - step_z * h, z + step_z * h

        @pl.when(valid(behind))
        def _():
            pick = lookup(codes[behind])
            for n in range(HALVES):
                if passing:
                    pass_table(h, n)
                for c in range(n * each, (n + 1) * each):
                    serve(behind, pick, c, h)

        @pl.when(valid(ahead))
        def _():
            pick = lookup(codes[ahead])
            for n in range(HALVES):
                drain(col.at[ahead, :, half(n)], par_recv.at[h - 1, n])
                for c in range(n * each, (n + 1) * each):
                    serve(ahead, pick, c, h)

    def own_aside():
        drain(col.at[z, :, half(0)], aux_recv.at[0])
        for j in range(2):
            block = aux.at[z, :, strip(2 * j + parity)]
            remote(block, block, send, aux_recv.at[1], partner, me)

    def landing(h, way, c):
        if h == 1:
            return 2 + way * PIECES + c
        return 2 + 2 * PIECES + way * len(PARTIAL) + PARTIAL.index(c)

    def near_aside(h):
        behind, ahead = z - step_z * h, z + step_z * h

        def each_block(layer, use):
            for c in sorted(range(PIECES), key=lambda c: c not in PARTIAL):
                for block, shared in blocks(h, c):
                    if shared is True:
                        use(block)
                    elif shared is None:

                        @pl.when(inner(layer))
                        def _():
                            use(block)

        @pl.when(valid(behind))
        def _():
            picks = look_aside(behind)

            def use(block):
                c = block[0]
                part = aux.at[behind, :, span(block)]
                drain(part, aux_recv.at[landing(h, 0, c)])
                if h == 1 and c in PARTIAL:

                    @pl.when(inner(behind) & ahead_ok)
                    def _():
                        onward = aux.at[behind, :, span(tail(c))]
                        remote(
                            onward, onward, send, aux_recv.at[landing(2, 0, c)],
                            sec, at(z + step_z, p_me),
                        )

                remote(part, part, send, aux_recv.at[landing(h, 1, c)], partner, me)
                serve_aside(behind, picks, block)

            each_block(behind, use)

        @pl.when(valid(ahead))
        def _():
            picks = look_aside(ahead)

            def use(block):
                drain(aux.at[ahead, :, span(block)], aux_recv.at[landing(h, 1, block[0])])
                serve_aside(ahead, picks, block)

            each_block(ahead, use)

    def reduce_step(k, starts, follows):
        for turn in range(2):
            way = jnp.where(z < LAYERS // 2, 1 - turn, turn)
            up = way == 0
            place = jnp.where(up, z, last - z)
            layer = jnp.where(up, last - (k - place), k - place)
            target = jnp.where(up, z + 1, z - 1)

            def pass_on(earlier):
                for c in range(2):
                    cols = pl.ds(c * (part // 2), part // 2)
                    if earlier:
                        drain(rs_in.at[way, k - 1, :, cols], rs_recv.at[way, k - 1, c])
                    total = summed(layer, cols)
                    if earlier:
                        total = total + rs_in[way, k - 1, :, cols].astype(F32)
                    rs_out[way, k, :, cols] = total.astype(BF16)
                    remote(
                        rs_out.at[way, k, :, cols], rs_in.at[way, k, :, cols],
                        send, rs_recv.at[way, k, c], sec, at(target, p_me),
                    )

            if starts:

                @pl.when(place == 0)
                def _():
                    drain(arrived.at[layer], grad_recv.at[layer])
                    pass_on(False)

            if follows:

                @pl.when((place > 0) & (place <= k))
                def _():
                    drain(arrived.at[layer], grad_recv.at[layer])
                    pass_on(True)

    own_aside()
    pass_table(1, 0)

    drain(asked, ask_recv)
    served, summing = asked[sec * plane], asked[0]
    for q in range(1, plane):
        served = served + asked[sec * plane + q]
    for q in range(1, group):
        summing = summing + asked[q]
    for layer in range(LAYERS):
        codes[layer] = served[layer : layer + 1]
        codes_sum[layer] = summing[layer : layer + 1]

    for j, side in enumerate((x_side, y_side)):
        served = message[side] + asked[group + j]
        for layer in range(LAYERS):
            codes_aux[j, layer] = served[layer : layer + 1]

    pick = lookup(codes[z])
    for c in range(PIECES):
        serve(z, pick, c, 0)
    drain(col.at[z, :, half(0)], aux_recv.at[1])
    picks = look_aside(z)
    for c in range(PIECES):
        serve_aside(z, picks, whole(c))
    for n in range(1, HALVES):
        pass_table(1, n)

    def pass_aside(c):
        block = aux.at[z, :, strip(c)]
        remote(block, block, send, aux_recv.at[landing(1, 0, c)], sec, at(z + step_z, p_me))

    @pl.when(ahead_ok & inner(z))
    def _():
        for c in sorted(range(PIECES), key=lambda c: c not in PARTIAL):
            pass_aside(c)

    reduce_step(0, True, False)

    @pl.when(ahead_ok & ~inner(z))
    def _():
        for c in PARTIAL:
            pass_aside(c)

    serve_layer(1, False)

    mix_wide[:tokens] = contract(mixing_t[:, :tokens], wide_a, ((0,), (1,))).astype(BF16)
    mix_wide[tokens:] = contract(mixing_t[:, tokens:], wide_b, ((0,), (1,))).astype(BF16)
    scores[...] = jnp.zeros_like(scores)
    place_a = jnp.broadcast_to(spot_a * (2 * ROW_LIMIT) + rank_a, (tokens, listed))
    spots[...] = jnp.take_along_axis(place_a, slots[0], axis=1)

    serve_layer(2, True)
    reduce_step(1, True, True)
    near_aside(1)
    for k in range(2, last):
        reduce_step(k, True, False)
    for h in range(3, LAYERS):
        serve_layer(h, True)
    near_aside(2)
    for k in range(2, last):
        reduce_step(k, False, True)

    drain(arrived.at[z], grad_recv.at[z])

    @pl.loop(0, part // CHUNK)
    def _(c):
        cols = pl.ds(pl.multiple_of(c * CHUNK, CHUNK), CHUNK)
        grad_table[:, cols] = summed(z, cols)

    drain(gate_b, load.at[3])
    for c in ORDER[:-1]:
        drain(fetched.at[:, :, :, strip(c)], row_recv.at[c])
        finish(c, gate_a, cot_a, gate_b, fetched, mix_wide, grad_memory, mixed_b, grad_gate, scores)

    for way in range(2):

        @pl.when((z > 0) if way == 0 else (z < last))
        def _():
            for c in range(2):
                cols = pl.ds(c * (part // 2), part // 2)
                drain(rs_in.at[way, last - 1, :, cols], rs_recv.at[way, last - 1, c])
                grad_table[:, cols] += rs_in[way, last - 1, :, cols].astype(F32)

    drain(fetched.at[:, :, :, strip(ORDER[-1])], row_recv.at[ORDER[-1]])
    drain(asked.at[pl.ds(0, group + 1)], send)
    drain(arrived.at[:, pl.ds(0, group - 1)], send)
    drain(rows_out.at[0, pl.ds(0, plane - 2)], send)
    for c in range(2):
        drain(col.at[z, :, strip(c)], send)
        drain(col.at[z, :, strip(c)], send)

    @pl.when(ahead_ok)
    def _():
        drain(col.at[z], send)
        drain(col.at[z, :, half(0)], send)

    @pl.when(ahead_ok & inner(z))
    def _():
        drain(col.at[z, :, half(0)], send)

    for h in range(1, LAYERS):
        behind, ahead = z - step_z * h, z + step_z * h

        @pl.when(valid(behind))
        def _():
            drain(col.at[behind], send)

            @pl.when(ahead_ok)
            def _():
                drain(col.at[behind], send)

            for c in range(PIECES):
                for block, shared in blocks(h, c):
                    if shared is True:
                        drain(aux.at[z, :, span(block)], send)
                    elif shared is None:

                        @pl.when(inner(behind))
                        def _():
                            drain(aux.at[z, :, span(block)], send)

                if h == 1 and c in PARTIAL:

                    @pl.when(inner(behind) & ahead_ok)
                    def _():
                        drain(aux.at[z, :, span(tail(c))], send)

        for layer in (behind, ahead):

            @pl.when(valid(layer))
            def _():
                drain(rows_out.at[0, pl.ds(0, plane - 2)], send)
                for c in range(PIECES):
                    for block, shared in blocks(h, c):
                        if shared is not True:

                            @pl.when(~inner(layer) if shared is None else z >= 0)
                            def _():
                                drain(rows_out.at[0, 0, :, span(block)], send)

    for k in range(last):
        for way in range(2):

            @pl.when(k >= (z if way == 0 else last - z))
            def _():
                drain(rs_out.at[way, k], send)


def store(
    mixed_b, grad_gate, grad_table, scores, spots,
    gate_a, cot_a, gate_b, fetched, mix_wide, grad_memory,
    mixed_out, grad_gate_out, grad_table_out, grad_weights_out, grad_weights, sems,
):
    features = gate_a.shape[1]
    done = pl.ds(0, features - features // PIECES)
    rest = pl.ds(features - features // PIECES, features // PIECES)

    def put(source, target, n):
        copy = pltpu.make_async_copy(source, target, sems.at[n])
        copy.start()
        return copy

    copies = [
        put(mixed_b.at[:, done], mixed_out.at[:, done], 0),
        put(grad_gate.at[:, done], grad_gate_out.at[:, done], 1),
        put(grad_table, grad_table_out, 2),
    ]
    finish(
        ORDER[-1], gate_a, cot_a, gate_b, fetched, mix_wide, grad_memory,
        mixed_b, grad_gate, scores,
    )
    copies.append(put(mixed_b.at[:, rest], mixed_out.at[:, rest], 3))
    copies.append(put(grad_gate.at[:, rest], grad_gate_out.at[:, rest], 4))
    picks = grad_weights.shape[1]
    where = spots[...]
    found = jnp.zeros(grad_weights.shape, F32)
    for first in range(0, scores.shape[1], picks):
        near = where - first
        inside = (near >= 0) & (near < picks)
        got = jnp.take_along_axis(
            scores[:, first : first + picks], jnp.where(inside, near, 0), axis=1
        )
        found = jnp.where(inside, got, found)
    grad_weights[...] = found
    copies.append(put(grad_weights, grad_weights_out, 5))
    for copy in copies:
        copy.wait()


def local(gate_a, cotangent_a, gate_b, table, row_ids, slots, weights):
    owners = lax.axis_size("table")
    sections = lax.axis_size("section")
    plane = owners // LAYERS
    group = sections * plane
    rows_dev, features = table.shape
    tokens = gate_a.shape[1]
    listed = row_ids.shape[-1]
    picks = slots.shape[-1]
    part = features // sections
    lanes = -(-(2 * plane + group) * ROW_LIMIT // 128) * 128
    slot_rows = owners * 2 * ROW_LIMIT
    vmem = pl.BlockSpec(memory_space=pltpu.VMEM)
    hbm = pl.BlockSpec(memory_space=pl.ANY)
    dma = pltpu.SemaphoreType.DMA
    results = pl.pallas_call(
        exchange,
        out_shape=(
            pltpu.VMEM((tokens, features), BF16),
            pltpu.VMEM((tokens, features), BF16),
            pltpu.VMEM((rows_dev, part), F32),
            pltpu.VMEM((tokens, slot_rows), F32),
            pltpu.VMEM((tokens, picks), jnp.int32),
            pltpu.VMEM((tokens, features), BF16),
            pltpu.VMEM((tokens, features), BF16),
            pltpu.VMEM((tokens, features), BF16),
            pltpu.VMEM((plane, LAYERS, 2 * ROW_LIMIT, features), BF16),
            pltpu.VMEM((2 * tokens, slot_rows), BF16),
            pltpu.VMEM((tokens, features), BF16),
        ),
        in_specs=[pl.BlockSpec(memory_space=pltpu.HBM)] * 7,
        out_specs=(vmem,) * 11,
        scratch_shapes=[
            pltpu.VMEM((2, listed), jnp.int32),
            pltpu.VMEM((2, tokens, picks), jnp.int32),
            pltpu.VMEM((2, tokens, picks), F32),
            pltpu.VMEM((LAYERS, rows_dev, features), BF16),
            pltpu.VMEM((LAYERS, rows_dev, features), BF16),
            pltpu.VMEM((picks, 2 * tokens), F32),
            pltpu.VMEM((picks, 2 * tokens), F32),
            pltpu.VMEM((owners * ROW_LIMIT, tokens), BF16),
            pltpu.VMEM((plane, LAYERS, lanes), F32),
            pltpu.VMEM((group + 2, LAYERS, lanes), F32),
            pltpu.VMEM((LAYERS, 1, lanes), F32),
            pltpu.VMEM((LAYERS, 1, lanes), F32),
            pltpu.VMEM((2, LAYERS, 1, lanes), F32),
            pltpu.VMEM((sections, plane, LAYERS, ROW_LIMIT, part), BF16),
            pltpu.VMEM((LAYERS, group, ROW_LIMIT, part), BF16),
            pltpu.VMEM((LAYERS, plane, 2 * ROW_LIMIT, features), BF16),
            pltpu.VMEM((LAYERS, plane, 2 * ROW_LIMIT, features), BF16),
            pltpu.VMEM((2, LAYERS - 1, rows_dev, part), BF16),
            pltpu.VMEM((2, LAYERS - 1, rows_dev, part), BF16),
            dma((7,)),
            dma,
            dma,
            dma((LAYERS - 1, HALVES)),
            dma((LAYERS - 1, HALVES)),
            dma((2 + 2 * PIECES + 2 * len(PARTIAL),)),
            dma((LAYERS,)),
            dma((PIECES,)),
            dma((2, LAYERS - 1, HALVES)),
            pltpu.SemaphoreType.REGULAR,
        ],
        compiler_params=pltpu.CompilerParams(
            collective_id=0, has_side_effects=True, vmem_limit_bytes=44 * 1024 * 1024
        ),
    )(
        *(
            pltpu.with_memory_space_constraint(x, pltpu.HBM)
            for x in (
                gate_a[0], cotangent_a[0], gate_b[0], table, row_ids[0, :, 0], slots[0], weights[0]
            )
        )
    )
    mixed_b, grad_gate, grad_table, grad_weights = pl.pallas_call(
        store,
        out_shape=(
            jax.ShapeDtypeStruct((tokens, features), BF16),
            jax.ShapeDtypeStruct((tokens, features), BF16),
            jax.ShapeDtypeStruct((rows_dev, part), F32),
            jax.ShapeDtypeStruct((tokens, picks), F32),
        ),
        in_specs=[vmem] * 11,
        out_specs=(hbm,) * 4,
        scratch_shapes=[pltpu.VMEM((tokens, picks), F32), dma((6,))],
        compiler_params=pltpu.CompilerParams(vmem_limit_bytes=8 * 1024 * 1024),
    )(*(pltpu.with_memory_space_constraint(r, pltpu.VMEM) for r in results))
    return mixed_b[None], grad_gate[None], grad_weights[None], grad_table


def solution(mesh):
    return jax.shard_map(
        local,
        mesh=mesh,
        in_specs=(
            P("section", "table", None),
            P("section", "table", None),
            P("section", "table", None),
            P("table", None),
            P("section", None, "table", None),
            P("section", None, "table", None),
            P("section", None, "table", None),
        ),
        out_specs=(
            P("section", "table", None),
            P("section", "table", None),
            P("section", "table", None),
            P("table", "section"),
        ),
        check_vma=False,
    )
```
